32 devices in a mesh: dp: 4 (over y, x), seq: 8 (over z, core).
Axes of the slice: x: 2, y: 2, z: 4, core: 2. Of those that a mesh axis runs over, the one named last changes fastest.
Arguments:
- tokens: bfloat16 [16, 2048, 768], P('dp', 'seq'), may hold values from -6 to 6
- lengths: int32 [16], P('dp'), may hold values from 512 to 2048, as said below
- query_weight: bfloat16 [768, 768], P(('dp', 'seq')), may hold values from -0.21875 to 0.21875
- key_weight: bfloat16 [768, 768], P(('dp', 'seq')), may hold values from -0.21875 to 0.21875
- value_weight: bfloat16 [768, 768], P(('dp', 'seq')), may hold values from -0.21875 to 0.21875
- out_weight: bfloat16 [768, 768], P(('dp', 'seq')), may hold values from -6 to 6
- up_weight: bfloat16 [768, 3072], P(('dp', 'seq')), may hold values from -0.21875 to 0.21875
- down_weight: bfloat16 [3072, 768], P(('dp', 'seq')), may hold values from -0.109375 to 0.109375
- query_bias: bfloat16 [768], P(('dp', 'seq')), may hold values from -3 to 3
- value_bias: bfloat16 [768], P(('dp', 'seq')), may hold values from -3 to 3
- out_bias: bfloat16 [768], P(('dp', 'seq')), may hold values from -3 to 3
- up_bias: bfloat16 [3072], P(('dp', 'seq')), may hold values from -3 to 3
- down_bias: bfloat16 [768], P(('dp', 'seq')), may hold values from -3 to 3
- first_gain: bfloat16 [768], P(('dp', 'seq')), may hold values from 0.5 to 1.5
- first_shift: bfloat16 [768], P(('dp', 'seq')), may hold values from -2 to 2
- second_gain: bfloat16 [768], P(('dp', 'seq')), may hold values from 0.5 to 1.5
- second_shift: bfloat16 [768], P(('dp', 'seq')), may hold values from -2 to 2
- cotangent: bfloat16 [16, 2048, 768], P('dp', 'seq'), may hold values from -6 to 6
Outputs:
- output: bfloat16 [16, 2048, 768], P('dp', 'seq')
- tokens_grad: float32 [16, 2048, 768], P('dp', 'seq')
- query_weight_grad: float32 [768, 768], P(('dp', 'seq'))
- key_weight_grad: float32 [768, 768], P(('dp', 'seq'))
- value_weight_grad: float32 [768, 768], P(('dp', 'seq'))
- out_weight_grad: float32 [768, 768], P(('dp', 'seq'))
- up_weight_grad: float32 [768, 3072], P(('dp', 'seq'))
- down_weight_grad: float32 [3072, 768], P(('dp', 'seq'))
- query_bias_grad: float32 [768], P(('dp', 'seq'))
- value_bias_grad: float32 [768], P(('dp', 'seq'))
- out_bias_grad: float32 [768], P(('dp', 'seq'))
- up_bias_grad: float32 [3072], P(('dp', 'seq'))
- down_bias_grad: float32 [768], P(('dp', 'seq'))
- first_gain_grad: float32 [768], P(('dp', 'seq'))
- first_shift_grad: float32 [768], P(('dp', 'seq'))
- second_gain_grad: float32 [768], P(('dp', 'seq'))
- second_shift_grad: float32 [768], P(('dp', 'seq'))
The draws below stay inside these ranges and needn't reach their ends.
Inputs may be any that keep to these rules, and one draw needn't show every extreme that they name: `lengths`: each length lies in 512 to 2048; some sequence is full and some has exactly 512 valid tokens.
All inputs are finite; a program needn't handle non-finite values.
Results may differ from the reference program's by a relative error of at most 0.018.
Values may be sent and summed in bfloat16 or wider, within the bound.
A program may use at most 192 MiB of HBM per device.

```python
import jax
import jax.numpy as jnp
from jax import lax

D = 768
H = 12
HD = 64
FF = 3072
LENGTH = 2048
LEAST = 512
SEQS = 16


def draw_lengths(key, part):
    first_key, second_key, third_key = jax.random.split(jax.random.fold_in(key, 17), 3)
    drawn = jax.random.randint(first_key, (SEQS,), LEAST, LENGTH + 1)
    full_spot = jax.random.randint(second_key, (), 0, SEQS)
    short_spot = (full_spot + 1 + jax.random.randint(third_key, (), 0, SEQS - 1)) % SEQS
    places = jnp.arange(SEQS)
    drawn = jnp.where(places == full_spot, LENGTH, drawn)
    drawn = jnp.where(places == short_spot, LEAST, drawn)
    return drawn.astype(jnp.int32)


def block_levels(rng, dims, cuts, smallest, top_value):
    gain, own = 1.0, jax.random.fold_in(rng, 6)
    for dim, shards_of in cuts:
        heights = jnp.exp(jax.random.uniform(jax.random.fold_in(own, dim), (shards_of,), jnp.float32, smallest / len(cuts), top_value / len(cuts)))
        gain = gain * jnp.repeat(heights, dims[dim] // shards_of).reshape([-1 if axis == dim else 1 for axis in range(len(dims))])
    return gain


def normal_values(rng, dims, scale, limit, cuts=(), kind=jnp.bfloat16):
    values = jax.random.normal(rng, dims, jnp.float32) * scale
    if len(cuts) > 0:
        values = block_levels(rng, dims, cuts, -0.22, 0.18) * values
    return jnp.clip(values, min=-limit, max=limit).astype(kind)


def setup_inputs(seed: int = 0) -> dict:
    seeds = jax.random.split(jax.random.key(seed), 19)
    tokens = normal_values(seeds[0], (SEQS, LENGTH, D), 1.0, 6.0, ((0, 4), (1, 8)))
    lengths = draw_lengths(jax.random.fold_in(seeds[18], 71), 0)
    query_weight = normal_values(seeds[2], (D, D), D ** -0.5, 0.21875, ((0, 32),))
    key_weight = normal_values(seeds[3], (D, D), D ** -0.5, 0.21875, ((0, 32),))
    value_weight = normal_values(seeds[4], (D, D), D ** -0.5, 0.21875, ((0, 32),))
    out_weight = normal_values(seeds[5], (D, D), (max(1, D * 4 // LENGTH)) ** -0.5, 6.0, ((0, 32),))
    up_weight = normal_values(seeds[6], (D, FF), D ** -0.5, 0.21875, ((0, 32),))
    down_weight = normal_values(seeds[7], (FF, D), FF ** -0.5, 0.109375, ((0, 32),))
    query_bias = normal_values(seeds[8], (D,), 0.5, 3.0, ((0, 32),))
    value_bias = normal_values(seeds[9], (D,), 0.5, 3.0, ((0, 32),))
    out_bias = normal_values(seeds[10], (D,), 0.5, 3.0, ((0, 32),))
    up_bias = normal_values(seeds[11], (FF,), 0.5, 3.0, ((0, 32),))
    down_bias = normal_values(seeds[12], (D,), 0.5, 3.0, ((0, 32),))
    first_gain = jnp.clip(1.0 + 0.1 * jax.random.normal(seeds[13], (D,), jnp.float32), 0.5, 1.5).astype(jnp.bfloat16)
    first_shift = normal_values(seeds[14], (D,), 0.3, 2.0, ((0, 32),))
    second_gain = jnp.clip(1.0 + 0.1 * jax.random.normal(seeds[15], (D,), jnp.float32), 0.5, 1.5).astype(jnp.bfloat16)
    second_shift = normal_values(seeds[16], (D,), 0.3, 2.0, ((0, 32),))
    cotangent = normal_values(seeds[17], (SEQS, LENGTH, D), 1.0, 6.0, ((0, 4), (1, 8)))
    return dict(tokens=tokens, lengths=lengths, query_weight=query_weight, key_weight=key_weight, value_weight=value_weight, out_weight=out_weight, up_weight=up_weight, down_weight=down_weight, query_bias=query_bias, value_bias=value_bias, out_bias=out_bias, up_bias=up_bias, down_bias=down_bias, first_gain=first_gain, first_shift=first_shift, second_gain=second_gain, second_shift=second_shift, cotangent=cotangent)


@jax.custom_vjp
def low(v):
    return lax.optimization_barrier(v.astype(jnp.bfloat16)).astype(jnp.float32)

@jax.custom_vjp
def low_back(v):
    return v

def low_keep(v):
    return (low(v), None)

def low_pass(kept, grad):
    return (grad,)

def back_keep(v):
    return (v, None)

def back_low(kept, grad):
    return (low(grad),)
low.defvjp(low_keep, low_pass)
low_back.defvjp(back_keep, back_low)
EPSILON = 1e-05
HIGHEST = lax.Precision.HIGHEST

def matmul(left, right):
    return jnp.dot(left, right, precision=HIGHEST)

def normalize(inputs, gains, shifts):
    centre = inputs - lax.optimization_barrier(jnp.mean(inputs, axis=-1, keepdims=True))
    factor = lax.rsqrt(lax.optimization_barrier(jnp.mean(centre * centre, axis=-1, keepdims=True)) + EPSILON)
    return centre * factor * gains + shifts

def layer(params, inputs, live):
    query_weight, key_weight, value_weight, out_weight, up_weight, down_weight, query_bias, value_bias, out_bias, up_bias, down_bias, first_gain, first_shift, second_gain, second_shift = params
    query = low(low_back(matmul(inputs, query_weight) + query_bias))
    keys = low(low_back(matmul(inputs, key_weight)))
    values = low(low_back(matmul(inputs, value_weight) + value_bias))
    query_heads = query.reshape(LENGTH, H, HD).transpose(1, 0, 2)
    key_heads = keys.reshape(LENGTH, H, HD).transpose(1, 0, 2)
    value_heads = values.reshape(LENGTH, H, HD).transpose(1, 0, 2)
    scores = jnp.einsum('hqe,hke->hqk', query_heads, key_heads, precision=HIGHEST) * 0.125
    scores = low_back(jnp.where(live[None, None, :], scores, -1e+30))
    probs = low(jax.nn.softmax(scores, axis=-1))
    context = jnp.einsum('hqk,hke->hqe', probs, value_heads, precision=HIGHEST)
    context = low(low_back(context.transpose(1, 0, 2).reshape(LENGTH, D)))
    branch = low_back(matmul(context, out_weight) + out_bias)
    first = low(normalize(inputs + branch, first_gain, first_shift))
    up_pre = low_back(matmul(first, up_weight) + up_bias)
    activated = low(jax.nn.gelu(up_pre, approximate=False))
    second = first + low_back(matmul(activated, down_weight) + down_bias)
    return normalize(second, second_gain, second_shift) * live[:, None].astype(jnp.float32)

def reference(tokens, lengths, query_weight, key_weight, value_weight, out_weight, up_weight, down_weight, query_bias, value_bias, out_bias, up_bias, down_bias, first_gain, first_shift, second_gain, second_shift, cotangent):
    params = tuple((array_in.astype(jnp.float32) for array_in in (query_weight, key_weight, value_weight, out_weight, up_weight, down_weight, query_bias, value_bias, out_bias, up_bias, down_bias, first_gain, first_shift, second_gain, second_shift)))
    inputs = tokens.astype(jnp.float32)
    live = jnp.arange(LENGTH, dtype=jnp.int32)[None, :] < lengths.astype(jnp.int32)[:, None]

    def forward(weights, sequences):
        return lax.map(lambda together: jax.checkpoint(layer)(weights, together[0], together[1]), (sequences, live))
    result, pullback = jax.vjp(forward, params, inputs)
    grads, input_grad = pullback(cotangent.astype(jnp.float32))
    return (result.astype(jnp.bfloat16), input_grad, grads[0], grads[1], grads[2], grads[3], grads[4], grads[5], grads[6], grads[7], grads[8], grads[9], grads[10], grads[11], grads[12], grads[13], grads[14])
```

```python
import jax
import jax.numpy as jnp
from jax import lax
from jax.experimental import pallas as pl
from jax.experimental.pallas import tpu as pltpu
from jax.sharding import PartitionSpec as P

H = 12
HD = 64

EPSILON = 1e-05
ROOT_HALF = 0.7071067811865476
INV_ROOT_TWO_PI = 0.3989422804014327
BF = jnp.bfloat16
F32 = jnp.float32


def matmul(left, right):
    return jnp.dot(left, right, preferred_element_type=F32)


def left_product(left, right):
    return lax.dot_general(left, right, (((0,), (0,)), ((), ())), preferred_element_type=F32)


def right_product(left, right):
    return lax.dot_general(left, right, (((1,), (1,)), ((), ())), preferred_element_type=F32)


def normalize(inputs, gains, shifts):
    centre = inputs - jnp.mean(inputs, axis=-1, keepdims=True)
    factor = lax.rsqrt(jnp.mean(centre * centre, axis=-1, keepdims=True) + EPSILON)
    unit_rows = centre * factor
    return (unit_rows * gains + shifts, unit_rows, factor)


def norm_back(grad_in, unit_rows, factor, gains):
    grad_unit = grad_in * gains
    return factor * (
        grad_unit
        - jnp.mean(grad_unit, axis=-1, keepdims=True)
        - unit_rows * jnp.mean(grad_unit * unit_rows, axis=-1, keepdims=True)
    )


def gelu_slope(inputs):
    return 0.5 * (1.0 + lax.erf(inputs * ROOT_HALF)) + inputs * INV_ROOT_TWO_PI * jnp.exp(
        -0.5 * inputs * inputs
    )


def swap_index(place, step, count):
    if count & (count - 1) == 0:
        return place ^ step
    return (place + step) % count


def source_index(place, step, count):
    if count & (count - 1) == 0:
        return place ^ step
    return (place - step) % count


class Grid:
    def __init__(self, seqs):
        self.columns = lax.axis_size("dp")
        self.n = lax.axis_size("seq")
        self.seqs = seqs
        self.group = self.n // seqs
        self.chips = self.n // 2
        self.column = lax.axis_index("dp")
        place = lax.axis_index("seq")
        self.chip = place // 2
        self.core = place % 2
        self.owner = place // self.group
        self.member = place % self.group

    def to_chip(self, array_in, step):
        pairs = [(s, swap_index(s // 2, step, self.chips) * 2 + s % 2) for s in range(self.n)]
        return lax.ppermute(array_in, "seq", pairs)

    def to_column(self, array_in, step):
        pairs = [(s, swap_index(s, step, self.columns)) for s in range(self.columns)]
        return lax.ppermute(array_in, "dp", pairs)

    def to_core(self, array_in):
        return lax.ppermute(array_in, "seq", [(s, s ^ 1) for s in range(self.n)])

    def to_owner(self, array_in, step, back=False):
        move = source_index if back else swap_index
        pairs = [
            (s, move(s // self.group, step, self.seqs) * self.group + s % self.group)
            for s in range(self.n)
        ]
        return lax.ppermute(array_in, "seq", pairs)

    def to_member(self, array_in, step, back=False):
        shift = -step if back else step
        pairs = [
            (s, (s // self.group) * self.group + (s % self.group + shift) % self.group)
            for s in range(self.n)
        ]
        return lax.ppermute(array_in, "seq", pairs)


def take_block(array_in, index):
    return lax.dynamic_index_in_dim(array_in, index, 0, keepdims=False)


def to_sequences(grid, array_in):
    parts = [take_block(array_in, grid.owner)]
    for step in range(1, grid.seqs):
        target = swap_index(grid.owner, step, grid.seqs)
        parts.append(grid.to_owner(take_block(array_in, target), step))
    return jnp.concatenate(parts, axis=0)


def from_sequences(grid, rows, length):
    blocks = rows.reshape(grid.seqs, length, rows.shape[1])
    out = jnp.zeros_like(blocks)
    out = lax.dynamic_update_index_in_dim(out, blocks[0], grid.owner, 0)
    for step in range(1, grid.seqs):
        got = grid.to_owner(blocks[step], step, back=True)
        place = swap_index(grid.owner, step, grid.seqs)
        out = lax.dynamic_update_index_in_dim(out, got, place, 0)
    return out


def row_positions(grid, length):
    def positions(member):
        spots = []
        for step in range(grid.seqs):
            source = source_index(grid.owner, step, grid.seqs)
            spots.append((source * grid.group + member) * length + jnp.arange(length, dtype=jnp.int32))
        return jnp.concatenate(spots)

    return positions


def gather_packed(grid, shard):
    parts = [shard] + [grid.to_chip(shard, step) for step in range(1, grid.chips)]
    chips = jnp.stack(parts)
    wide = [chips] + [grid.to_column(chips, step) for step in range(1, grid.columns)]
    mine = jnp.concatenate(wide, axis=0)
    other = grid.to_core(mine)
    return mine, other


def relative_order(grid):
    column = jnp.arange(grid.columns, dtype=jnp.int32)[:, None]
    chip = jnp.arange(grid.chips, dtype=jnp.int32)[None, :]
    if grid.columns & (grid.columns - 1) == 0:
        column_step = column ^ grid.column
    else:
        column_step = (grid.column - column) % grid.columns
    if grid.chips & (grid.chips - 1) == 0:
        chip_step = chip ^ grid.chip
    else:
        chip_step = (grid.chip - chip) % grid.chips
    return (column_step * grid.chips + chip_step).reshape(-1)


def assemble(grid, mine, other, cuts):
    order = relative_order(grid)
    count, rows, width = mine.shape
    spot = jnp.concatenate([grid.core[None].astype(jnp.int32), order])
    if any(cut[1] % 8 for cut in cuts):
        first = jnp.where(grid.core == 0, mine, other)[order]
        second = jnp.where(grid.core == 0, other, mine)[order]
        both = jnp.stack([first, second], axis=1).reshape(2 * count, rows, width)
        outs = []
        for start, height, blocks in cuts:
            piece = both[:, start : start + height * blocks]
            piece = piece.reshape(2 * count, blocks, height, width).transpose(0, 2, 1, 3)
            outs.append(piece.reshape(2 * count * height, blocks * width))
        return outs

    def kernel(spot_ref, mine_ref, other_ref, *out_refs):
        for core in range(2):

            @pl.when(spot_ref[0] == core)
            def _(core=core):
                for source, place in ((mine_ref, core), (other_ref, 1 - core)):
                    for (start, height, blocks), out_ref in zip(cuts, out_refs):
                        for block in range(blocks):
                            out_ref[
                                place * height : (place + 1) * height,
                                block * width : (block + 1) * width,
                            ] = source[start + block * height : start + (block + 1) * height, :]

    return pl.pallas_call(
        kernel,
        grid_spec=pltpu.PrefetchScalarGridSpec(
            num_scalar_prefetch=1,
            grid=(count,),
            in_specs=[
                pl.BlockSpec((None, rows, width), lambda i, spot: (spot[i + 1], 0, 0)),
                pl.BlockSpec((None, rows, width), lambda i, spot: (spot[i + 1], 0, 0)),
            ],
            out_specs=[
                pl.BlockSpec((2 * height, blocks * width), lambda i, spot: (i, 0))
                for _, height, blocks in cuts
            ],
        ),
        out_shape=[
            jax.ShapeDtypeStruct((2 * count * height, blocks * width), mine.dtype)
            for _, height, blocks in cuts
        ],
        name="assemble",
    )(spot, mine, other)


def scatter_sum(grid, array_in):
    width = array_in.shape[1]
    blocks = array_in.reshape(grid.columns * grid.chips, 2, -1, width)
    keep = lax.dynamic_index_in_dim(blocks, grid.core, 1, keepdims=False)
    send = lax.dynamic_index_in_dim(blocks, 1 - grid.core, 1, keepdims=False)
    half = (keep.astype(F32) + grid.to_core(send).astype(F32)).astype(BF)
    half = half.reshape(grid.columns, -1, width)
    total = take_block(half, grid.column).astype(F32)
    for step in range(1, grid.columns):
        target = swap_index(grid.column, step, grid.columns)
        total = total + grid.to_column(take_block(half, target), step).astype(F32)
    part = total.astype(BF).reshape(grid.chips, -1, width)
    total = take_block(part, grid.chip).astype(F32)
    for step in range(1, grid.chips):
        target = swap_index(grid.chip, step, grid.chips)
        total = total + grid.to_chip(take_block(part, target), step).astype(F32)
    return total


def split_heads(rows):
    return rows.reshape(rows.shape[0], H, HD).transpose(1, 0, 2)


def join_heads(heads):
    return heads.transpose(1, 0, 2).reshape(heads.shape[1], H * HD)


def attention(query, keys, values, key_bias):
    def attend(operands):
        query_h, key_h, value_h = operands
        scores = right_product(query_h, key_h) * 0.125 + key_bias[None, :]
        largest = jnp.max(scores, axis=-1, keepdims=True)
        exponent = jnp.exp(scores - largest)
        totals = jnp.sum(exponent, axis=-1, keepdims=True)
        context_h = matmul((exponent / totals).astype(BF), value_h)
        return (context_h.astype(BF), (largest + jnp.log(totals))[..., 0])

    context, log_totals = lax.map(attend, (split_heads(query), split_heads(keys), split_heads(values)))
    return join_heads(context), log_totals


def attention_back(query, keys, values, key_bias, log_totals, grad_context):
    def attend_back(operands):
        query_h, key_h, value_h, grad_h, log_h = operands
        scores = right_product(query_h, key_h) * 0.125 + key_bias[None, :]
        exact = jnp.exp(scores - log_h[..., None])
        grad_weights = right_product(grad_h, value_h)
        grad_value_h = left_product(exact.astype(BF), grad_h)
        centre_term = jnp.sum(exact * grad_weights, axis=-1, keepdims=True)
        grad_scores = (exact * (grad_weights - centre_term)).astype(BF)
        grad_query_h = matmul(grad_scores, key_h) * 0.125
        grad_key_h = left_product(grad_scores, query_h) * 0.125
        return (grad_query_h.astype(BF), grad_key_h.astype(BF), grad_value_h.astype(BF))

    heads = tuple(split_heads(a) for a in (query, keys, values, grad_context))
    grads = lax.map(attend_back, heads + (log_totals,))
    return tuple(join_heads(a) for a in grads)


def body(
    tokens,
    lengths,
    query_weight,
    key_weight,
    value_weight,
    out_weight,
    up_weight,
    down_weight,
    query_bias,
    value_bias,
    out_bias,
    up_bias,
    down_bias,
    first_gain,
    first_shift,
    second_gain,
    second_shift,
    cotangent,
):
    seqs, length, width = tokens.shape
    grid = Grid(seqs)
    devices = grid.columns * grid.n
    slim = query_weight.shape[0]
    hidden = up_weight.shape[1]
    tall = hidden // devices
    wide = hidden // width

    flat_in = to_sequences(grid, tokens)

    vectors = (
        query_bias,
        value_bias,
        out_bias,
        down_bias,
        first_gain,
        first_shift,
        second_gain,
        second_shift,
    )
    vector_row = jnp.concatenate(vectors + (up_bias,))
    vector_size = vector_row.shape[0]
    vector_rows = jnp.zeros((8, width), BF).at[0, :vector_size].set(vector_row)
    early = jnp.concatenate([query_weight, key_weight, value_weight, vector_rows], axis=0)
    late = jnp.concatenate(
        [out_weight]
        + [up_weight[:, i * width : (i + 1) * width] for i in range(wide)]
        + [down_weight],
        axis=0,
    )
    mine, other = gather_packed(grid, early)
    into_full, vector_full = assemble(
        grid, mine, other, ((0, slim, 3), (3 * slim, 8, 1))
    )
    late_mine, late_other = gather_packed(grid, late)
    out_full, up_full, down_full = assemble(
        grid,
        late_mine,
        late_other,
        ((0, slim, 1), (slim, slim, wide), (slim * (1 + wide), tall, 1)),
    )
    vector_table = vector_full.reshape(devices, 8, width)[:, 0, :vector_size]
    small = vector_table[:, : 8 * slim].reshape(devices, 8, slim).transpose(1, 0, 2)
    small = small.reshape(8, width).astype(F32)
    query_add, value_add, out_add, down_add, gain_one, shift_one, gain_two, shift_two = (
        small[i] for i in range(8)
    )
    up_add = vector_table[:, 8 * slim :].reshape(hidden).astype(F32)

    positions = row_positions(grid, length)
    my_length = take_block(lengths, grid.owner)
    live_rows = (positions(grid.member) < my_length).astype(F32)[:, None]
    key_bias = jnp.concatenate(
        [
            jnp.where(positions((grid.member - step) % grid.group) < my_length, 0.0, -1e30)
            for step in range(grid.group)
        ]
    ).astype(F32)

    into = matmul(flat_in, into_full)
    query = (into[:, :width] + query_add).astype(BF)
    key_value = jnp.concatenate([into[:, width : 2 * width], into[:, 2 * width :] + value_add], axis=1)
    key_value = key_value.astype(BF)
    key_value_all = jnp.concatenate(
        [key_value] + [grid.to_member(key_value, step) for step in range(1, grid.group)], axis=0
    )
    keys, values = key_value_all[:, :width], key_value_all[:, width:]

    context, log_totals = attention(query, keys, values, key_bias)
    grad_in = to_sequences(grid, cotangent)

    first_sum = flat_in.astype(F32) + matmul(context, out_full) + out_add
    first_norm, first_unit, first_factor = normalize(first_sum, gain_one, shift_one)
    first_low = first_norm.astype(BF)
    up_pre = matmul(first_low, up_full) + up_add
    activated = jax.nn.gelu(up_pre, approximate=False).astype(BF)
    second_sum = first_low.astype(F32) + matmul(activated, down_full) + down_add
    second_norm, second_unit, second_factor = normalize(second_sum, gain_two, shift_two)
    output = from_sequences(grid, (second_norm * live_rows).astype(BF), length)

    grad_output = grad_in.astype(F32) * live_rows
    grad_gain_two = jnp.sum(grad_output * second_unit, axis=0)
    grad_shift_two = jnp.sum(grad_output, axis=0)
    grad_second = norm_back(grad_output, second_unit, second_factor, gain_two)
    grad_branch = grad_second.astype(BF)
    grad_down_add = jnp.sum(grad_branch.astype(F32), axis=0)
    grad_down = left_product(activated, grad_branch).astype(BF)
    grad_up_low = (right_product(grad_branch, down_full) * gelu_slope(up_pre)).astype(BF)
    grad_up_add = jnp.sum(grad_up_low.astype(F32), axis=0)
    grad_up = left_product(first_low, grad_up_low).astype(BF)
    grad_first = right_product(grad_up_low, up_full) + grad_second
    grad_gain_one = jnp.sum(grad_first * first_unit, axis=0)
    grad_shift_one = jnp.sum(grad_first, axis=0)
    grad_residual = norm_back(grad_first, first_unit, first_factor, gain_one)
    grad_attend = grad_residual.astype(BF)
    grad_out_add = jnp.sum(grad_attend.astype(F32), axis=0)
    grad_out = left_product(context, grad_attend).astype(BF)
    grad_context = right_product(grad_attend, out_full).astype(BF)

    grad_down_own = scatter_sum(grid, grad_down)
    grad_up_own = scatter_sum(grid, grad_up)
    grad_out_own = scatter_sum(grid, grad_out)

    grad_query_low, grad_keys, grad_values = attention_back(
        query, keys, values, key_bias, log_totals, grad_context
    )
    rows = seqs * length
    grad_kv = jnp.concatenate([grad_keys, grad_values], axis=1)
    grad_kv_sum = grad_kv[:rows].astype(F32)
    for step in range(1, grid.group):
        piece = grad_kv[step * rows : (step + 1) * rows]
        grad_kv_sum = grad_kv_sum + grid.to_member(piece, step, back=True).astype(F32)
    grad_kv_low = grad_kv_sum.astype(BF)
    grad_into_low = jnp.concatenate([grad_query_low, grad_kv_low], axis=1)
    grad_query_add = jnp.sum(grad_query_low.astype(F32), axis=0)
    grad_value_add = jnp.sum(grad_kv_low[:, width:].astype(F32), axis=0)
    tokens_grad = right_product(grad_into_low, into_full) + grad_residual
    tokens_grad = from_sequences(grid, tokens_grad.astype(BF), length).astype(F32)
    grad_into = left_product(flat_in, grad_into_low).astype(BF)
    grad_into_own = scatter_sum(grid, grad_into)

    small_grads = jnp.stack(
        [
            grad_query_add,
            grad_value_add,
            grad_out_add,
            grad_down_add,
            grad_gain_one,
            grad_shift_one,
            grad_gain_two,
            grad_shift_two,
        ]
    )
    small_grads = small_grads.reshape(8, devices, slim).transpose(1, 0, 2).reshape(devices, 8 * slim)
    vector_grads = jnp.concatenate([small_grads, grad_up_add.reshape(devices, tall)], axis=1).astype(BF)
    vector_own = scatter_sum(grid, vector_grads)[0]
    vector_outs = [vector_own[i * slim : (i + 1) * slim] for i in range(8)]
    up_add_own = vector_own[8 * slim :]
    return (
        output,
        tokens_grad,
        grad_into_own[:, :width],
        grad_into_own[:, width : 2 * width],
        grad_into_own[:, 2 * width :],
        grad_out_own,
        grad_up_own,
        grad_down_own,
        vector_outs[0],
        vector_outs[1],
        vector_outs[2],
        up_add_own,
        vector_outs[3],
        vector_outs[4],
        vector_outs[5],
        vector_outs[6],
        vector_outs[7],
    )


def solution(mesh):
    whole = ("dp", "seq")
    matrix, vector, rows = P(whole, None), P(whole), P("dp", "seq", None)
    return jax.shard_map(
        body,
        mesh=mesh,
        in_specs=(rows, P("dp")) + (matrix,) * 6 + (vector,) * 9 + (rows,),
        out_specs=(rows, rows) + (matrix,) * 6 + (vector,) * 9,
        check_vma=False,
    )
```

```python
import jax
import jax.numpy as jnp
from jax import lax
from jax.experimental import pallas as pl
from jax.experimental.pallas import tpu as pltpu
from jax.sharding import PartitionSpec as P

H = 12
HD = 64

EPSILON = 1e-05
ROOT_HALF = 0.7071067811865476
INV_ROOT_TWO_PI = 0.3989422804014327
BF = jnp.bfloat16
F32 = jnp.float32


def matmul(left, right):
    return jnp.dot(left, right, preferred_element_type=F32)


def left_product(left, right):
    return lax.dot_general(left, right, (((0,), (0,)), ((), ())), preferred_element_type=F32)


def right_product(left, right):
    return lax.dot_general(left, right, (((1,), (1,)), ((), ())), preferred_element_type=F32)


def normalize(inputs, gains, shifts):
    centre = inputs - jnp.mean(inputs, axis=-1, keepdims=True)
    factor = lax.rsqrt(jnp.mean(centre * centre, axis=-1, keepdims=True) + EPSILON)
    unit_rows = centre * factor
    return (unit_rows * gains + shifts, unit_rows, factor)


def norm_back(grad_in, unit_rows, factor, gains):
    grad_unit = grad_in * gains
    return factor * (
        grad_unit
        - jnp.mean(grad_unit, axis=-1, keepdims=True)
        - unit_rows * jnp.mean(grad_unit * unit_rows, axis=-1, keepdims=True)
    )


def gelu_slope(inputs):
    return 0.5 * (1.0 + lax.erf(inputs * ROOT_HALF)) + inputs * INV_ROOT_TWO_PI * jnp.exp(
        -0.5 * inputs * inputs
    )


def swap_index(place, step, count):
    if count & (count - 1) == 0:
        return place ^ step
    return (place + step) % count


def source_index(place, step, count):
    if count & (count - 1) == 0:
        return place ^ step
    return (place - step) % count


class Grid:
    def __init__(self, seqs):
        self.columns = lax.axis_size("dp")
        self.n = lax.axis_size("seq")
        self.seqs = seqs
        self.group = self.n // seqs
        self.chips = self.n // 2
        self.column = lax.axis_index("dp")
        place = lax.axis_index("seq")
        self.chip = place // 2
        self.core = place % 2
        self.owner = place // self.group
        self.member = place % self.group

    def to_chip(self, array_in, step):
        pairs = [(s, swap_index(s // 2, step, self.chips) * 2 + s % 2) for s in range(self.n)]
        return lax.ppermute(array_in, "seq", pairs)

    def to_column(self, array_in, step):
        pairs = [(s, swap_index(s, step, self.columns)) for s in range(self.columns)]
        return lax.ppermute(array_in, "dp", pairs)

    def to_core(self, array_in):
        return lax.ppermute(array_in, "seq", [(s, s ^ 1) for s in range(self.n)])

    def to_owner(self, array_in, step, back=False):
        move = source_index if back else swap_index
        pairs = [
            (s, move(s // self.group, step, self.seqs) * self.group + s % self.group)
            for s in range(self.n)
        ]
        return lax.ppermute(array_in, "seq", pairs)

    def to_member(self, array_in, step, back=False):
        shift = -step if back else step
        pairs = [
            (s, (s // self.group) * self.group + (s % self.group + shift) % self.group)
            for s in range(self.n)
        ]
        return lax.ppermute(array_in, "seq", pairs)


def take_block(array_in, index):
    return lax.dynamic_index_in_dim(array_in, index, 0, keepdims=False)


def to_sequences(grid, array_in):
    parts = [take_block(array_in, grid.owner)]
    for step in range(1, grid.seqs):
        target = swap_index(grid.owner, step, grid.seqs)
        parts.append(grid.to_owner(take_block(array_in, target), step))
    return jnp.concatenate(parts, axis=0)


def from_sequences(grid, rows, length):
    blocks = rows.reshape(grid.seqs, length, rows.shape[1])
    out = jnp.zeros_like(blocks)
    out = lax.dynamic_update_index_in_dim(out, blocks[0], grid.owner, 0)
    for step in range(1, grid.seqs):
        got = grid.to_owner(blocks[step], step, back=True)
        place = swap_index(grid.owner, step, grid.seqs)
        out = lax.dynamic_update_index_in_dim(out, got, place, 0)
    return out


def row_positions(grid, length):
    def positions(member):
        spots = []
        for step in range(grid.seqs):
            source = source_index(grid.owner, step, grid.seqs)
            spots.append((source * grid.group + member) * length + jnp.arange(length, dtype=jnp.int32))
        return jnp.concatenate(spots)

    return positions


def gather_packed(grid, shard):
    parts = [shard] + [grid.to_chip(shard, step) for step in range(1, grid.chips)]
    chips = jnp.stack(parts)
    wide = [chips] + [grid.to_column(chips, step) for step in range(1, grid.columns)]
    mine = jnp.concatenate(wide, axis=0)
    other = grid.to_core(mine)
    return mine, other


def relative_order(grid):
    column = jnp.arange(grid.columns, dtype=jnp.int32)[:, None]
    chip = jnp.arange(grid.chips, dtype=jnp.int32)[None, :]
    if grid.columns & (grid.columns - 1) == 0:
        column_step = column ^ grid.column
    else:
        column_step = (grid.column - column) % grid.columns
    if grid.chips & (grid.chips - 1) == 0:
        chip_step = chip ^ grid.chip
    else:
        chip_step = (grid.chip - chip) % grid.chips
    return (column_step * grid.chips + chip_step).reshape(-1)


def assemble(grid, mine, other, cuts):
    order = relative_order(grid)
    count, rows, width = mine.shape
    spot = jnp.concatenate([grid.core[None].astype(jnp.int32), order])
    wides = [sum(piece[3] for piece in pieces) for _, pieces in cuts]
    if any(height % 8 for height, _ in cuts):
        first = jnp.where(grid.core == 0, mine, other)[order]
        second = jnp.where(grid.core == 0, other, mine)[order]
        both = jnp.stack([first, second], axis=1).reshape(2 * count, rows, width)
        outs = []
        for height, pieces in cuts:
            ordered = sorted(pieces, key=lambda piece: piece[2])
            strips = [both[:, p[0] : p[0] + height, p[1] : p[1] + p[3]] for p in ordered]
            outs.append(jnp.concatenate(strips, axis=2).reshape(2 * count * height, -1))
        return outs

    def kernel(spot_ref, mine_ref, other_ref, *out_refs):
        for core in range(2):

            @pl.when(spot_ref[0] == core)
            def _(core=core):
                for source, place in ((mine_ref, core), (other_ref, 1 - core)):
                    for (height, pieces), out_ref in zip(cuts, out_refs):
                        for row, column, target, columns in pieces:
                            out_ref[place * height : (place + 1) * height, target : target + columns] = source[
                                row : row + height, column : column + columns
                            ]

    return pl.pallas_call(
        kernel,
        grid_spec=pltpu.PrefetchScalarGridSpec(
            num_scalar_prefetch=1,
            grid=(count,),
            in_specs=[
                pl.BlockSpec((None, rows, width), lambda i, spot: (spot[i + 1], 0, 0)),
                pl.BlockSpec((None, rows, width), lambda i, spot: (spot[i + 1], 0, 0)),
            ],
            out_specs=[
                pl.BlockSpec((2 * height, wide), lambda i, spot: (i, 0))
                for (height, _), wide in zip(cuts, wides)
            ],
        ),
        out_shape=[
            jax.ShapeDtypeStruct((2 * count * height, wide), mine.dtype)
            for (height, _), wide in zip(cuts, wides)
        ],
        cost_estimate=pl.CostEstimate(flops=0, bytes_accessed=8 * count * rows * width, transcendentals=0),
        name="assemble",
    )(spot, mine, other)


def scatter_sum(grid, array_in):
    width = array_in.shape[1]
    blocks = array_in.reshape(grid.columns * grid.chips, 2, -1, width)
    keep = lax.dynamic_index_in_dim(blocks, grid.core, 1, keepdims=False)
    send = lax.dynamic_index_in_dim(blocks, 1 - grid.core, 1, keepdims=False)
    half = (keep.astype(F32) + grid.to_core(send).astype(F32)).astype(BF)
    half = half.reshape(grid.columns, -1, width)
    total = take_block(half, grid.column).astype(F32)
    for step in range(1, grid.columns):
        target = swap_index(grid.column, step, grid.columns)
        total = total + grid.to_column(take_block(half, target), step).astype(F32)
    part = total.astype(BF).reshape(grid.chips, -1, width)
    total = take_block(part, grid.chip).astype(F32)
    for step in range(1, grid.chips):
        target = swap_index(grid.chip, step, grid.chips)
        total = total + grid.to_chip(take_block(part, target), step).astype(F32)
    return total


PARTS = 3
LOG2E = 1.4426950408889634
SCALE = 0.125 * LOG2E


def dot_nt(left, right):
    return lax.dot_general(left, right, (((1,), (1,)), ((), ())), preferred_element_type=F32)


def own_lanes(half, count):
    lane = lax.broadcasted_iota(jnp.int32, (count, 2 * HD), 1)
    return (lane // HD) == half, lane == HD * (1 - half)


def attention(part, inputs, others, key_bias, context, log_totals, block=256):
    rows, width = inputs.shape
    pairs = width // (6 * HD)
    sources = [inputs] + list(others)
    count = len(sources)
    keys = rows * count

    def kernel(q_ref, bias_ref, *refs):
        k_refs, v_refs = refs[:count], refs[count : 2 * count]
        o_ref, l_ref, k_own, v_own = refs[-4:]

        @pl.when(pl.program_id(1) == 0)
        def _():
            for half in range(2):
                own, spare = own_lanes(half, rows)
                zero = jnp.zeros((rows, 2 * HD), BF)
                for i in range(count):
                    at = slice(i * rows, (i + 1) * rows)
                    k_own[half, at, :] = jnp.where(own, k_refs[i][...], jnp.where(spare, bias_ref[at, :], zero))
                    v_own[half, at, :] = jnp.where(own, v_refs[i][...], jnp.where(spare, zero + 1, zero))

        query = q_ref[...]
        results = []
        for half in range(2):
            own, spare = own_lanes(half, block)
            zero = jnp.zeros_like(query)
            query_h = jnp.where(own, query, jnp.where(spare, zero + 1, zero))
            scores = dot_nt(query_h, k_own[half])
            largest = jnp.max(scores, axis=1, keepdims=True)
            weights = jnp.exp2((scores - largest) * SCALE).astype(BF)
            summed = matmul(weights, v_own[half])
            totals = summed[:, HD * (1 - half) : HD * (1 - half) + 1]
            results.append(summed / totals)
            log_total = jnp.broadcast_to(largest * SCALE + jnp.log2(totals), (block, 2 * HD))
            l_ref[half : half + 1, :] = jnp.transpose(log_total)[0:1, :]
        lane = lax.broadcasted_iota(jnp.int32, (block, 2 * HD), 1)
        o_ref[...] = jnp.where(lane < HD, results[0], results[1]).astype(BF)

    def columns(first):
        return [pl.BlockSpec((rows, 2 * HD), lambda i, j: (0, i + first)) for _ in range(count)]

    first = part * pairs
    arguments = [inputs, key_bias] + sources + sources
    specs = [
        pl.BlockSpec((block, 2 * HD), lambda i, j: (j, i)),
        pl.BlockSpec((keys, 2 * HD), lambda i, j: (0, 0)),
    ]
    specs = specs + columns(pairs) + columns(2 * pairs)
    aliases = {}
    if context is not None:
        aliases = {len(arguments): 0, len(arguments) + 1: 1}
        arguments = arguments + [context, log_totals]
        specs = specs + [pl.BlockSpec(memory_space=pl.ANY)] * 2
    heads = 2 * pairs
    return pl.pallas_call(
        kernel,
        grid=(pairs, rows // block),
        in_specs=specs,
        out_specs=[
            pl.BlockSpec((block, 2 * HD), lambda i, j: (j, i + first)),
            pl.BlockSpec((None, 8, block), lambda i, j: (i + first, 0, j)),
        ],
        out_shape=[
            jax.ShapeDtypeStruct((rows, H * HD), BF),
            jax.ShapeDtypeStruct((H // 2, 8, rows), F32),
        ],
        scratch_shapes=[pltpu.VMEM((2, keys, 2 * HD), BF), pltpu.VMEM((2, keys, 2 * HD), BF)],
        input_output_aliases=aliases,
        compiler_params=pltpu.CompilerParams(vmem_limit_bytes=40 << 20),
        cost_estimate=pl.CostEstimate(
            flops=16 * heads * rows * keys * HD, bytes_accessed=8 * rows * width, transcendentals=heads * rows * keys
        ),
        name="attention",
    )(*arguments)


def attention_back(part, inputs, others, key_bias, log_totals, context, grad_context, block=256, chunk=1024):
    rows, width = inputs.shape
    pairs = width // (6 * HD)
    sources = [inputs] + list(others)
    count = len(sources)
    keys = rows * count
    blocks = rows // block
    chunk = min(chunk, rows)
    chunks = keys // chunk

    def kernel(q_ref, bias_ref, l_ref, o_ref, g_ref, *refs):
        k_refs, v_refs = refs[:count], refs[count : 2 * count]
        out_ref, other_refs = refs[2 * count], refs[2 * count + 1 : 3 * count]
        k_own, k_turned, v_all, grad_k, grad_v = refs[3 * count :]
        for i in range(count):
            at = slice(i * rows, (i + 1) * rows)
            v_all[at, :] = v_refs[i][...]
            for half in range(2):
                own, spare = own_lanes(half, rows)
                key = k_refs[i][...]
                zero = jnp.zeros_like(key)
                k_own[half, at, :] = jnp.where(own, key, jnp.where(spare, bias_ref[at, :], zero))
                k_turned[half, :, at] = jnp.transpose(jnp.where(own, key, zero))
        grad_k[...] = jnp.zeros_like(grad_k)
        grad_v[...] = jnp.zeros_like(grad_v)
        place = pl.program_id(0)

        @pl.loop(0, blocks)
        def _(j):
            at = pl.ds(pl.multiple_of(j * block, block), block)
            query, grad = q_ref[at, :], g_ref[at, :]
            turned = jnp.transpose(grad.astype(F32) * o_ref[at, :].astype(F32))
            asks, plain, grads, centres, logs = [], [], [], [], []
            for half in range(2):
                own, spare = own_lanes(half, block)
                zero = jnp.zeros_like(query)
                asks.append(jnp.where(own, query, jnp.where(spare, zero + 1, zero)))
                plain.append(jnp.where(own, query, zero))
                grads.append(jnp.where(own, grad, zero))
                centres.append(jnp.sum(turned[HD * half : HD * half + HD], axis=0, keepdims=True))
                logs.append(l_ref[half : half + 1, at])
            grad_q = None
            for c in range(chunks):
                span = slice(c * chunk, (c + 1) * chunk)
                weights, slopes = [], []
                for half in range(2):
                    scores = dot_nt(k_own[half, span, :], asks[half])
                    grad_weights = dot_nt(v_all[span, :], grads[half])
                    exact = jnp.exp2(scores * SCALE - logs[half])
                    slope = (exact * (grad_weights - centres[half])).astype(BF)
                    weights.append(exact.astype(BF))
                    slopes.append(slope)
                    step = matmul(k_turned[half, :, span], slope)
                    grad_q = step if grad_q is None else grad_q + step
                grad_v[span, :] += matmul(weights[0], grads[0]) + matmul(weights[1], grads[1])
                grad_k[span, :] += matmul(slopes[0], plain[0]) + matmul(slopes[1], plain[1])
            columns = pl.ds(pl.multiple_of(place * 2 * HD, 2 * HD), 2 * HD)
            out_ref[at, columns] = (jnp.transpose(grad_q) * 0.125).astype(BF)

        for i in range(count):
            at = slice(i * rows, (i + 1) * rows)
            target, shift = (out_ref, pairs) if i == 0 else (other_refs[i - 1], 0)
            for value, offset, scale in ((grad_k, 0, 0.125), (grad_v, pairs, 1.0)):
                first_column = pl.multiple_of((place + shift + offset) * 2 * HD, 2 * HD)
                target[:, pl.ds(first_column, 2 * HD)] = (value[at, :] * scale).astype(BF)

    def column(first):
        return pl.BlockSpec((rows, 2 * HD), lambda i: (0, i + first))

    first = part * pairs
    heads = 2 * pairs
    return pl.pallas_call(
        kernel,
        grid=(pairs,),
        in_specs=[
            column(0),
            pl.BlockSpec((keys, 2 * HD), lambda i: (0, 0)),
            pl.BlockSpec((None, 8, rows), lambda i: (i + first, 0, 0)),
            column(first),
            column(first),
        ]
        + [column(pairs)] * count
        + [column(2 * pairs)] * count,
        out_specs=[pl.BlockSpec((rows, width), lambda i: (0, 0))]
        + [pl.BlockSpec((rows, 4 * HD * pairs), lambda i: (0, 0))] * (count - 1),
        out_shape=[jax.ShapeDtypeStruct((rows, width), BF)]
        + [jax.ShapeDtypeStruct((rows, 4 * HD * pairs), BF)] * (count - 1),
        scratch_shapes=[
            pltpu.VMEM((2, keys, 2 * HD), BF),
            pltpu.VMEM((2, 2 * HD, keys), BF),
            pltpu.VMEM((keys, 2 * HD), BF),
            pltpu.VMEM((keys, 2 * HD), F32),
            pltpu.VMEM((keys, 2 * HD), F32),
        ],
        compiler_params=pltpu.CompilerParams(vmem_limit_bytes=48 << 20),
        cost_estimate=pl.CostEstimate(
            flops=40 * heads * rows * keys * HD, bytes_accessed=12 * rows * width, transcendentals=heads * rows * keys
        ),
        name="attention_back",
    )(inputs, key_bias, log_totals, context, grad_context, *sources, *sources)


def body(
    tokens,
    lengths,
    query_weight,
    key_weight,
    value_weight,
    out_weight,
    up_weight,
    down_weight,
    query_bias,
    value_bias,
    out_bias,
    up_bias,
    down_bias,
    first_gain,
    first_shift,
    second_gain,
    second_shift,
    cotangent,
):
    seqs, length, width = tokens.shape
    grid = Grid(seqs)
    devices = grid.columns * grid.n
    slim = query_weight.shape[0]
    hidden = up_weight.shape[1]
    tall = hidden // devices
    wide = hidden // width

    flat_in = to_sequences(grid, tokens)

    vectors = (
        query_bias,
        value_bias,
        out_bias,
        down_bias,
        first_gain,
        first_shift,
        second_gain,
        second_shift,
    )
    vector_row = jnp.concatenate(vectors + (up_bias,))
    vector_size = vector_row.shape[0]
    vector_rows = jnp.zeros((8, width), BF).at[0, :vector_size].set(vector_row)
    early = jnp.concatenate([query_weight, key_weight, value_weight, vector_rows], axis=0)
    ups = [up_weight[:, i * width : (i + 1) * width] for i in range(wide)]
    late = jnp.concatenate([out_weight] + ups, axis=0)
    strip = width // PARTS
    cuts = [
        (slim, tuple((i * slim, part * strip, i * strip, strip) for i in range(3))) for part in range(PARTS)
    ]
    cuts.append((8, ((3 * slim, 0, 0, width),)))
    *into_full, vector_full = assemble(grid, *gather_packed(grid, early), cuts)
    cuts = [
        (slim, ((0, 0, 0, width),)),
        (slim, tuple((slim * (1 + i), 0, i * width, width) for i in range(wide))),
    ]
    out_full, up_full = assemble(grid, *gather_packed(grid, late), cuts)
    (down_full,) = assemble(grid, *gather_packed(grid, down_weight), [(tall, ((0, 0, 0, width),))])
    vector_table = vector_full.reshape(devices, 8, width)[:, 0, :vector_size]
    small = vector_table[:, : 8 * slim].reshape(devices, 8, slim).transpose(1, 0, 2)
    small = small.reshape(8, width).astype(F32)
    query_add, value_add, out_add, down_add, gain_one, shift_one, gain_two, shift_two = (
        small[i] for i in range(8)
    )
    up_add = vector_table[:, 8 * slim :].reshape(hidden).astype(F32)

    positions = row_positions(grid, length)
    my_length = take_block(lengths, grid.owner)
    live_rows = (positions(grid.member) < my_length).astype(F32)[:, None]
    key_bias = jnp.concatenate(
        [
            jnp.where(positions((grid.member - step) % grid.group) < my_length, 0.0, -1e30)
            for step in range(grid.group)
        ]
    ).astype(F32)

    key_bias = jnp.broadcast_to(key_bias[:, None], (key_bias.shape[0], 2 * HD)).astype(BF)
    inputs, others = [], []
    for part in range(PARTS):
        at = slice(part * strip, (part + 1) * strip)
        add = jnp.concatenate([query_add[at], jnp.zeros((strip,), F32), value_add[at]])
        own = (matmul(flat_in, into_full[part]) + add).astype(BF)
        inputs.append(own)
        others.append([grid.to_member(own, step) for step in range(1, grid.group)])
    context, log_totals = None, None
    for part in range(PARTS):
        context, log_totals = attention(part, inputs[part], others[part], key_bias, context, log_totals)
    grad_in = to_sequences(grid, cotangent)

    first_sum = flat_in.astype(F32) + matmul(context, out_full) + out_add
    first_norm, first_unit, first_factor = normalize(first_sum, gain_one, shift_one)
    first_low = first_norm.astype(BF)
    up_pre = matmul(first_low, up_full) + up_add
    activated = jax.nn.gelu(up_pre, approximate=False).astype(BF)
    second_sum = first_low.astype(F32) + matmul(activated, down_full) + down_add
    second_norm, second_unit, second_factor = normalize(second_sum, gain_two, shift_two)
    output = from_sequences(grid, (second_norm * live_rows).astype(BF), length)

    grad_output = grad_in.astype(F32) * live_rows
    grad_gain_two = jnp.sum(grad_output * second_unit, axis=0)
    grad_shift_two = jnp.sum(grad_output, axis=0)
    grad_second = norm_back(grad_output, second_unit, second_factor, gain_two)
    grad_branch = grad_second.astype(BF)
    grad_down_add = jnp.sum(grad_branch.astype(F32), axis=0)
    grad_down = left_product(activated, grad_branch).astype(BF)
    grad_up_low = (right_product(grad_branch, down_full) * gelu_slope(up_pre)).astype(BF)
    grad_up_add = jnp.sum(grad_up_low.astype(F32), axis=0)
    grad_up = left_product(first_low, grad_up_low).astype(BF)
    grad_first = right_product(grad_up_low, up_full) + grad_second
    grad_gain_one = jnp.sum(grad_first * first_unit, axis=0)
    grad_shift_one = jnp.sum(grad_first, axis=0)
    grad_residual = norm_back(grad_first, first_unit, first_factor, gain_one)
    grad_attend = grad_residual.astype(BF)
    grad_out_add = jnp.sum(grad_attend.astype(F32), axis=0)
    grad_out = left_product(context, grad_attend).astype(BF)
    grad_context = right_product(grad_attend, out_full).astype(BF)

    grad_down_own = scatter_sum(grid, grad_down)
    grad_up_own = scatter_sum(grid, grad_up)
    grad_out_own = scatter_sum(grid, grad_out)

    tokens_grad = grad_residual
    grad_into_own, query_adds, value_adds = [], [], []
    for part in range(PARTS):
        own, *away = attention_back(
            part, inputs[part], others[part], key_bias, log_totals, context, grad_context
        )
        grad_kv = own[:, strip:].astype(F32)
        for step, piece in enumerate(away, 1):
            grad_kv = grad_kv + grid.to_member(piece, step, back=True).astype(F32)
        low = jnp.concatenate([own[:, :strip], grad_kv.astype(BF)], axis=1)
        query_adds.append(jnp.sum(low[:, :strip].astype(F32), axis=0))
        value_adds.append(jnp.sum(low[:, 2 * strip :].astype(F32), axis=0))
        tokens_grad = tokens_grad + right_product(low, into_full[part])
        grad_into_own.append(scatter_sum(grid, left_product(flat_in, low).astype(BF)))
    tokens_grad = from_sequences(grid, tokens_grad.astype(BF), length).astype(F32)

    def pack(grads):
        count = len(grads)
        table = jnp.stack(grads).reshape(count, devices, slim).transpose(1, 0, 2)
        return table.reshape(devices, count * slim)

    middle = pack([grad_out_add, grad_down_add, grad_gain_one, grad_shift_one, grad_gain_two, grad_shift_two])
    middle = jnp.concatenate([middle, grad_up_add.reshape(devices, tall)], axis=1).astype(BF)
    middle_own = scatter_sum(grid, middle)[0]
    last = pack([jnp.concatenate(query_adds), jnp.concatenate(value_adds)]).astype(BF)
    last_own = scatter_sum(grid, last)[0]
    vector_outs = [last_own[:slim], last_own[slim:]]
    vector_outs = vector_outs + [middle_own[i * slim : (i + 1) * slim] for i in range(6)]
    up_add_own = middle_own[6 * slim :]
    matrix_outs = [
        jnp.concatenate([own[:, i * strip : (i + 1) * strip] for own in grad_into_own], axis=1)
        for i in range(3)
    ]
    return (
        output,
        tokens_grad,
        matrix_outs[0],
        matrix_outs[1],
        matrix_outs[2],
        grad_out_own,
        grad_up_own,
        grad_down_own,
        vector_outs[0],
        vector_outs[1],
        vector_outs[2],
        up_add_own,
        vector_outs[3],
        vector_outs[4],
        vector_outs[5],
        vector_outs[6],
        vector_outs[7],
    )


def solution(mesh):
    whole = ("dp", "seq")
    matrix, vector, rows = P(whole, None), P(whole), P("dp", "seq", None)
    return jax.shard_map(
        body,
        mesh=mesh,
        in_specs=(rows, P("dp")) + (matrix,) * 6 + (vector,) * 9 + (rows,),
        out_specs=(rows, rows) + (matrix,) * 6 + (vector,) * 9,
        check_vma=False,
    )
```

```python
import jax
import jax.numpy as jnp
from jax import lax
from jax.experimental import pallas as pl
from jax.experimental.pallas import tpu as pltpu
from jax.sharding import PartitionSpec as P

H = 12
HD = 64

EPSILON = 1e-05
ROOT_HALF = 0.7071067811865476
INV_ROOT_TWO_PI = 0.3989422804014327
BF = jnp.bfloat16
F32 = jnp.float32


def matmul(left, right):
    return jnp.dot(left, right, preferred_element_type=F32)


def left_product(left, right):
    return lax.dot_general(left, right, (((0,), (0,)), ((), ())), preferred_element_type=F32)


def right_product(left, right):
    return lax.dot_general(left, right, (((1,), (1,)), ((), ())), preferred_element_type=F32)


def normalize(inputs, gains, shifts):
    centre = inputs - jnp.mean(inputs, axis=-1, keepdims=True)
    factor = lax.rsqrt(jnp.mean(centre * centre, axis=-1, keepdims=True) + EPSILON)
    unit_rows = centre * factor
    return (unit_rows * gains + shifts, unit_rows, factor)


def norm_back(grad_in, unit_rows, factor, gains):
    grad_unit = grad_in * gains
    return factor * (
        grad_unit
        - jnp.mean(grad_unit, axis=-1, keepdims=True)
        - unit_rows * jnp.mean(grad_unit * unit_rows, axis=-1, keepdims=True)
    )


def gelu_slope(inputs):
    return 0.5 * (1.0 + lax.erf(inputs * ROOT_HALF)) + inputs * INV_ROOT_TWO_PI * jnp.exp(
        -0.5 * inputs * inputs
    )


def swap_index(place, step, count):
    if count & (count - 1) == 0:
        return place ^ step
    return (place + step) % count


def source_index(place, step, count):
    if count & (count - 1) == 0:
        return place ^ step
    return (place - step) % count


class Grid:
    def __init__(self, seqs):
        self.columns = lax.axis_size("dp")
        self.n = lax.axis_size("seq")
        self.seqs = seqs
        self.group = self.n // seqs
        self.chips = self.n // 2
        self.column = lax.axis_index("dp")
        place = lax.axis_index("seq")
        self.chip = place // 2
        self.core = place % 2
        self.owner = place // self.group
        self.member = place % self.group

    def to_chip(self, array_in, step):
        pairs = [(s, swap_index(s // 2, step, self.chips) * 2 + s % 2) for s in range(self.n)]
        return lax.ppermute(array_in, "seq", pairs)

    def to_column(self, array_in, step):
        pairs = [(s, swap_index(s, step, self.columns)) for s in range(self.columns)]
        return lax.ppermute(array_in, "dp", pairs)

    def to_core(self, array_in):
        return lax.ppermute(array_in, "seq", [(s, s ^ 1) for s in range(self.n)])

    def to_owner(self, array_in, step, back=False):
        move = source_index if back else swap_index
        pairs = [
            (s, move(s // self.group, step, self.seqs) * self.group + s % self.group)
            for s in range(self.n)
        ]
        return lax.ppermute(array_in, "seq", pairs)

    def to_member(self, array_in, step, back=False):
        shift = -step if back else step
        pairs = [
            (s, (s // self.group) * self.group + (s % self.group + shift) % self.group)
            for s in range(self.n)
        ]
        return lax.ppermute(array_in, "seq", pairs)


def take_block(array_in, index):
    return lax.dynamic_index_in_dim(array_in, index, 0, keepdims=False)


def to_sequences(grid, array_in):
    out = jnp.zeros_like(array_in)
    out = lax.dynamic_update_index_in_dim(out, take_block(array_in, grid.owner), grid.owner, 0)
    for step in range(1, grid.seqs):
        place = swap_index(grid.owner, step, grid.seqs)
        got = grid.to_owner(take_block(array_in, place), step)
        out = lax.dynamic_update_index_in_dim(out, got, place, 0)
    return out.reshape(-1, array_in.shape[2])


def from_sequences(grid, rows, length):
    return to_sequences(grid, rows.reshape(grid.seqs, length, rows.shape[1])).reshape(grid.seqs, length, -1)


def row_positions(grid, length):
    def positions(member):
        source = jnp.arange(grid.seqs, dtype=jnp.int32)[:, None]
        return ((source * grid.group + member) * length + jnp.arange(length, dtype=jnp.int32)).reshape(-1)

    return positions


MESH = pl.DeviceIdType.MESH
HBM = pl.BlockSpec(memory_space=pl.ANY)


def remote(source, target, send, receive, device):
    return pltpu.make_async_remote_copy(
        src_ref=source, dst_ref=target, send_sem=send, recv_sem=receive, device_id=device, device_id_type=MESH
    )


def meet(devices):
    barrier = pltpu.get_barrier_semaphore()
    for device in devices:
        pl.semaphore_signal(barrier, inc=1, device_id=device, device_id_type=MESH)
    pl.semaphore_wait(barrier, len(devices))


class Place:
    def __init__(self, grid):
        self.columns, self.chips, self.n = grid.columns, grid.chips, grid.n
        self.seqs, self.group = grid.seqs, grid.group
        self.column = lax.axis_index("dp")
        self.spot = lax.axis_index("seq")
        self.chip = lax.div(self.spot, 2)
        self.core = lax.rem(self.spot, 2)
        self.owner = lax.div(self.spot, self.group)
        self.member = lax.rem(self.spot, self.group)

    def near(self, chip_step):
        return (self.column, (self.chip ^ chip_step) * 2 + self.core)

    def beside(self, column_step):
        return (self.column ^ column_step, self.spot)

    def twin(self):
        return (self.column, self.chip * 2 + (1 - self.core))

    def at_owner(self, step):
        return (self.column, (self.owner ^ step) * self.group + self.member)

    def at_member(self, step):
        return (self.column, self.owner * self.group + lax.rem(self.member + step, self.group))

    def index(self, column_step, chip_step, other=False):
        core = 1 - self.core if other else self.core
        return ((self.column ^ column_step) * self.chips + (self.chip ^ chip_step)) * 2 + core

    def neighbours(self):
        chips = [self.near(step) for step in range(1, self.chips)]
        columns = [self.beside(step) for step in range(1, self.columns)]
        return chips + columns + [self.twin()]


class Gather:
    def __init__(self, place, arrays, send, receive):
        self.place, self.arrays, self.send, self.receive = place, arrays, send, receive
        self.square = place.columns == 4
        self.sent = []

    def copies(self, kind, column_step, chip_step, device, own=False, where=None):
        slot = column_step * self.place.chips + chip_step
        for k, (shard, whole, block) in enumerate(self.arrays):
            held = block(whole, self.place.index(*(where or (column_step, chip_step))))
            yield remote(
                shard if own else held, held, self.send.at[k, kind, slot], self.receive.at[k, kind, slot], device
            )

    def begin(self, kind, column_step, chip_step, device, own=False, where=None):
        self.sent.append((kind, column_step, chip_step, own, where))
        for copy in self.copies(kind, column_step, chip_step, device, own, where):
            copy.start()

    def to_twin(self, column_step, chip_step, own=False):
        self.begin(1, column_step, chip_step, self.place.twin(), own=own)

    def outward(self, chip_step):
        place, own = self.place, chip_step == 0
        for step in range(1, place.columns):
            if not (self.square and step == 3):
                self.begin(0, step, chip_step, place.beside(step), own=own, where=(0, chip_step))
        self.to_twin(0, chip_step, own=own)

    def start(self):
        for step in range(1, self.place.chips):
            self.begin(0, 0, step, self.place.near(step), own=True, where=(0, 0))
        self.outward(0)

    def arrive(self, column_step, chip_step, other=False):
        for k, (_, whole, block) in enumerate(self.arrays):
            held = block(whole, self.place.index(column_step, chip_step, other))
            kind = 1 if other else 0
            slot = column_step * self.place.chips + chip_step
            remote(
                held, held, self.send.at[k, kind, slot], self.receive.at[k, kind, slot], self.place.twin()
            ).wait_recv()

    def from_chip(self, chip_step):
        self.arrive(0, chip_step)
        self.outward(chip_step)

    def from_columns(self, chip_step):
        for step in range(1, self.place.columns):
            if self.square and step == 3:
                continue
            self.arrive(step, chip_step)
            if self.square and step == 1 + chip_step % 2:
                self.begin(0, 3, chip_step, self.place.beside(3 - step), where=(step, chip_step))
            self.to_twin(step, chip_step)

    def from_corner(self, chip_step):
        if self.square:
            self.arrive(3, chip_step)
            self.to_twin(3, chip_step)

    def finish(self):
        place = self.place
        for column_step in range(place.columns):
            for chip_step in range(place.chips):
                self.arrive(column_step, chip_step, other=True)
        for kind, column_step, chip_step, own, where in self.sent:
            for copy in self.copies(kind, column_step, chip_step, place.twin(), own, where):
                copy.wait_send()


def gather_semaphores(grid, count):
    shape = (count, 2, grid.columns * grid.chips)
    return [pltpu.SemaphoreType.DMA(shape), pltpu.SemaphoreType.DMA(shape)]


def through(source, held, target, sem):
    copy = pltpu.make_async_copy(source, held, sem)
    copy.start()
    copy.wait()
    copy = pltpu.make_async_copy(held, target, sem)
    copy.start()
    copy.wait()


def start_exchange(grid, tokens, into, vectors):
    seqs, length, width = tokens.shape
    devices = grid.columns * grid.n
    parts, slim, _ = into.shape

    def kernel(
        tokens_ref, into_ref, vectors_ref, rows_ref, into_all, vectors_all, *scratch
    ):
        row_hold, into_hold, vector_hold, hold_sem, send, receive, row_send, row_receive = scratch
        place = Place(grid)
        meet(place.neighbours())
        gather = Gather(
            place,
            [
                (into_ref, into_all, lambda ref, i: ref.at[:, i]),
                (vectors_ref, vectors_all, lambda ref, i: ref.at[i]),
            ],
            send,
            receive,
        )
        gather.start()

        def row_copy(step):
            return remote(
                tokens_ref.at[place.owner ^ step],
                rows_ref.at[place.owner],
                row_send.at[step],
                row_receive.at[step],
                place.at_owner(step),
            )

        for step in range(1, seqs):
            row_copy(step).start()
        me = place.index(0, 0)
        through(into_ref, into_hold, into_all.at[:, me], hold_sem)
        through(vectors_ref, vector_hold, vectors_all.at[me], hold_sem)
        through(tokens_ref.at[place.owner], row_hold, rows_ref.at[place.owner], hold_sem)
        for step in range(1, place.chips):
            gather.from_chip(step)
            gather.from_columns(step - 1)
        gather.from_columns(place.chips - 1)
        for step in range(place.chips):
            gather.from_corner(step)
        gather.finish()
        for step in range(1, seqs):
            landed = rows_ref.at[place.owner ^ step]
            remote(
                landed, landed, row_send.at[step], row_receive.at[step], place.at_owner(step)
            ).wait_recv()
            row_copy(step).wait_send()

    shapes = [tokens.shape, (parts, devices, slim, width), (devices,) + vectors.shape]
    return pl.pallas_call(
        kernel,
        in_specs=[HBM] * 3,
        out_specs=[HBM] * 3,
        out_shape=[jax.ShapeDtypeStruct(shape, BF) for shape in shapes],
        scratch_shapes=[
            pltpu.VMEM(tokens.shape[1:], BF),
            pltpu.VMEM(into.shape, BF),
            pltpu.VMEM(vectors.shape, BF),
            pltpu.SemaphoreType.DMA(()),
        ]
        + gather_semaphores(grid, 2)
        + [pltpu.SemaphoreType.DMA((seqs,)), pltpu.SemaphoreType.DMA((seqs,))],
        compiler_params=pltpu.CompilerParams(collective_id=0, has_side_effects=True),
        name="start_exchange",
    )(tokens, into, vectors)


def scatter_sum(grid, array_in):
    width = array_in.shape[1]
    blocks = array_in.reshape(grid.columns * grid.chips, 2, -1, width)
    keep = lax.dynamic_index_in_dim(blocks, grid.core, 1, keepdims=False)
    send = lax.dynamic_index_in_dim(blocks, 1 - grid.core, 1, keepdims=False)
    half = (keep.astype(F32) + grid.to_core(send).astype(F32)).astype(BF)
    half = half.reshape(grid.columns, -1, width)
    total = take_block(half, grid.column).astype(F32)
    for step in range(1, grid.columns):
        target = swap_index(grid.column, step, grid.columns)
        total = total + grid.to_column(take_block(half, target), step).astype(F32)
    part = total.astype(BF).reshape(grid.chips, -1, width)
    total = take_block(part, grid.chip).astype(F32)
    for step in range(1, grid.chips):
        target = swap_index(grid.chip, step, grid.chips)
        total = total + grid.to_chip(take_block(part, target), step).astype(F32)
    return total


LOG2E = 1.4426950408889634
SCALE = 0.125 * LOG2E


def dot_nt(left, right):
    return lax.dot_general(left, right, (((1,), (1,)), ((), ())), preferred_element_type=F32)


def own_lanes(half, count):
    lane = lax.broadcasted_iota(jnp.int32, (count, 2 * HD), 1)
    return (lane // HD) == half, lane == HD * (1 - half)


def attention(grid, inputs, key_bias, shards, block=256):
    rows = inputs.shape[0]
    width = inputs.shape[1] // 3
    pairs = width // (2 * HD)
    count = grid.group
    keys = rows * count
    blocks = rows // block
    steps = pairs * blocks
    devices = grid.columns * grid.n
    late = len(shards)

    def kernel(q_ref, bias_ref, k_ref, v_ref, all_ref, *refs):
        shard_refs = refs[:late]
        o_ref, l_ref = refs[late : late + 2]
        whole_refs = refs[late + 2 : 2 * late + 2]
        k_own, v_own, far, hold_sem, send, receive, far_send, far_receive = refs[2 * late + 2 : 2 * late + 10]
        holds = refs[2 * late + 10 :]
        pair, turn = pl.program_id(0), pl.program_id(1)
        now = pair * blocks + turn
        place = Place(grid)
        gather = Gather(
            place,
            [(s, w, lambda ref, i: ref.at[i]) for s, w in zip(shard_refs, whole_refs)],
            send,
            receive,
        )

        def far_copy(step, which, kind):
            first = pl.multiple_of(which * 2 * HD + (kind + 1) * width, 2 * HD)
            return remote(
                all_ref.at[:, pl.ds(first, 2 * HD)],
                far.at[step - 1, kind, which],
                far_send.at[step - 1, kind, which],
                far_receive.at[step - 1, kind, which],
                place.at_member(step),
            )

        def first_step():
            meet(place.neighbours() + [place.at_member(s) for s in range(1, count) if count > 2])
            for which in range(pairs):
                for step in range(1, count):
                    for kind in range(2):
                        far_copy(step, which, kind).start()
            gather.start()
            me = place.index(0, 0)
            for shard, whole, hold in zip(shard_refs, whole_refs, holds):
                through(shard, hold, whole.at[me], hold_sem)

        plan = [(0.0, first_step)]
        for step in range(1, place.chips):
            plan.append((step * 0.66 / (place.chips - 1), lambda step=step: gather.from_chip(step)))
            plan.append((0.1 + step * 0.66 / (place.chips - 1), lambda step=step: gather.from_columns(step - 1)))

        def last_step():
            gather.from_columns(place.chips - 1)
            for step in range(place.chips):
                gather.from_corner(step)
            gather.finish()
            for step in range(1, count):
                for which in range(pairs):
                    for kind in range(2):
                        far_copy(step, which, kind).wait_send()

        for moment, action in plan:
            pl.when(now == int(moment * steps))(action)

        @pl.when(turn == 0)
        def _():
            for step in range(1, count):
                for kind in range(2):
                    far_copy(step, pair, kind).wait_recv()
            for half in range(2):
                own, spare = own_lanes(half, rows)
                zero = jnp.zeros((rows, 2 * HD), BF)
                for i in range(count):
                    at = slice(i * rows, (i + 1) * rows)
                    key = k_ref[...] if i == 0 else far[i - 1, 0, pair]
                    value = v_ref[...] if i == 0 else far[i - 1, 1, pair]
                    k_own[half, at, :] = jnp.where(own, key, jnp.where(spare, bias_ref[at, :], zero))
                    v_own[half, at, :] = jnp.where(own, value, jnp.where(spare, zero + 1, zero))

        query = q_ref[...]
        results = []
        for half in range(2):
            own, spare = own_lanes(half, block)
            zero = jnp.zeros_like(query)
            query_h = jnp.where(own, query, jnp.where(spare, zero + 1, zero))
            scores = dot_nt(query_h, k_own[half])
            largest = jnp.max(scores, axis=1, keepdims=True)
            weights = jnp.exp2((scores - largest) * SCALE).astype(BF)
            summed = matmul(weights, v_own[half])
            totals = summed[:, HD * (1 - half) : HD * (1 - half) + 1]
            results.append(summed / totals)
            log_total = jnp.broadcast_to(largest * SCALE + jnp.log2(totals), (block, 2 * HD))
            l_ref[half : half + 1, :] = jnp.transpose(log_total)[0:1, :]
        lane = lax.broadcasted_iota(jnp.int32, (block, 2 * HD), 1)
        o_ref[...] = jnp.where(lane < HD, results[0], results[1]).astype(BF)
        pl.when(now == steps - 1)(last_step)

    def column(first):
        return pl.BlockSpec((rows, 2 * HD), lambda i, j: (0, i + first))

    far_sems = pltpu.SemaphoreType.DMA((max(count - 1, 1), 2, pairs))
    return pl.pallas_call(
        kernel,
        grid=(pairs, blocks),
        in_specs=[
            pl.BlockSpec((block, 2 * HD), lambda i, j: (j, i)),
            pl.BlockSpec((keys, 2 * HD), lambda i, j: (0, 0)),
            column(pairs),
            column(2 * pairs),
            HBM,
        ]
        + [HBM] * late,
        out_specs=[
            pl.BlockSpec((block, 2 * HD), lambda i, j: (j, i)),
            pl.BlockSpec((None, 8, block), lambda i, j: (i, 0, j)),
        ]
        + [HBM] * late,
        out_shape=[
            jax.ShapeDtypeStruct((rows, width), BF),
            jax.ShapeDtypeStruct((pairs, 8, rows), F32),
        ]
        + [jax.ShapeDtypeStruct((devices,) + shard.shape, BF) for shard in shards],
        scratch_shapes=[
            pltpu.VMEM((2, keys, 2 * HD), BF),
            pltpu.VMEM((2, keys, 2 * HD), BF),
            pltpu.VMEM((max(count - 1, 1), 2, pairs, rows, 2 * HD), BF),
            pltpu.SemaphoreType.DMA(()),
        ]
        + gather_semaphores(grid, late)
        + [far_sems, far_sems]
        + [pltpu.VMEM(shard.shape, BF) for shard in shards],
        compiler_params=pltpu.CompilerParams(
            collective_id=1, has_side_effects=True, vmem_limit_bytes=48 << 20
        ),
        cost_estimate=pl.CostEstimate(
            flops=16 * H * rows * keys * HD, bytes_accessed=8 * rows * width, transcendentals=H * rows * keys
        ),
        name="attention",
    )(inputs, key_bias, inputs, inputs, inputs, *shards)


def attention_back(inputs, others, key_bias, log_totals, context, grad_context, block=256, chunk=1024):
    rows, width = inputs.shape
    pairs = width // (6 * HD)
    sources = [inputs] + list(others)
    count = len(sources)
    keys = rows * count
    blocks = rows // block
    chunk = min(chunk, rows)
    chunks = keys // chunk

    def kernel(q_ref, bias_ref, l_ref, o_ref, g_ref, *refs):
        k_refs, v_refs = refs[:count], refs[count : 2 * count]
        out_ref, other_refs = refs[2 * count], refs[2 * count + 1 : 3 * count]
        k_own, k_turned, v_all, grad_k, grad_v = refs[3 * count :]
        for i in range(count):
            at = slice(i * rows, (i + 1) * rows)
            v_all[at, :] = v_refs[i][...]
            for half in range(2):
                own, spare = own_lanes(half, rows)
                key = k_refs[i][...]
                zero = jnp.zeros_like(key)
                k_own[half, at, :] = jnp.where(own, key, jnp.where(spare, bias_ref[at, :], zero))
                k_turned[half, :, at] = jnp.transpose(jnp.where(own, key, zero))
        grad_k[...] = jnp.zeros_like(grad_k)
        grad_v[...] = jnp.zeros_like(grad_v)
        place = pl.program_id(0)

        @pl.loop(0, blocks)
        def _(j):
            at = pl.ds(pl.multiple_of(j * block, block), block)
            query, grad = q_ref[at, :], g_ref[at, :]
            turned = jnp.transpose(grad.astype(F32) * o_ref[at, :].astype(F32))
            asks, plain, grads, centres, logs = [], [], [], [], []
            for half in range(2):
                own, spare = own_lanes(half, block)
                zero = jnp.zeros_like(query)
                asks.append(jnp.where(own, query, jnp.where(spare, zero + 1, zero)))
                plain.append(jnp.where(own, query, zero))
                grads.append(jnp.where(own, grad, zero))
                centres.append(jnp.sum(turned[HD * half : HD * half + HD], axis=0, keepdims=True))
                logs.append(l_ref[half : half + 1, at])
            grad_q = None
            for c in range(chunks):
                span = slice(c * chunk, (c + 1) * chunk)
                weights, slopes = [], []
                for half in range(2):
                    scores = dot_nt(k_own[half, span, :], asks[half])
                    grad_weights = dot_nt(v_all[span, :], grads[half])
                    exact = jnp.exp2(scores * SCALE - logs[half])
                    slope = (exact * (grad_weights - centres[half])).astype(BF)
                    weights.append(exact.astype(BF))
                    slopes.append(slope)
                    step = matmul(k_turned[half, :, span], slope)
                    grad_q = step if grad_q is None else grad_q + step
                grad_v[span, :] += matmul(weights[0], grads[0]) + matmul(weights[1], grads[1])
                grad_k[span, :] += matmul(slopes[0], plain[0]) + matmul(slopes[1], plain[1])
            columns = pl.ds(pl.multiple_of(place * 2 * HD, 2 * HD), 2 * HD)
            out_ref[at, columns] = (jnp.transpose(grad_q) * 0.125).astype(BF)

        for i in range(count):
            at = slice(i * rows, (i + 1) * rows)
            target, shift = (out_ref, pairs) if i == 0 else (other_refs[i - 1], 0)
            for value, offset, scale in ((grad_k, 0, 0.125), (grad_v, pairs, 1.0)):
                first_column = pl.multiple_of((place + shift + offset) * 2 * HD, 2 * HD)
                target[:, pl.ds(first_column, 2 * HD)] = (value[at, :] * scale).astype(BF)

    def column(first):
        return pl.BlockSpec((rows, 2 * HD), lambda i: (0, i + first))

    first = 0
    heads = 2 * pairs
    return pl.pallas_call(
        kernel,
        grid=(pairs,),
        in_specs=[
            column(0),
            pl.BlockSpec((keys, 2 * HD), lambda i: (0, 0)),
            pl.BlockSpec((None, 8, rows), lambda i: (i + first, 0, 0)),
            column(first),
            column(first),
        ]
        + [column(pairs)] * count
        + [column(2 * pairs)] * count,
        out_specs=[pl.BlockSpec((rows, width), lambda i: (0, 0))]
        + [pl.BlockSpec((rows, 4 * HD * pairs), lambda i: (0, 0))] * (count - 1),
        out_shape=[jax.ShapeDtypeStruct((rows, width), BF)]
        + [jax.ShapeDtypeStruct((rows, 4 * HD * pairs), BF)] * (count - 1),
        scratch_shapes=[
            pltpu.VMEM((2, keys, 2 * HD), BF),
            pltpu.VMEM((2, 2 * HD, keys), BF),
            pltpu.VMEM((keys, 2 * HD), BF),
            pltpu.VMEM((keys, 2 * HD), F32),
            pltpu.VMEM((keys, 2 * HD), F32),
        ],
        compiler_params=pltpu.CompilerParams(vmem_limit_bytes=48 << 20),
        cost_estimate=pl.CostEstimate(
            flops=40 * heads * rows * keys * HD, bytes_accessed=12 * rows * width, transcendentals=heads * rows * keys
        ),
        name="attention_back",
    )(inputs, key_bias, log_totals, context, grad_context, *sources, *sources)


def body(
    tokens,
    lengths,
    query_weight,
    key_weight,
    value_weight,
    out_weight,
    up_weight,
    down_weight,
    query_bias,
    value_bias,
    out_bias,
    up_bias,
    down_bias,
    first_gain,
    first_shift,
    second_gain,
    second_shift,
    cotangent,
):
    seqs, length, width = tokens.shape
    grid = Grid(seqs)
    devices = grid.columns * grid.n
    slim = query_weight.shape[0]
    hidden = up_weight.shape[1]
    tall = hidden // devices
    wide = hidden // width

    vectors = (
        query_bias,
        value_bias,
        out_bias,
        down_bias,
        first_gain,
        first_shift,
        second_gain,
        second_shift,
    )
    vector_row = jnp.concatenate(vectors + (up_bias,))
    vector_size = vector_row.shape[0]
    vector_rows = jnp.zeros((8, -(-vector_size // 128) * 128), BF).at[0, :vector_size].set(vector_row)
    into_shard = jnp.stack([query_weight, key_weight, value_weight])
    flat_in, into_full, vector_full = start_exchange(grid, tokens, into_shard, vector_rows)
    flat_in = flat_in.reshape(-1, width)
    into_full = into_full.reshape(3, width, width)
    vector_table = vector_full[:, 0, :vector_size]
    small = vector_table[:, : 8 * slim].reshape(devices, 8, slim).transpose(1, 0, 2)
    small = small.reshape(8, width).astype(F32)
    query_add, value_add, out_add, down_add, gain_one, shift_one, gain_two, shift_two = (
        small[i] for i in range(8)
    )
    up_add = vector_table[:, 8 * slim :].reshape(hidden).astype(F32)

    positions = row_positions(grid, length)
    my_length = take_block(lengths, grid.owner)
    live_rows = (positions(grid.member) < my_length).astype(F32)[:, None]
    key_bias = jnp.concatenate(
        [
            jnp.where(positions((grid.member - step) % grid.group) < my_length, 0.0, -1e30)
            for step in range(grid.group)
        ]
    ).astype(F32)

    key_bias = jnp.broadcast_to(key_bias[:, None], (key_bias.shape[0], 2 * HD)).astype(BF)
    adds = (query_add, jnp.zeros_like(query_add), value_add)
    inputs = [(matmul(flat_in, into_full[i]) + adds[i]).astype(BF) for i in range(3)]
    inputs = jnp.concatenate(inputs, axis=1)
    context, log_totals, out_full, up_full, down_full = attention(
        grid, inputs, key_bias, (out_weight, up_weight, down_weight)
    )
    out_full = out_full.reshape(width, width)
    up_full = up_full.reshape(width, hidden)
    down_full = down_full.reshape(hidden, width)
    others = [grid.to_member(inputs, step) for step in range(1, grid.group)]
    grad_in = to_sequences(grid, cotangent)

    first_sum = flat_in.astype(F32) + matmul(context, out_full) + out_add
    first_norm, first_unit, first_factor = normalize(first_sum, gain_one, shift_one)
    first_low = first_norm.astype(BF)
    up_pre = matmul(first_low, up_full) + up_add
    activated = jax.nn.gelu(up_pre, approximate=False).astype(BF)
    second_sum = first_low.astype(F32) + matmul(activated, down_full) + down_add
    second_norm, second_unit, second_factor = normalize(second_sum, gain_two, shift_two)
    output = from_sequences(grid, (second_norm * live_rows).astype(BF), length)

    grad_output = grad_in.astype(F32) * live_rows
    grad_gain_two = jnp.sum(grad_output * second_unit, axis=0)
    grad_shift_two = jnp.sum(grad_output, axis=0)
    grad_second = norm_back(grad_output, second_unit, second_factor, gain_two)
    grad_branch = grad_second.astype(BF)
    grad_down_add = jnp.sum(grad_branch.astype(F32), axis=0)
    grad_down = left_product(activated, grad_branch).astype(BF)
    grad_up_low = (right_product(grad_branch, down_full) * gelu_slope(up_pre)).astype(BF)
    grad_up_add = jnp.sum(grad_up_low.astype(F32), axis=0)
    grad_up = left_product(first_low, grad_up_low).astype(BF)
    grad_first = right_product(grad_up_low, up_full) + grad_second
    grad_gain_one = jnp.sum(grad_first * first_unit, axis=0)
    grad_shift_one = jnp.sum(grad_first, axis=0)
    grad_residual = norm_back(grad_first, first_unit, first_factor, gain_one)
    grad_attend = grad_residual.astype(BF)
    grad_out_add = jnp.sum(grad_attend.astype(F32), axis=0)
    grad_out = left_product(context, grad_attend).astype(BF)
    grad_context = right_product(grad_attend, out_full).astype(BF)

    grad_down_own = scatter_sum(grid, grad_down)
    grad_up_own = scatter_sum(grid, grad_up)
    grad_out_own = scatter_sum(grid, grad_out)

    own, *away = attention_back(inputs, others, key_bias, log_totals, context, grad_context)
    grad_kv = own[:, width:].astype(F32)
    for step, piece in enumerate(away, 1):
        grad_kv = grad_kv + grid.to_member(piece, step, back=True).astype(F32)
    low = jnp.concatenate([own[:, :width], grad_kv.astype(BF)], axis=1)
    query_adds = jnp.sum(low[:, :width].astype(F32), axis=0)
    value_adds = jnp.sum(low[:, 2 * width :].astype(F32), axis=0)
    tokens_grad = grad_residual
    for i in range(3):
        tokens_grad = tokens_grad + right_product(low[:, i * width : (i + 1) * width], into_full[i])
    grad_into_own = scatter_sum(grid, left_product(flat_in, low).astype(BF))
    tokens_grad = from_sequences(grid, tokens_grad.astype(BF), length).astype(F32)

    def pack(grads):
        count = len(grads)
        table = jnp.stack(grads).reshape(count, devices, slim).transpose(1, 0, 2)
        return table.reshape(devices, count * slim)

    middle = pack([grad_out_add, grad_down_add, grad_gain_one, grad_shift_one, grad_gain_two, grad_shift_two])
    middle = jnp.concatenate([middle, grad_up_add.reshape(devices, tall)], axis=1).astype(BF)
    middle_own = scatter_sum(grid, middle)[0]
    last = pack([query_adds, value_adds]).astype(BF)
    last_own = scatter_sum(grid, last)[0]
    vector_outs = [last_own[:slim], last_own[slim:]]
    vector_outs = vector_outs + [middle_own[i * slim : (i + 1) * slim] for i in range(6)]
    up_add_own = middle_own[6 * slim :]
    matrix_outs = [grad_into_own[:, i * width : (i + 1) * width] for i in range(3)]
    return (
        output,
        tokens_grad,
        matrix_outs[0],
        matrix_outs[1],
        matrix_outs[2],
        grad_out_own,
        grad_up_own,
        grad_down_own,
        vector_outs[0],
        vector_outs[1],
        vector_outs[2],
        up_add_own,
        vector_outs[3],
        vector_outs[4],
        vector_outs[5],
        vector_outs[6],
        vector_outs[7],
    )


def solution(mesh):
    whole = ("dp", "seq")
    matrix, vector, rows = P(whole, None), P(whole), P("dp", "seq", None)
    return jax.shard_map(
        body,
        mesh=mesh,
        in_specs=(rows, P("dp")) + (matrix,) * 6 + (vector,) * 9 + (rows,),
        out_specs=(rows, rows) + (matrix,) * 6 + (vector,) * 9,
        check_vma=False,
    )
```

```python
import jax
import jax.numpy as jnp
from jax import lax
from jax.experimental import pallas as pl
from jax.experimental.pallas import tpu as pltpu
from jax.sharding import PartitionSpec as P

H = 12
HD = 64

EPSILON = 1e-05
ROOT_HALF = 0.7071067811865476
INV_ROOT_TWO_PI = 0.3989422804014327
BF = jnp.bfloat16
F32 = jnp.float32


def matmul(left, right):
    return jnp.dot(left, right, preferred_element_type=F32)


def left_product(left, right):
    return lax.dot_general(left, right, (((0,), (0,)), ((), ())), preferred_element_type=F32)


def right_product(left, right):
    return lax.dot_general(left, right, (((1,), (1,)), ((), ())), preferred_element_type=F32)


def normalize(inputs, gains, shifts):
    centre = inputs - jnp.mean(inputs, axis=-1, keepdims=True)
    factor = lax.rsqrt(jnp.mean(centre * centre, axis=-1, keepdims=True) + EPSILON)
    unit_rows = centre * factor
    return (unit_rows * gains + shifts, unit_rows, factor)


def norm_back(grad_in, unit_rows, factor, gains):
    grad_unit = grad_in * gains
    return factor * (
        grad_unit
        - jnp.mean(grad_unit, axis=-1, keepdims=True)
        - unit_rows * jnp.mean(grad_unit * unit_rows, axis=-1, keepdims=True)
    )


def gelu_slope(inputs):
    return 0.5 * (1.0 + lax.erf(inputs * ROOT_HALF)) + inputs * INV_ROOT_TWO_PI * jnp.exp(
        -0.5 * inputs * inputs
    )


def swap_index(place, step, count):
    if count & (count - 1) == 0:
        return place ^ step
    return (place + step) % count


def source_index(place, step, count):
    if count & (count - 1) == 0:
        return place ^ step
    return (place - step) % count


class Grid:
    def __init__(self, seqs):
        self.columns = lax.axis_size("dp")
        self.n = lax.axis_size("seq")
        self.seqs = seqs
        self.group = self.n // seqs
        self.chips = self.n // 2
        self.column = lax.axis_index("dp")
        place = lax.axis_index("seq")
        self.chip = place // 2
        self.core = place % 2
        self.owner = place // self.group
        self.member = place % self.group

    def to_chip(self, array_in, step):
        pairs = [(s, swap_index(s // 2, step, self.chips) * 2 + s % 2) for s in range(self.n)]
        return lax.ppermute(array_in, "seq", pairs)

    def to_column(self, array_in, step):
        pairs = [(s, swap_index(s, step, self.columns)) for s in range(self.columns)]
        return lax.ppermute(array_in, "dp", pairs)

    def to_core(self, array_in):
        return lax.ppermute(array_in, "seq", [(s, s ^ 1) for s in range(self.n)])

    def to_owner(self, array_in, step, back=False):
        move = source_index if back else swap_index
        pairs = [
            (s, move(s // self.group, step, self.seqs) * self.group + s % self.group)
            for s in range(self.n)
        ]
        return lax.ppermute(array_in, "seq", pairs)

    def to_member(self, array_in, step, back=False):
        shift = -step if back else step
        pairs = [
            (s, (s // self.group) * self.group + (s % self.group + shift) % self.group)
            for s in range(self.n)
        ]
        return lax.ppermute(array_in, "seq", pairs)


def take_block(array_in, index):
    return lax.dynamic_index_in_dim(array_in, index, 0, keepdims=False)


def to_sequences(grid, array_in):
    out = jnp.zeros_like(array_in)
    out = lax.dynamic_update_index_in_dim(out, take_block(array_in, grid.owner), grid.owner, 0)
    for step in range(1, grid.seqs):
        place = swap_index(grid.owner, step, grid.seqs)
        got = grid.to_owner(take_block(array_in, place), step)
        out = lax.dynamic_update_index_in_dim(out, got, place, 0)
    return out.reshape(-1, array_in.shape[2])


def from_sequences(grid, rows, length):
    return to_sequences(grid, rows.reshape(grid.seqs, length, rows.shape[1])).reshape(grid.seqs, length, -1)


def row_positions(grid, length):
    def positions(member):
        source = jnp.arange(grid.seqs, dtype=jnp.int32)[:, None]
        return ((source * grid.group + member) * length + jnp.arange(length, dtype=jnp.int32)).reshape(-1)

    return positions


MESH = pl.DeviceIdType.MESH
HBM = pl.BlockSpec(memory_space=pl.ANY)


def remote(source, target, send, receive, device):
    return pltpu.make_async_remote_copy(
        src_ref=source, dst_ref=target, send_sem=send, recv_sem=receive, device_id=device, device_id_type=MESH
    )


def meet(devices):
    barrier = pltpu.get_barrier_semaphore()
    for device in devices:
        pl.semaphore_signal(barrier, inc=1, device_id=device, device_id_type=MESH)
    pl.semaphore_wait(barrier, len(devices))


class Place:
    def __init__(self, grid):
        self.columns, self.chips, self.n = grid.columns, grid.chips, grid.n
        self.seqs, self.group = grid.seqs, grid.group
        self.column = lax.axis_index("dp")
        self.spot = lax.axis_index("seq")
        self.chip = lax.div(self.spot, 2)
        self.core = lax.rem(self.spot, 2)
        self.owner = lax.div(self.spot, self.group)
        self.member = lax.rem(self.spot, self.group)

    def near(self, chip_step):
        return (self.column, (self.chip ^ chip_step) * 2 + self.core)

    def beside(self, column_step):
        return (self.column ^ column_step, self.spot)

    def twin(self):
        return (self.column, self.chip * 2 + (1 - self.core))

    def at_owner(self, step):
        return (self.column, (self.owner ^ step) * self.group + self.member)

    def at_member(self, step):
        return (self.column, self.owner * self.group + lax.rem(self.member + step, self.group))

    def index(self, column_step, chip_step, other=False):
        core = 1 - self.core if other else self.core
        return ((self.column ^ column_step) * self.chips + (self.chip ^ chip_step)) * 2 + core

    def neighbours(self):
        chips = [self.near(step) for step in range(1, self.chips)]
        columns = [self.beside(step) for step in range(1, self.columns)]
        return chips + columns + [self.twin()]


class Gather:
    def __init__(self, place, arrays, send, receive):
        self.place, self.arrays, self.send, self.receive = place, arrays, send, receive
        self.square = place.columns == 4
        self.sent = []

    def copies(self, kind, column_step, chip_step, device, own=False, where=None):
        slot = column_step * self.place.chips + chip_step
        for k, (shard, whole, block) in enumerate(self.arrays):
            held = block(whole, self.place.index(*(where or (column_step, chip_step))))
            yield remote(
                shard if own else held, held, self.send.at[k, kind, slot], self.receive.at[k, kind, slot], device
            )

    def begin(self, kind, column_step, chip_step, device, own=False, where=None):
        self.sent.append((kind, column_step, chip_step, own, where))
        for copy in self.copies(kind, column_step, chip_step, device, own, where):
            copy.start()

    def to_twin(self, column_step, chip_step, own=False):
        self.begin(1, column_step, chip_step, self.place.twin(), own=own)

    def outward(self, chip_step):
        place, own = self.place, chip_step == 0
        for step in range(1, place.columns):
            if not (self.square and step == 3):
                self.begin(0, step, chip_step, place.beside(step), own=own, where=(0, chip_step))
        self.to_twin(0, chip_step, own=own)

    def start(self):
        for step in range(1, self.place.chips):
            self.begin(0, 0, step, self.place.near(step), own=True, where=(0, 0))
        self.outward(0)

    def arrive(self, column_step, chip_step, other=False):
        for k, (_, whole, block) in enumerate(self.arrays):
            held = block(whole, self.place.index(column_step, chip_step, other))
            kind = 1 if other else 0
            slot = column_step * self.place.chips + chip_step
            remote(
                held, held, self.send.at[k, kind, slot], self.receive.at[k, kind, slot], self.place.twin()
            ).wait_recv()

    def from_chip(self, chip_step):
        self.arrive(0, chip_step)
        self.outward(chip_step)

    def from_columns(self, chip_step):
        for step in range(1, self.place.columns):
            if self.square and step == 3:
                continue
            self.arrive(step, chip_step)
            if self.square and step == 1 + chip_step % 2:
                self.begin(0, 3, chip_step, self.place.beside(3 - step), where=(step, chip_step))
            self.to_twin(step, chip_step)

    def from_corner(self, chip_step):
        if self.square:
            self.arrive(3, chip_step)
            self.to_twin(3, chip_step)

    def finish(self):
        place = self.place
        for column_step in range(place.columns):
            for chip_step in range(place.chips):
                self.arrive(column_step, chip_step, other=True)
        for kind, column_step, chip_step, own, where in self.sent:
            for copy in self.copies(kind, column_step, chip_step, place.twin(), own, where):
                copy.wait_send()


def gather_semaphores(grid, count):
    shape = (count, 2, grid.columns * grid.chips)
    return [pltpu.SemaphoreType.DMA(shape), pltpu.SemaphoreType.DMA(shape)]


def through(source, held, target, sem):
    copy = pltpu.make_async_copy(source, held, sem)
    copy.start()
    copy.wait()
    copy = pltpu.make_async_copy(held, target, sem)
    copy.start()
    copy.wait()


def start_exchange(grid, tokens, into, vectors):
    seqs, length, width = tokens.shape
    devices = grid.columns * grid.n
    parts, slim, _ = into.shape

    def kernel(
        tokens_ref, into_ref, vectors_ref, rows_ref, into_all, vectors_all, *scratch
    ):
        row_hold, into_hold, vector_hold, hold_sem, send, receive, row_send, row_receive = scratch
        place = Place(grid)
        meet(place.neighbours())
        gather = Gather(
            place,
            [
                (into_ref, into_all, lambda ref, i: ref.at[:, i]),
                (vectors_ref, vectors_all, lambda ref, i: ref.at[i]),
            ],
            send,
            receive,
        )
        gather.start()

        def row_copy(step):
            return remote(
                tokens_ref.at[place.owner ^ step],
                rows_ref.at[place.owner],
                row_send.at[step],
                row_receive.at[step],
                place.at_owner(step),
            )

        for step in range(1, seqs):
            row_copy(step).start()
        me = place.index(0, 0)
        through(into_ref, into_hold, into_all.at[:, me], hold_sem)
        through(vectors_ref, vector_hold, vectors_all.at[me], hold_sem)
        through(tokens_ref.at[place.owner], row_hold, rows_ref.at[place.owner], hold_sem)
        for step in range(1, place.chips):
            gather.from_chip(step)
            gather.from_columns(step - 1)
        gather.from_columns(place.chips - 1)
        for step in range(place.chips):
            gather.from_corner(step)
        gather.finish()
        for step in range(1, seqs):
            landed = rows_ref.at[place.owner ^ step]
            remote(
                landed, landed, row_send.at[step], row_receive.at[step], place.at_owner(step)
            ).wait_recv()
            row_copy(step).wait_send()

    shapes = [tokens.shape, (parts, devices, slim, width), (devices,) + vectors.shape]
    return pl.pallas_call(
        kernel,
        in_specs=[HBM] * 3,
        out_specs=[HBM] * 3,
        out_shape=[jax.ShapeDtypeStruct(shape, BF) for shape in shapes],
        scratch_shapes=[
            pltpu.VMEM(tokens.shape[1:], BF),
            pltpu.VMEM(into.shape, BF),
            pltpu.VMEM(vectors.shape, BF),
            pltpu.SemaphoreType.DMA(()),
        ]
        + gather_semaphores(grid, 2)
        + [pltpu.SemaphoreType.DMA((seqs,)), pltpu.SemaphoreType.DMA((seqs,))],
        compiler_params=pltpu.CompilerParams(collective_id=0, has_side_effects=True),
        name="start_exchange",
    )(tokens, into, vectors)


class Reduce:
    def __init__(self, place, arrays, buffers, semaphores):
        self.place, self.arrays = place, arrays
        self.halves, self.twins, self.sides, self.deeps = buffers
        self.load, self.twin_sems, self.side_sems, self.deep_sems = semaphores
        self.square = place.columns == 4
        self.every = range(len(arrays))
        self.sent = []

    def spot(self, column_step, chip_step):
        return (self.place.column ^ column_step) * self.place.chips + (self.place.chip ^ chip_step)

    def strip(self, column_step):
        return pl.ds((self.place.column ^ column_step) * self.place.chips, self.place.chips)

    def load_copy(self, k, step):
        whole = self.arrays[k][0].at[self.strip(step), self.place.core]
        return pltpu.make_async_copy(whole, self.halves[k].at[self.strip(step)], self.load.at[k, step])

    def twin_copy(self, k, step):
        place = self.place
        whole = self.arrays[k][0].at[self.strip(step), 1 - place.core]
        return remote(
            whole,
            self.twins[k].at[self.strip(step)],
            self.twin_sems[0].at[k, step],
            self.twin_sems[1].at[k, step],
            place.twin(),
        )

    def side_copy(self, k, column_step, chip_step, device):
        return remote(
            self.halves[k].at[self.spot(column_step, chip_step)],
            self.sides[k].at[column_step, chip_step],
            self.side_sems[0].at[k, column_step, chip_step],
            self.side_sems[1].at[k, column_step, chip_step],
            device,
        )

    def deep_copy(self, k, chip_step):
        return remote(
            self.halves[k].at[self.spot(0, chip_step)],
            self.deeps[k].at[chip_step],
            self.deep_sems[0].at[k, chip_step],
            self.deep_sems[1].at[k, chip_step],
            self.place.near(chip_step),
        )

    def start(self):
        order = range(self.place.columns - 1, -1, -1)
        for step in order:
            for k in self.every:
                self.twin_copy(k, step).start()
                self.load_copy(k, step).start()

    def fold(self, step):
        for k in self.every:
            self.load_copy(k, step).wait()
            self.twin_copy(k, step).wait_recv()
            half, twin = self.halves[k], self.twins[k]
            for chip_step in range(self.place.chips):
                spot = self.spot(step, chip_step)
                half[spot] = (half[spot].astype(F32) + twin[spot].astype(F32)).astype(BF)

    def corner(self, chip_step):
        self.sent.append((3, chip_step))
        for k in self.every:
            self.side_copy(k, 3, chip_step, self.place.beside(1 + chip_step % 2)).start()

    def side(self, column_step, chip_step):
        self.sent.append((column_step, chip_step))
        for k in self.every:
            self.side_copy(k, column_step, chip_step, self.place.beside(column_step)).start()

    def combine(self, chip_step):
        for k in self.every:
            self.side_copy(k, 3, chip_step, self.place.twin()).wait_recv()
            spot = self.spot(2 - chip_step % 2, chip_step)
            half = self.halves[k]
            half[spot] = (half[spot].astype(F32) + self.sides[k][3, chip_step].astype(F32)).astype(BF)

    def merge(self, chip_step):
        last = 3 if self.square else self.place.columns
        for k in self.every:
            spot = self.spot(0, chip_step)
            total = self.halves[k][spot].astype(F32)
            for step in range(1, last):
                self.side_copy(k, step, chip_step, self.place.twin()).wait_recv()
                total = total + self.sides[k][step, chip_step].astype(F32)
            self.halves[k][spot] = total.astype(BF)

    def deep(self, chip_step):
        for k in self.every:
            self.deep_copy(k, chip_step).start()

    def finish(self):
        place = self.place
        for k in self.every:
            total = self.halves[k][self.spot(0, 0)].astype(F32)
            for step in range(1, place.chips):
                self.deep_copy(k, step).wait_recv()
                total = total + self.deeps[k][step].astype(F32)
            self.arrays[k][1][...] = total
            for step in range(1, place.chips):
                self.deep_copy(k, step).wait_send()
            for step in range(place.columns):
                self.twin_copy(k, step).wait_send()
            for column_step, chip_step in self.sent:
                self.side_copy(k, column_step, chip_step, place.twin()).wait_send()

    def plan(self):
        chips, columns = self.place.chips, self.place.columns
        stages = [(0, self.start)]
        if not self.square:
            for step in range(columns):
                stages.append((1, lambda step=step: self.fold(step)))
            for step in range(1, columns):
                for chip_step in range(chips):
                    stages.append((3, lambda a=step, b=chip_step: self.side(a, b)))
            for chip_step in range(chips):
                stages.append((16, lambda b=chip_step: self.merge(b)))
            for chip_step in range(1, chips):
                stages.append((17, lambda b=chip_step: self.deep(b)))
            return stages
        odd = list(range(1, chips, 2))
        even = list(range(2, chips, 2))

        def many(moment, call, *steps):
            for step in steps:
                stages.append((moment, lambda step=step: call(*step)))

        many(1, self.fold, (3,))
        many(2, self.corner, *[(b,) for b in even + odd])
        many(2, self.fold, (1,), (2,))
        many(3, self.side, *[(1, b) for b in even], *[(2, b) for b in odd])
        many(4, self.fold, (0,))
        many(7, self.combine, *[(b,) for b in odd + even])
        many(8, self.side, *[(1, b) for b in odd], *[(2, b) for b in even])
        many(8, self.corner, (0,))
        many(8, self.side, (1, 0))
        for i, b in enumerate(odd):
            moment = 11 + (2 * i * 2) // max(len(odd), 1)
            many(moment, self.merge, (b,))
            many(moment + 1, self.deep, (b,))
        many(15, self.combine, (0,))
        many(15, self.merge, *[(b,) for b in even])
        many(16, self.side, (2, 0))
        many(16, self.deep, *[(b,) for b in even])
        many(20, self.merge, (0,))
        return stages


def reduce_scratch(grid, shapes):
    columns, chips, count = grid.columns, grid.chips, len(shapes)
    buffers = []
    for lead in ((columns * chips,), (columns * chips,), (columns, chips), (chips,)):
        buffers = buffers + [pltpu.VMEM(lead + tuple(shape), BF) for shape in shapes]
    dma = pltpu.SemaphoreType.DMA
    sems = [dma((count, columns))] * 3 + [dma((count, columns, chips))] * 2 + [dma((count, chips))] * 2
    return buffers + sems


def reduce_of(place, wholes, results, scratch):
    count = len(wholes)
    groups = [scratch[i * count : (i + 1) * count] for i in range(4)]
    sems = scratch[4 * count : 4 * count + 7]
    return Reduce(
        place, list(zip(wholes, results)), groups, (sems[0], sems[1:3], sems[3:5], sems[5:7])
    )


def by_place(grid, array_in, rows):
    return array_in.reshape(grid.columns * grid.chips, 2, rows, -1)


def row_exchange(place, source, target, send, receive):
    def copy(step):
        return remote(
            source.at[place.owner ^ step],
            target.at[place.owner],
            send.at[step],
            receive.at[step],
            place.at_owner(step),
        )

    def finish():
        for step in range(1, place.seqs):
            landed = target.at[place.owner ^ step]
            remote(landed, landed, send.at[step], receive.at[step], place.at_owner(step)).wait_recv()
            copy(step).wait_send()

    def start():
        for step in range(1, place.seqs):
            copy(step).start()

    return start, finish


def end_exchange(grid, rows, wholes):
    shapes = [whole.shape[2:] for whole in wholes]
    count = len(wholes)

    def kernel(rows_ref, *refs):
        whole_refs, back_ref, results = refs[:count], refs[count], refs[count + 1 : 2 * count + 1]
        row_hold, hold_sem, row_send, row_receive = refs[2 * count + 1 : 2 * count + 5]
        place = Place(grid)
        meet(place.neighbours())
        reduce = reduce_of(place, whole_refs, results, refs[2 * count + 5 :])
        start_rows, finish_rows = row_exchange(place, rows_ref, back_ref, row_send, row_receive)
        stages = reduce.plan()
        stages[0][1]()
        start_rows()
        through(rows_ref.at[place.owner], row_hold, back_ref.at[place.owner], hold_sem)
        for _, action in stages[1:]:
            action()
        reduce.finish()
        finish_rows()

    return pl.pallas_call(
        kernel,
        in_specs=[HBM] * (count + 1),
        out_specs=[HBM] + [pl.BlockSpec(memory_space=pltpu.VMEM)] * count,
        out_shape=[jax.ShapeDtypeStruct(rows.shape, BF)]
        + [jax.ShapeDtypeStruct(shape, F32) for shape in shapes],
        scratch_shapes=[
            pltpu.VMEM(rows.shape[1:], BF),
            pltpu.SemaphoreType.DMA(()),
            pltpu.SemaphoreType.DMA((grid.seqs,)),
            pltpu.SemaphoreType.DMA((grid.seqs,)),
        ]
        + reduce_scratch(grid, shapes),
        compiler_params=pltpu.CompilerParams(
            collective_id=3, has_side_effects=True, vmem_limit_bytes=40 << 20
        ),
        name="end_exchange",
    )(rows, *wholes)


LOG2E = 1.4426950408889634
SCALE = 0.125 * LOG2E


def dot_nt(left, right):
    return lax.dot_general(left, right, (((1,), (1,)), ((), ())), preferred_element_type=F32)


def own_lanes(half, count):
    lane = lax.broadcasted_iota(jnp.int32, (count, 2 * HD), 1)
    return (lane // HD) == half, lane == HD * (1 - half)


def attention(grid, inputs, key_bias, shards, block=256):
    rows = inputs.shape[0]
    width = inputs.shape[1] // 3
    pairs = width // (2 * HD)
    count = grid.group
    keys = rows * count
    blocks = rows // block
    steps = pairs * blocks
    devices = grid.columns * grid.n
    late = len(shards)

    def kernel(q_ref, bias_ref, k_ref, v_ref, all_ref, *refs):
        shard_refs = refs[:late]
        o_ref, l_ref = refs[late : late + 2]
        whole_refs = refs[late + 2 : 2 * late + 2]
        k_own, v_own, far, hold_sem, send, receive, far_send, far_receive = refs[2 * late + 2 : 2 * late + 10]
        holds = refs[2 * late + 10 :]
        pair, turn = pl.program_id(0), pl.program_id(1)
        now = pair * blocks + turn
        place = Place(grid)
        gather = Gather(
            place,
            [(s, w, lambda ref, i: ref.at[i]) for s, w in zip(shard_refs, whole_refs)],
            send,
            receive,
        )

        def far_copy(step, which, kind):
            first = pl.multiple_of(which * 2 * HD + (kind + 1) * width, 2 * HD)
            return remote(
                all_ref.at[:, pl.ds(first, 2 * HD)],
                far.at[step - 1, kind, which],
                far_send.at[step - 1, kind, which],
                far_receive.at[step - 1, kind, which],
                place.at_member(step),
            )

        def first_step():
            meet(place.neighbours() + [place.at_member(s) for s in range(1, count) if count > 2])
            for which in range(pairs):
                for step in range(1, count):
                    for kind in range(2):
                        far_copy(step, which, kind).start()
            gather.start()
            me = place.index(0, 0)
            for shard, whole, hold in zip(shard_refs, whole_refs, holds):
                through(shard, hold, whole.at[me], hold_sem)

        plan = [(0.0, first_step)]
        for step in range(1, place.chips):
            plan.append((step * 0.66 / (place.chips - 1), lambda step=step: gather.from_chip(step)))
            plan.append((0.1 + step * 0.66 / (place.chips - 1), lambda step=step: gather.from_columns(step - 1)))

        def last_step():
            gather.from_columns(place.chips - 1)
            for step in range(place.chips):
                gather.from_corner(step)
            gather.finish()
            for step in range(1, count):
                for which in range(pairs):
                    for kind in range(2):
                        far_copy(step, which, kind).wait_send()

        for moment, action in plan:
            pl.when(now == int(moment * steps))(action)

        @pl.when(turn == 0)
        def _():
            for step in range(1, count):
                for kind in range(2):
                    far_copy(step, pair, kind).wait_recv()
            for half in range(2):
                own, spare = own_lanes(half, rows)
                zero = jnp.zeros((rows, 2 * HD), BF)
                for i in range(count):
                    at = slice(i * rows, (i + 1) * rows)
                    key = k_ref[...] if i == 0 else far[i - 1, 0, pair]
                    value = v_ref[...] if i == 0 else far[i - 1, 1, pair]
                    k_own[half, at, :] = jnp.where(own, key, jnp.where(spare, bias_ref[at, :], zero))
                    v_own[half, at, :] = jnp.where(own, value, jnp.where(spare, zero + 1, zero))

        query = q_ref[...]
        results = []
        for half in range(2):
            own, spare = own_lanes(half, block)
            zero = jnp.zeros_like(query)
            query_h = jnp.where(own, query, jnp.where(spare, zero + 1, zero))
            scores = dot_nt(query_h, k_own[half])
            largest = jnp.max(scores, axis=1, keepdims=True)
            weights = jnp.exp2((scores - largest) * SCALE).astype(BF)
            summed = matmul(weights, v_own[half])
            totals = summed[:, HD * (1 - half) : HD * (1 - half) + 1]
            results.append(summed / totals)
            log_total = jnp.broadcast_to(largest * SCALE + jnp.log2(totals), (block, 2 * HD))
            l_ref[half : half + 1, :] = jnp.transpose(log_total)[0:1, :]
        lane = lax.broadcasted_iota(jnp.int32, (block, 2 * HD), 1)
        o_ref[...] = jnp.where(lane < HD, results[0], results[1]).astype(BF)
        pl.when(now == steps - 1)(last_step)

    def column(first):
        return pl.BlockSpec((rows, 2 * HD), lambda i, j: (0, i + first))

    far_sems = pltpu.SemaphoreType.DMA((max(count - 1, 1), 2, pairs))
    return pl.pallas_call(
        kernel,
        grid=(pairs, blocks),
        in_specs=[
            pl.BlockSpec((block, 2 * HD), lambda i, j: (j, i)),
            pl.BlockSpec((keys, 2 * HD), lambda i, j: (0, 0)),
            column(pairs),
            column(2 * pairs),
            HBM,
        ]
        + [HBM] * late,
        out_specs=[
            pl.BlockSpec((block, 2 * HD), lambda i, j: (j, i)),
            pl.BlockSpec((None, 8, block), lambda i, j: (i, 0, j)),
        ]
        + [HBM] * late,
        out_shape=[
            jax.ShapeDtypeStruct((rows, width), BF),
            jax.ShapeDtypeStruct((pairs, 8, rows), F32),
        ]
        + [jax.ShapeDtypeStruct((devices,) + shard.shape, BF) for shard in shards],
        scratch_shapes=[
            pltpu.VMEM((2, keys, 2 * HD), BF),
            pltpu.VMEM((2, keys, 2 * HD), BF),
            pltpu.VMEM((max(count - 1, 1), 2, pairs, rows, 2 * HD), BF),
            pltpu.SemaphoreType.DMA(()),
        ]
        + gather_semaphores(grid, late)
        + [far_sems, far_sems]
        + [pltpu.VMEM(shard.shape, BF) for shard in shards],
        compiler_params=pltpu.CompilerParams(
            collective_id=1, has_side_effects=True, vmem_limit_bytes=48 << 20
        ),
        cost_estimate=pl.CostEstimate(
            flops=16 * H * rows * keys * HD, bytes_accessed=8 * rows * width, transcendentals=H * rows * keys
        ),
        name="attention",
    )(inputs, key_bias, inputs, inputs, inputs, *shards)


def attention_back(grid, inputs, key_bias, log_totals, context, grad_context, wholes, rows_out, block=256, chunk=1024):
    rows = inputs.shape[0]
    width = inputs.shape[1] // 3
    pairs = width // (2 * HD)
    count = grid.group
    keys = rows * count
    blocks = rows // block
    steps = pairs * blocks
    chunk = min(chunk, rows)
    chunks = keys // chunk
    late = len(wholes)
    shapes = [whole.shape[2:] for whole in wholes]
    away = max(count - 1, 1)

    def kernel(q_ref, bias_ref, l_ref, o_ref, g_ref, k_ref, v_ref, all_ref, rows_ref, *refs):
        whole_refs = refs[:late]
        out_ref, back_ref = refs[late : late + 2]
        results = refs[late + 2 : 2 * late + 2]
        rest = refs[2 * late + 2 :]
        k_own, k_turned, v_all, grad_k, grad_v, far, far_out, far_in, row_hold, hold_sem = rest[:10]
        far_send, far_receive, out_send, in_receive, row_send, row_receive = rest[10:16]
        pair, turn = pl.program_id(0), pl.program_id(1)
        now = pair * blocks + turn
        place = Place(grid)
        reduce = reduce_of(place, whole_refs, results, rest[16:])
        start_rows, finish_rows = row_exchange(place, rows_ref, back_ref, row_send, row_receive)

        def far_copy(step, which, kind):
            first = pl.multiple_of(which * 2 * HD + (kind + 1) * width, 2 * HD)
            return remote(
                all_ref.at[:, pl.ds(first, 2 * HD)],
                far.at[step - 1, kind, which],
                far_send.at[step - 1, kind, which],
                far_receive.at[step - 1, kind, which],
                place.at_member(step),
            )

        def back_copy(step, which, kind):
            return remote(
                far_out.at[step - 1, kind, which],
                far_in.at[step - 1, kind, which],
                out_send.at[step - 1, kind, which],
                in_receive.at[step - 1, kind, which],
                place.at_member(count - step),
            )

        def take_back(which):
            for kind in range(2):
                first = pl.multiple_of(which * 2 * HD + (kind + 1) * width, 2 * HD)
                total = out_ref[:, pl.ds(first, 2 * HD)].astype(F32)
                for step in range(1, count):
                    back_copy(step, which, kind).wait_recv()
                    total = total + far_in[step - 1, kind, which].astype(F32)
                out_ref[:, pl.ds(first, 2 * HD)] = total.astype(BF)

        def send_back(which):
            for step in range(1, count):
                for kind in range(2):
                    back_copy(step, which, kind).start()

        def first_step():
            meet(place.neighbours() + [place.at_member(s) for s in range(1, count) if count > 2])
            for which in range(pairs):
                for step in range(1, count):
                    for kind in range(2):
                        far_copy(step, which, kind).start()

        actions = [(0, first_step)] + reduce.plan()
        actions.append((0, start_rows))
        actions.append(
            (1, lambda: through(rows_ref.at[place.owner], row_hold, back_ref.at[place.owner], hold_sem))
        )
        moments = {}
        for moment, action in actions:
            moments.setdefault(moment * steps // 24, []).append(action)
        for moment, group in sorted(moments.items()):

            @pl.when(now == moment)
            def _(group=group):
                for action in group:
                    action()

        @pl.when((turn == 0) & (pair > 0))
        def _():
            send_back(pair - 1)

        @pl.when(turn == 0)
        def _():
            for step in range(1, count):
                for kind in range(2):
                    far_copy(step, pair, kind).wait_recv()
            for i in range(count):
                at = slice(i * rows, (i + 1) * rows)
                v_all[at, :] = v_ref[...] if i == 0 else far[i - 1, 1, pair]
                key = k_ref[...] if i == 0 else far[i - 1, 0, pair]
                for half in range(2):
                    own, spare = own_lanes(half, rows)
                    zero = jnp.zeros_like(key)
                    k_own[half, at, :] = jnp.where(own, key, jnp.where(spare, bias_ref[at, :], zero))
                    k_turned[half, :, at] = jnp.transpose(jnp.where(own, key, zero))
            grad_k[...] = jnp.zeros_like(grad_k)
            grad_v[...] = jnp.zeros_like(grad_v)

        query, grad = q_ref[...], g_ref[...]
        turned = jnp.transpose(grad.astype(F32) * o_ref[...].astype(F32))
        asks, plain, grads, centres, logs = [], [], [], [], []
        for half in range(2):
            own, spare = own_lanes(half, block)
            zero = jnp.zeros_like(query)
            asks.append(jnp.where(own, query, jnp.where(spare, zero + 1, zero)))
            plain.append(jnp.where(own, query, zero))
            grads.append(jnp.where(own, grad, zero))
            centres.append(jnp.sum(turned[HD * half : HD * half + HD], axis=0, keepdims=True))
            logs.append(l_ref[half : half + 1, :])
        grad_q = None
        for c in range(chunks):
            span = slice(c * chunk, (c + 1) * chunk)
            weights, slopes = [], []
            for half in range(2):
                scores = dot_nt(k_own[half, span, :], asks[half])
                grad_weights = dot_nt(v_all[span, :], grads[half])
                exact = jnp.exp2(scores * SCALE - logs[half])
                slope = (exact * (grad_weights - centres[half])).astype(BF)
                weights.append(exact.astype(BF))
                slopes.append(slope)
                step = matmul(k_turned[half, :, span], slope)
                grad_q = step if grad_q is None else grad_q + step
            grad_v[span, :] += matmul(weights[0], grads[0]) + matmul(weights[1], grads[1])
            grad_k[span, :] += matmul(slopes[0], plain[0]) + matmul(slopes[1], plain[1])
        at = pl.ds(pl.multiple_of(turn * block, block), block)
        out_ref[at, pl.ds(pl.multiple_of(pair * 2 * HD, 2 * HD), 2 * HD)] = (
            jnp.transpose(grad_q) * 0.125
        ).astype(BF)

        @pl.when(turn == blocks - 1)
        def _():
            for i in range(count):
                at = slice(i * rows, (i + 1) * rows)
                for kind, value, scale in ((0, grad_k, 0.125), (1, grad_v, 1.0)):
                    low = (value[at, :] * scale).astype(BF)
                    if i == 0:
                        first = pl.multiple_of(pair * 2 * HD + (kind + 1) * width, 2 * HD)
                        out_ref[:, pl.ds(first, 2 * HD)] = low
                    else:
                        far_out[i - 1, kind, pair] = low

        @pl.when((turn == blocks - 1) & (pair > 0))
        def _():
            take_back(pair - 1)

        @pl.when(now == steps - 1)
        def _():
            reduce.finish()
            send_back(pairs - 1)
            finish_rows()
            take_back(pairs - 1)
            for step in range(1, count):
                for which in range(pairs):
                    for kind in range(2):
                        far_copy(step, which, kind).wait_send()
                        back_copy(step, which, kind).wait_send()

    def column(first):
        return pl.BlockSpec((rows, 2 * HD), lambda i, j: (0, i + first))

    def tile():
        return pl.BlockSpec((block, 2 * HD), lambda i, j: (j, i))

    def resident(shape):
        return pl.BlockSpec(shape, lambda i, j: (0,) * len(shape))

    far_sems = pltpu.SemaphoreType.DMA((away, 2, pairs))
    far_buffer = pltpu.VMEM((away, 2, pairs, rows, 2 * HD), BF)
    return pl.pallas_call(
        kernel,
        grid=(pairs, blocks),
        in_specs=[
            tile(),
            resident((keys, 2 * HD)),
            pl.BlockSpec((None, 8, block), lambda i, j: (i, 0, j)),
            tile(),
            tile(),
            column(pairs),
            column(2 * pairs),
            HBM,
            HBM,
        ]
        + [HBM] * late,
        out_specs=[resident(inputs.shape), HBM] + [resident(tuple(shape)) for shape in shapes],
        out_shape=[jax.ShapeDtypeStruct(inputs.shape, BF), jax.ShapeDtypeStruct(rows_out.shape, BF)]
        + [jax.ShapeDtypeStruct(shape, F32) for shape in shapes],
        scratch_shapes=[
            pltpu.VMEM((2, keys, 2 * HD), BF),
            pltpu.VMEM((2, 2 * HD, keys), BF),
            pltpu.VMEM((keys, 2 * HD), BF),
            pltpu.VMEM((keys, 2 * HD), F32),
            pltpu.VMEM((keys, 2 * HD), F32),
            far_buffer,
            far_buffer,
            far_buffer,
            pltpu.VMEM(rows_out.shape[1:], BF),
            pltpu.SemaphoreType.DMA(()),
        ]
        + [far_sems] * 4
        + [pltpu.SemaphoreType.DMA((grid.seqs,))] * 2
        + reduce_scratch(grid, shapes),
        compiler_params=pltpu.CompilerParams(
            collective_id=2, has_side_effects=True, vmem_limit_bytes=61 << 20
        ),
        cost_estimate=pl.CostEstimate(
            flops=40 * H * rows * keys * HD, bytes_accessed=12 * rows * width, transcendentals=H * rows * keys
        ),
        name="attention_back",
    )(inputs, key_bias, log_totals, context, grad_context, inputs, inputs, inputs, rows_out, *wholes)


def body(
    tokens,
    lengths,
    query_weight,
    key_weight,
    value_weight,
    out_weight,
    up_weight,
    down_weight,
    query_bias,
    value_bias,
    out_bias,
    up_bias,
    down_bias,
    first_gain,
    first_shift,
    second_gain,
    second_shift,
    cotangent,
):
    seqs, length, width = tokens.shape
    grid = Grid(seqs)
    devices = grid.columns * grid.n
    slim = query_weight.shape[0]
    hidden = up_weight.shape[1]
    tall = hidden // devices
    wide = hidden // width

    vectors = (
        query_bias,
        value_bias,
        out_bias,
        down_bias,
        first_gain,
        first_shift,
        second_gain,
        second_shift,
    )
    vector_row = jnp.concatenate(vectors + (up_bias,))
    vector_size = vector_row.shape[0]
    vector_rows = jnp.zeros((8, -(-vector_size // 128) * 128), BF).at[0, :vector_size].set(vector_row)
    into_shard = jnp.stack([query_weight, key_weight, value_weight])
    flat_in, into_full, vector_full = start_exchange(grid, tokens, into_shard, vector_rows)
    flat_in = flat_in.reshape(-1, width)
    into_full = into_full.reshape(3, width, width)
    vector_table = vector_full[:, 0, :vector_size]
    small = vector_table[:, : 8 * slim].reshape(devices, 8, slim).transpose(1, 0, 2)
    small = small.reshape(8, width).astype(F32)
    query_add, value_add, out_add, down_add, gain_one, shift_one, gain_two, shift_two = (
        small[i] for i in range(8)
    )
    up_add = vector_table[:, 8 * slim :].reshape(hidden).astype(F32)

    positions = row_positions(grid, length)
    my_length = take_block(lengths, grid.owner)
    live_rows = (positions(grid.member) < my_length).astype(F32)[:, None]
    key_bias = jnp.concatenate(
        [
            jnp.where(positions((grid.member - step) % grid.group) < my_length, 0.0, -1e30)
            for step in range(grid.group)
        ]
    ).astype(F32)

    key_bias = jnp.broadcast_to(key_bias[:, None], (key_bias.shape[0], 2 * HD)).astype(BF)
    adds = (query_add, jnp.zeros_like(query_add), value_add)
    inputs = [(matmul(flat_in, into_full[i]) + adds[i]).astype(BF) for i in range(3)]
    inputs = jnp.concatenate(inputs, axis=1)
    context, log_totals, out_full, up_full, down_full = attention(
        grid, inputs, key_bias, (out_weight, up_weight, down_weight)
    )
    out_full = out_full.reshape(width, width)
    up_full = up_full.reshape(width, hidden)
    down_full = down_full.reshape(hidden, width)
    cotangent = lax.optimization_barrier((cotangent, context))[0]
    grad_in = to_sequences(grid, cotangent)

    first_sum = flat_in.astype(F32) + matmul(context, out_full) + out_add
    first_norm, first_unit, first_factor = normalize(first_sum, gain_one, shift_one)
    first_low = first_norm.astype(BF)
    up_pre = matmul(first_low, up_full) + up_add
    activated = jax.nn.gelu(up_pre, approximate=False).astype(BF)
    second_sum = first_low.astype(F32) + matmul(activated, down_full) + down_add
    second_norm, second_unit, second_factor = normalize(second_sum, gain_two, shift_two)
    output = (second_norm * live_rows).astype(BF).reshape(seqs, length, width)

    grad_output = grad_in.astype(F32) * live_rows
    grad_gain_two = jnp.sum(grad_output * second_unit, axis=0)
    grad_shift_two = jnp.sum(grad_output, axis=0)
    grad_second = norm_back(grad_output, second_unit, second_factor, gain_two)
    grad_branch = grad_second.astype(BF)
    grad_down_add = jnp.sum(grad_branch.astype(F32), axis=0)
    grad_down = left_product(activated, grad_branch).astype(BF)
    grad_up_low = (right_product(grad_branch, down_full) * gelu_slope(up_pre)).astype(BF)
    grad_up_add = jnp.sum(grad_up_low.astype(F32), axis=0)
    grad_up = left_product(first_low, grad_up_low).astype(BF)
    grad_first = right_product(grad_up_low, up_full) + grad_second
    grad_gain_one = jnp.sum(grad_first * first_unit, axis=0)
    grad_shift_one = jnp.sum(grad_first, axis=0)
    grad_residual = norm_back(grad_first, first_unit, first_factor, gain_one)
    grad_attend = grad_residual.astype(BF)
    grad_out_add = jnp.sum(grad_attend.astype(F32), axis=0)
    grad_out = left_product(context, grad_attend).astype(BF)
    grad_context = right_product(grad_attend, out_full).astype(BF)

    def pack(grads, more=()):
        count = len(grads)
        table = jnp.stack(grads).reshape(count, devices, slim).transpose(1, 0, 2)
        table = jnp.concatenate([table.reshape(devices, count * slim), *more], axis=1).astype(BF)
        size = table.shape[1]
        table = jnp.pad(table, ((0, 0), (0, -size % 128)))
        return jnp.broadcast_to(table[:, None, :], (devices, 8, table.shape[1])).reshape(devices * 8, -1)

    middle = pack(
        [grad_out_add, grad_down_add, grad_gain_one, grad_shift_one, grad_gain_two, grad_shift_two],
        (grad_up_add.reshape(devices, tall),),
    )
    wholes = [
        by_place(grid, grad_up, slim),
        by_place(grid, grad_down, tall),
        by_place(grid, grad_out, slim),
        by_place(grid, middle, 8),
    ]
    low, output, grad_up_own, grad_down_own, grad_out_own, middle_own = attention_back(
        grid, inputs, key_bias, log_totals, context, grad_context, wholes, output
    )
    query_adds = jnp.sum(low[:, :width].astype(F32), axis=0)
    value_adds = jnp.sum(low[:, 2 * width :].astype(F32), axis=0)
    tokens_grad = grad_residual
    for i in range(3):
        tokens_grad = tokens_grad + right_product(low[:, i * width : (i + 1) * width], into_full[i])
    wholes = [
        by_place(grid, left_product(flat_in, low).astype(BF), slim),
        by_place(grid, pack([query_adds, value_adds]), 8),
    ]
    tokens_grad = tokens_grad.astype(BF).reshape(seqs, length, width)
    tokens_grad, grad_into_own, last_own = end_exchange(grid, tokens_grad, wholes)
    tokens_grad = tokens_grad.astype(F32)
    middle_own, last_own = middle_own[0], last_own[0]
    vector_outs = [last_own[:slim], last_own[slim : 2 * slim]]
    vector_outs = vector_outs + [middle_own[i * slim : (i + 1) * slim] for i in range(6)]
    up_add_own = middle_own[6 * slim : 6 * slim + tall]
    matrix_outs = [grad_into_own[:, i * width : (i + 1) * width] for i in range(3)]
    return (
        output,
        tokens_grad,
        matrix_outs[0],
        matrix_outs[1],
        matrix_outs[2],
        grad_out_own,
        grad_up_own,
        grad_down_own,
        vector_outs[0],
        vector_outs[1],
        vector_outs[2],
        up_add_own,
        vector_outs[3],
        vector_outs[4],
        vector_outs[5],
        vector_outs[6],
        vector_outs[7],
    )


def solution(mesh):
    whole = ("dp", "seq")
    matrix, vector, rows = P(whole, None), P(whole), P("dp", "seq", None)
    return jax.shard_map(
        body,
        mesh=mesh,
        in_specs=(rows, P("dp")) + (matrix,) * 6 + (vector,) * 9 + (rows,),
        out_specs=(rows, rows) + (matrix,) * 6 + (vector,) * 9,
        check_vma=False,
    )
```

```python
import jax
import jax.numpy as jnp
from jax import lax
from jax.experimental import pallas as pl
from jax.experimental.pallas import tpu as pltpu
from jax.sharding import PartitionSpec as P

H = 12
HD = 64

EPSILON = 1e-05
ROOT_HALF = 0.7071067811865476
INV_ROOT_TWO_PI = 0.3989422804014327
BF = jnp.bfloat16
F32 = jnp.float32


def matmul(left, right):
    return jnp.dot(left, right, preferred_element_type=F32)


def left_product(left, right):
    return lax.dot_general(left, right, (((0,), (0,)), ((), ())), preferred_element_type=F32)


def right_product(left, right):
    return lax.dot_general(left, right, (((1,), (1,)), ((), ())), preferred_element_type=F32)


def normalize(inputs, gains, shifts):
    centre = inputs - jnp.mean(inputs, axis=-1, keepdims=True)
    factor = lax.rsqrt(jnp.mean(centre * centre, axis=-1, keepdims=True) + EPSILON)
    unit_rows = centre * factor
    return (unit_rows * gains + shifts, unit_rows, factor)


def norm_back(grad_in, unit_rows, factor, gains):
    grad_unit = grad_in * gains
    return factor * (
        grad_unit
        - jnp.mean(grad_unit, axis=-1, keepdims=True)
        - unit_rows * jnp.mean(grad_unit * unit_rows, axis=-1, keepdims=True)
    )


def swap_index(place, step, count):
    if count & (count - 1) == 0:
        return place ^ step
    return (place + step) % count


def source_index(place, step, count):
    if count & (count - 1) == 0:
        return place ^ step
    return (place - step) % count


class Grid:
    def __init__(self, seqs):
        self.columns = lax.axis_size("dp")
        self.n = lax.axis_size("seq")
        self.seqs = seqs
        self.group = self.n // seqs
        self.chips = self.n // 2
        self.column = lax.axis_index("dp")
        place = lax.axis_index("seq")
        self.chip = place // 2
        self.core = place % 2
        self.owner = place // self.group
        self.member = place % self.group

    def to_chip(self, array_in, step):
        pairs = [(s, swap_index(s // 2, step, self.chips) * 2 + s % 2) for s in range(self.n)]
        return lax.ppermute(array_in, "seq", pairs)

    def to_column(self, array_in, step):
        pairs = [(s, swap_index(s, step, self.columns)) for s in range(self.columns)]
        return lax.ppermute(array_in, "dp", pairs)

    def to_core(self, array_in):
        return lax.ppermute(array_in, "seq", [(s, s ^ 1) for s in range(self.n)])

    def to_owner(self, array_in, step, back=False):
        move = source_index if back else swap_index
        pairs = [
            (s, move(s // self.group, step, self.seqs) * self.group + s % self.group)
            for s in range(self.n)
        ]
        return lax.ppermute(array_in, "seq", pairs)

    def to_member(self, array_in, step, back=False):
        shift = -step if back else step
        pairs = [
            (s, (s // self.group) * self.group + (s % self.group + shift) % self.group)
            for s in range(self.n)
        ]
        return lax.ppermute(array_in, "seq", pairs)


def take_block(array_in, index):
    return lax.dynamic_index_in_dim(array_in, index, 0, keepdims=False)


def to_sequences(grid, array_in):
    out = jnp.zeros_like(array_in)
    out = lax.dynamic_update_index_in_dim(out, take_block(array_in, grid.owner), grid.owner, 0)
    for step in range(1, grid.seqs):
        place = swap_index(grid.owner, step, grid.seqs)
        got = grid.to_owner(take_block(array_in, place), step)
        out = lax.dynamic_update_index_in_dim(out, got, place, 0)
    return out.reshape(-1, array_in.shape[2])


def from_sequences(grid, rows, length):
    return to_sequences(grid, rows.reshape(grid.seqs, length, rows.shape[1])).reshape(grid.seqs, length, -1)


MESH = pl.DeviceIdType.MESH
HBM = pl.BlockSpec(memory_space=pl.ANY)


def remote(source, target, send, receive, device):
    return pltpu.make_async_remote_copy(
        src_ref=source, dst_ref=target, send_sem=send, recv_sem=receive, device_id=device, device_id_type=MESH
    )


def meet(devices):
    barrier = pltpu.get_barrier_semaphore()
    for device in devices:
        pl.semaphore_signal(barrier, inc=1, device_id=device, device_id_type=MESH)
    pl.semaphore_wait(barrier, len(devices))


class Place:
    def __init__(self, grid):
        self.columns, self.chips, self.n = grid.columns, grid.chips, grid.n
        self.seqs, self.group = grid.seqs, grid.group
        self.column = lax.axis_index("dp")
        self.spot = lax.axis_index("seq")
        self.chip = lax.div(self.spot, 2)
        self.core = lax.rem(self.spot, 2)
        self.owner = lax.div(self.spot, self.group)
        self.member = lax.rem(self.spot, self.group)

    def near(self, chip_step):
        return (self.column, (self.chip ^ chip_step) * 2 + self.core)

    def beside(self, column_step):
        return (self.column ^ column_step, self.spot)

    def twin(self):
        return (self.column, self.chip * 2 + (1 - self.core))

    def at_owner(self, step):
        return (self.column, (self.owner ^ step) * self.group + self.member)

    def at_member(self, step):
        return (self.column, self.owner * self.group + lax.rem(self.member + step, self.group))

    def index(self, column_step, chip_step, other=False):
        core = 1 - self.core if other else self.core
        return ((self.column ^ column_step) * self.chips + (self.chip ^ chip_step)) * 2 + core

    def neighbours(self):
        chips = [self.near(step) for step in range(1, self.chips)]
        columns = [self.beside(step) for step in range(1, self.columns)]
        return chips + columns + [self.twin()]


class Gather:
    def __init__(self, place, arrays, send, receive):
        self.place, self.arrays, self.send, self.receive = place, arrays, send, receive
        self.square = place.columns == 4
        self.sent = []

    def copies(self, kind, column_step, chip_step, device, own=False, where=None):
        slot = column_step * self.place.chips + chip_step
        for k, (shard, whole, block) in enumerate(self.arrays):
            held = block(whole, self.place.index(*(where or (column_step, chip_step))))
            yield remote(
                shard if own else held, held, self.send.at[k, kind, slot], self.receive.at[k, kind, slot], device
            )

    def begin(self, kind, column_step, chip_step, device, own=False, where=None):
        self.sent.append((kind, column_step, chip_step, own, where))
        for copy in self.copies(kind, column_step, chip_step, device, own, where):
            copy.start()

    def to_twin(self, column_step, chip_step, own=False):
        self.begin(1, column_step, chip_step, self.place.twin(), own=own)

    def outward(self, chip_step):
        place, own = self.place, chip_step == 0
        for step in range(1, place.columns):
            if not (self.square and step == 3):
                self.begin(0, step, chip_step, place.beside(step), own=own, where=(0, chip_step))
        self.to_twin(0, chip_step, own=own)

    def start(self):
        for step in range(1, self.place.chips):
            self.begin(0, 0, step, self.place.near(step), own=True, where=(0, 0))
        self.outward(0)

    def arrive(self, column_step, chip_step, other=False):
        for k, (_, whole, block) in enumerate(self.arrays):
            held = block(whole, self.place.index(column_step, chip_step, other))
            kind = 1 if other else 0
            slot = column_step * self.place.chips + chip_step
            remote(
                held, held, self.send.at[k, kind, slot], self.receive.at[k, kind, slot], self.place.twin()
            ).wait_recv()

    def from_chip(self, chip_step):
        self.arrive(0, chip_step)
        self.outward(chip_step)

    def from_columns(self, chip_step):
        for step in range(1, self.place.columns):
            if self.square and step == 3:
                continue
            self.arrive(step, chip_step)
            if self.square and step == 1 + chip_step % 2:
                self.begin(0, 3, chip_step, self.place.beside(3 - step), where=(step, chip_step))
            self.to_twin(step, chip_step)

    def from_corner(self, chip_step):
        if self.square:
            self.arrive(3, chip_step)
            self.to_twin(3, chip_step)

    def finish(self):
        place = self.place
        for column_step in range(place.columns):
            for chip_step in range(place.chips):
                self.arrive(column_step, chip_step, other=True)
        for kind, column_step, chip_step, own, where in self.sent:
            for copy in self.copies(kind, column_step, chip_step, place.twin(), own, where):
                copy.wait_send()


def gather_semaphores(grid, count):
    shape = (count, 2, grid.columns * grid.chips)
    return [pltpu.SemaphoreType.DMA(shape), pltpu.SemaphoreType.DMA(shape)]


def through(source, held, target, sem):
    copy = pltpu.make_async_copy(source, held, sem)
    copy.start()
    copy.wait()
    copy = pltpu.make_async_copy(held, target, sem)
    copy.start()
    copy.wait()


def start_exchange(grid, tokens, into, vectors, lengths, vector_widths):
    seqs, length, width = tokens.shape
    devices = grid.columns * grid.n
    slim = into[0].shape[0]
    parts = len(into)
    rows = seqs * length
    tile = vectors.shape

    def spread(table, size):
        lane = lax.broadcasted_iota(jnp.int32, (128, devices * size), 1).astype(F32)
        row = lax.broadcasted_iota(jnp.int32, (128, devices * size), 0).astype(F32)
        within = lane - size * jnp.floor((lane + 0.5) * (1.0 / size))
        return matmul(table, (row == within).astype(BF))

    def own_block(count, size):
        lane = lax.broadcasted_iota(jnp.int32, (count, devices * size), 1).astype(F32)
        return jnp.floor((lane + 0.5) * (1.0 / size))

    def kernel(tokens_ref, query_ref, key_ref, value_ref, vectors_ref, lengths_ref, rows_ref, into_all, vectors_all, *rest):
        into_refs = (query_ref, key_ref, value_ref)
        bias_ref, live_ref = rest[:2]
        vector_refs = rest[2 : 2 + len(vector_widths)]
        scratch = rest[2 + len(vector_widths) :]
        row_hold, into_hold, vector_hold, table_hold, hold_sem, send, receive, row_send, row_receive = scratch
        place = Place(grid)
        meet(place.neighbours())

        def part(k):
            return lambda ref, i: ref.at[i, :, pl.ds(k * width, width)]

        gather = Gather(
            place,
            [(into_refs[k], into_all, part(k)) for k in range(parts)]
            + [(vectors_ref, vectors_all, lambda ref, i: ref.at[i])],
            send,
            receive,
        )
        gather.start()

        def row_copy(step):
            return remote(
                tokens_ref.at[place.owner ^ step],
                rows_ref.at[place.owner],
                row_send.at[step],
                row_receive.at[step],
                place.at_owner(step),
            )

        for step in range(1, seqs):
            row_copy(step).start()
        me = place.index(0, 0)
        for k in range(parts):
            through(into_refs[k], into_hold, part(k)(into_all, me), hold_sem)
        through(vectors_ref, vector_hold, vectors_all.at[me], hold_sem)
        through(tokens_ref.at[place.owner], row_hold, rows_ref.at[place.owner], hold_sem)

        my_length = lengths_ref[place.owner]
        for step in range(place.group):
            member = lax.rem(place.member - step + place.group, place.group)
            for source in range(seqs):
                first = (source * place.group + member) * length
                at = slice(step * rows + source * length, step * rows + (source + 1) * length)
                here = lax.broadcasted_iota(jnp.int32, (length, 2 * HD), 0) + first
                bias_ref[at, :] = jnp.where(here < my_length, 0.0, -1e30).astype(BF)
                if step == 0:
                    here = lax.broadcasted_iota(jnp.int32, (length, 1), 0) + first
                    live_ref[at, :] = jnp.where(here < my_length, 1.0, 0.0).astype(F32)

        for step in range(1, place.chips):
            gather.from_chip(step)
            gather.from_columns(step - 1)
        gather.from_columns(place.chips - 1)
        for step in range(place.chips):
            gather.from_corner(step)
        gather.finish()
        copy = pltpu.make_async_copy(vectors_all, table_hold, hold_sem)
        copy.start()
        copy.wait()
        table = table_hold[...].astype(F32)
        kind = lax.broadcasted_iota(jnp.int32, table.shape, 1)
        source = lax.broadcasted_iota(jnp.int32, (devices, 1), 0).astype(F32)
        for k, size in enumerate(vector_widths):
            own = jnp.sum(jnp.where(kind == k, table, 0.0), axis=1).astype(BF)
            apart = jnp.where(own_block(devices, size) == source, spread(own, size), 0.0)
            vector_refs[k][...] = jnp.sum(apart, axis=0, keepdims=True)
        for step in range(1, seqs):
            landed = rows_ref.at[place.owner ^ step]
            remote(
                landed, landed, row_send.at[step], row_receive.at[step], place.at_owner(step)
            ).wait_recv()
            row_copy(step).wait_send()

    vmem = pl.BlockSpec(memory_space=pltpu.VMEM)
    shapes = [tokens.shape, (devices, slim, parts * width), (devices,) + tile]
    return pl.pallas_call(
        kernel,
        in_specs=[HBM] * (parts + 2) + [pl.BlockSpec(memory_space=pltpu.SMEM)],
        out_specs=[HBM] * 3 + [vmem] * (2 + len(vector_widths)),
        out_shape=[jax.ShapeDtypeStruct(shape, BF) for shape in shapes]
        + [jax.ShapeDtypeStruct((grid.group * rows, 2 * HD), BF), jax.ShapeDtypeStruct((rows, 1), F32)]
        + [jax.ShapeDtypeStruct((1, devices * size), F32) for size in vector_widths],
        scratch_shapes=[
            pltpu.VMEM(tokens.shape[1:], BF),
            pltpu.VMEM(into[0].shape, BF),
            pltpu.VMEM(tile, BF),
            pltpu.VMEM((devices,) + tile, BF),
            pltpu.SemaphoreType.DMA(()),
        ]
        + gather_semaphores(grid, parts + 1)
        + [pltpu.SemaphoreType.DMA((seqs,)), pltpu.SemaphoreType.DMA((seqs,))],
        compiler_params=pltpu.CompilerParams(collective_id=0, has_side_effects=True),
        name="start_exchange",
    )(tokens, *into, vectors, lengths)


class Reduce:
    def __init__(self, place, arrays, buffers, semaphores):
        self.place, self.arrays = place, arrays
        self.halves, self.twins, self.sides, self.deeps = buffers
        self.load, self.twin_sems, self.side_sems, self.deep_sems = semaphores
        self.square = place.columns == 4
        self.every = range(len(arrays))
        self.sent = []

    def spot(self, column_step, chip_step):
        return (self.place.column ^ column_step) * self.place.chips + (self.place.chip ^ chip_step)

    def strip(self, column_step):
        return pl.ds((self.place.column ^ column_step) * self.place.chips, self.place.chips)

    def load_copy(self, k, step):
        whole = self.arrays[k][0].at[self.strip(step), self.place.core]
        return pltpu.make_async_copy(whole, self.halves[k].at[self.strip(step)], self.load.at[k, step])

    def twin_copy(self, k, step):
        place = self.place
        whole = self.arrays[k][0].at[self.strip(step), 1 - place.core]
        return remote(
            whole,
            self.twins[k].at[self.strip(step)],
            self.twin_sems[0].at[k, step],
            self.twin_sems[1].at[k, step],
            place.twin(),
        )

    def side_copy(self, k, column_step, chip_step, device):
        return remote(
            self.halves[k].at[self.spot(column_step, chip_step)],
            self.sides[k].at[column_step, chip_step],
            self.side_sems[0].at[k, column_step, chip_step],
            self.side_sems[1].at[k, column_step, chip_step],
            device,
        )

    def deep_copy(self, k, chip_step):
        return remote(
            self.halves[k].at[self.spot(0, chip_step)],
            self.deeps[k].at[chip_step],
            self.deep_sems[0].at[k, chip_step],
            self.deep_sems[1].at[k, chip_step],
            self.place.near(chip_step),
        )

    def start(self):
        order = range(self.place.columns - 1, -1, -1)
        for step in order:
            for k in self.every:
                self.twin_copy(k, step).start()
                self.load_copy(k, step).start()

    def fold(self, step):
        for k in self.every:
            self.load_copy(k, step).wait()
            self.twin_copy(k, step).wait_recv()
            half, twin = self.halves[k], self.twins[k]
            for chip_step in range(self.place.chips):
                spot = self.spot(step, chip_step)
                half[spot] = (half[spot].astype(F32) + twin[spot].astype(F32)).astype(BF)

    def corner(self, chip_step):
        self.sent.append((3, chip_step))
        for k in self.every:
            self.side_copy(k, 3, chip_step, self.place.beside(1 + chip_step % 2)).start()

    def side(self, column_step, chip_step):
        self.sent.append((column_step, chip_step))
        for k in self.every:
            self.side_copy(k, column_step, chip_step, self.place.beside(column_step)).start()

    def combine(self, chip_step):
        for k in self.every:
            self.side_copy(k, 3, chip_step, self.place.twin()).wait_recv()
            spot = self.spot(2 - chip_step % 2, chip_step)
            half = self.halves[k]
            half[spot] = (half[spot].astype(F32) + self.sides[k][3, chip_step].astype(F32)).astype(BF)

    def merge(self, chip_step):
        last = 3 if self.square else self.place.columns
        for k in self.every:
            spot = self.spot(0, chip_step)
            total = self.halves[k][spot].astype(F32)
            for step in range(1, last):
                self.side_copy(k, step, chip_step, self.place.twin()).wait_recv()
                total = total + self.sides[k][step, chip_step].astype(F32)
            self.halves[k][spot] = total.astype(BF)

    def deep(self, chip_step):
        for k in self.every:
            self.deep_copy(k, chip_step).start()

    def finish(self):
        place = self.place
        for k in self.every:
            total = self.halves[k][self.spot(0, 0)].astype(F32)
            for step in range(1, place.chips):
                self.deep_copy(k, step).wait_recv()
                total = total + self.deeps[k][step].astype(F32)
            self.arrays[k][1][...] = total
            for step in range(1, place.chips):
                self.deep_copy(k, step).wait_send()
            for step in range(place.columns):
                self.twin_copy(k, step).wait_send()
            for column_step, chip_step in self.sent:
                self.side_copy(k, column_step, chip_step, place.twin()).wait_send()

    def plan(self):
        chips, columns = self.place.chips, self.place.columns
        stages = [(0, self.start)]
        if not self.square:
            for step in range(columns):
                stages.append((1, lambda step=step: self.fold(step)))
            for step in range(1, columns):
                for chip_step in range(chips):
                    stages.append((3, lambda a=step, b=chip_step: self.side(a, b)))
            for chip_step in range(chips):
                stages.append((16, lambda b=chip_step: self.merge(b)))
            for chip_step in range(1, chips):
                stages.append((17, lambda b=chip_step: self.deep(b)))
            return stages
        odd = list(range(1, chips, 2))
        even = list(range(2, chips, 2))

        def many(moment, call, *steps):
            for step in steps:
                stages.append((moment, lambda step=step: call(*step)))

        many(1, self.fold, (3,))
        many(2, self.corner, *[(b,) for b in even + odd])
        many(2, self.fold, (1,), (2,))
        many(3, self.side, *[(1, b) for b in even], *[(2, b) for b in odd])
        many(4, self.fold, (0,))
        many(7, self.combine, *[(b,) for b in odd + even])
        many(8, self.side, *[(1, b) for b in odd], *[(2, b) for b in even])
        many(8, self.corner, (0,))
        many(8, self.side, (1, 0))
        for i, b in enumerate(odd):
            moment = 11 + (2 * i * 2) // max(len(odd), 1)
            many(moment, self.merge, (b,))
            many(moment + 1, self.deep, (b,))
        many(15, self.combine, (0,))
        many(15, self.merge, *[(b,) for b in even])
        many(16, self.side, (2, 0))
        many(16, self.deep, *[(b,) for b in even])
        many(20, self.merge, (0,))
        return stages


def reduce_scratch(grid, shapes):
    columns, chips, count = grid.columns, grid.chips, len(shapes)
    buffers = []
    for lead in ((columns * chips,), (columns * chips,), (columns, chips), (chips,)):
        buffers = buffers + [pltpu.VMEM(lead + tuple(shape), BF) for shape in shapes]
    dma = pltpu.SemaphoreType.DMA
    sems = [dma((count, columns))] * 3 + [dma((count, columns, chips))] * 2 + [dma((count, chips))] * 2
    return buffers + sems


def reduce_of(place, wholes, results, scratch):
    count = len(wholes)
    groups = [scratch[i * count : (i + 1) * count] for i in range(4)]
    sems = scratch[4 * count : 4 * count + 7]
    return Reduce(
        place, list(zip(wholes, results)), groups, (sems[0], sems[1:3], sems[3:5], sems[5:7])
    )


def by_place(grid, array_in, rows):
    return array_in.reshape(grid.columns * grid.chips, 2, rows, -1)


def row_exchange(place, source, target, send, receive):
    def copy(step):
        return remote(
            source.at[place.owner ^ step],
            target.at[place.owner],
            send.at[step],
            receive.at[step],
            place.at_owner(step),
        )

    def finish():
        for step in range(1, place.seqs):
            landed = target.at[place.owner ^ step]
            remote(landed, landed, send.at[step], receive.at[step], place.at_owner(step)).wait_recv()
            copy(step).wait_send()

    def start():
        for step in range(1, place.seqs):
            copy(step).start()

    return start, finish


def end_exchange(grid, rows, wholes):
    shapes = [whole.shape[2:] for whole in wholes]
    count = len(wholes)

    def kernel(rows_ref, *refs):
        whole_refs, back_ref, results = refs[:count], refs[count], refs[count + 1 : 2 * count + 1]
        row_hold, hold_sem, row_send, row_receive = refs[2 * count + 1 : 2 * count + 5]
        place = Place(grid)
        meet(place.neighbours())
        reduce = reduce_of(place, whole_refs, results, refs[2 * count + 5 :])
        start_rows, finish_rows = row_exchange(place, rows_ref, back_ref, row_send, row_receive)
        stages = reduce.plan()
        stages[0][1]()
        start_rows()
        through(rows_ref.at[place.owner], row_hold, back_ref.at[place.owner], hold_sem)
        for _, action in stages[1:]:
            action()
        reduce.finish()
        finish_rows()

    return pl.pallas_call(
        kernel,
        in_specs=[HBM] * (count + 1),
        out_specs=[HBM] + [pl.BlockSpec(memory_space=pltpu.VMEM)] * count,
        out_shape=[jax.ShapeDtypeStruct(rows.shape, BF)]
        + [jax.ShapeDtypeStruct(shape, F32) for shape in shapes],
        scratch_shapes=[
            pltpu.VMEM(rows.shape[1:], BF),
            pltpu.SemaphoreType.DMA(()),
            pltpu.SemaphoreType.DMA((grid.seqs,)),
            pltpu.SemaphoreType.DMA((grid.seqs,)),
        ]
        + reduce_scratch(grid, shapes),
        compiler_params=pltpu.CompilerParams(
            collective_id=3, has_side_effects=True, vmem_limit_bytes=40 << 20
        ),
        name="end_exchange",
    )(rows, *wholes)


LOG2E = 1.4426950408889634
SCALE = 0.125 * LOG2E


def dot_nt(left, right):
    return lax.dot_general(left, right, (((1,), (1,)), ((), ())), preferred_element_type=F32)


def own_lanes(half, count):
    lane = lax.broadcasted_iota(jnp.int32, (count, 2 * HD), 1)
    return (lane // HD) == half, lane == HD * (1 - half)


def attention(grid, inputs, key_bias, shards, block=256):
    rows = inputs.shape[0]
    width = inputs.shape[1] // 3
    pairs = width // (2 * HD)
    count = grid.group
    keys = rows * count
    blocks = rows // block
    steps = pairs * blocks
    devices = grid.columns * grid.n
    late = len(shards)

    def kernel(q_ref, bias_ref, k_ref, v_ref, all_ref, *refs):
        shard_refs = refs[:late]
        o_ref, l_ref = refs[late : late + 2]
        whole_refs = refs[late + 2 : 2 * late + 2]
        k_own, v_own, far, hold_sem, send, receive, far_send, far_receive = refs[2 * late + 2 : 2 * late + 10]
        holds = refs[2 * late + 10 :]
        pair, turn = pl.program_id(0), pl.program_id(1)
        now = pair * blocks + turn
        place = Place(grid)
        gather = Gather(
            place,
            [(s, w, lambda ref, i: ref.at[i]) for s, w in zip(shard_refs, whole_refs)],
            send,
            receive,
        )

        def far_copy(step, which, kind):
            first = pl.multiple_of(which * 2 * HD + (kind + 1) * width, 2 * HD)
            return remote(
                all_ref.at[:, pl.ds(first, 2 * HD)],
                far.at[step - 1, kind, which],
                far_send.at[step - 1, kind, which],
                far_receive.at[step - 1, kind, which],
                place.at_member(step),
            )

        def first_step():
            meet(place.neighbours() + [place.at_member(s) for s in range(1, count) if count > 2])
            for which in range(pairs):
                for step in range(1, count):
                    for kind in range(2):
                        far_copy(step, which, kind).start()
            gather.start()
            me = place.index(0, 0)
            for shard, whole, hold in zip(shard_refs, whole_refs, holds):
                through(shard, hold, whole.at[me], hold_sem)

        plan = [(0.0, first_step)]
        for step in range(1, place.chips):
            plan.append((step * 0.66 / (place.chips - 1), lambda step=step: gather.from_chip(step)))
            plan.append((0.1 + step * 0.66 / (place.chips - 1), lambda step=step: gather.from_columns(step - 1)))

        def last_step():
            gather.from_columns(place.chips - 1)
            for step in range(place.chips):
                gather.from_corner(step)
            gather.finish()
            for step in range(1, count):
                for which in range(pairs):
                    for kind in range(2):
                        far_copy(step, which, kind).wait_send()

        for moment, action in plan:
            pl.when(now == int(moment * steps))(action)

        @pl.when(turn == 0)
        def _():
            for step in range(1, count):
                for kind in range(2):
                    far_copy(step, pair, kind).wait_recv()
            for half in range(2):
                own, spare = own_lanes(half, rows)
                zero = jnp.zeros((rows, 2 * HD), BF)
                for i in range(count):
                    at = slice(i * rows, (i + 1) * rows)
                    key = k_ref[...] if i == 0 else far[i - 1, 0, pair]
                    value = v_ref[...] if i == 0 else far[i - 1, 1, pair]
                    k_own[half, at, :] = jnp.where(own, key, jnp.where(spare, bias_ref[at, :], zero))
                    v_own[half, at, :] = jnp.where(own, value, jnp.where(spare, zero + 1, zero))

        query = q_ref[...]
        results = []
        for half in range(2):
            own, spare = own_lanes(half, block)
            zero = jnp.zeros_like(query)
            query_h = jnp.where(own, query, jnp.where(spare, zero + 1, zero))
            scores = dot_nt(query_h, k_own[half])
            largest = jnp.max(scores, axis=1, keepdims=True)
            weights = jnp.exp2((scores - largest) * SCALE).astype(BF)
            summed = matmul(weights, v_own[half])
            totals = summed[:, HD * (1 - half) : HD * (1 - half) + 1]
            results.append(summed / totals)
            log_total = jnp.broadcast_to(largest * SCALE + jnp.log2(totals), (block, 2 * HD))
            l_ref[half : half + 1, :] = jnp.transpose(log_total)[0:1, :]
        lane = lax.broadcasted_iota(jnp.int32, (block, 2 * HD), 1)
        o_ref[...] = jnp.where(lane < HD, results[0], results[1]).astype(BF)
        pl.when(now == steps - 1)(last_step)

    def column(first):
        return pl.BlockSpec((rows, 2 * HD), lambda i, j: (0, i + first))

    far_sems = pltpu.SemaphoreType.DMA((max(count - 1, 1), 2, pairs))
    return pl.pallas_call(
        kernel,
        grid=(pairs, blocks),
        in_specs=[
            pl.BlockSpec((block, 2 * HD), lambda i, j: (j, i)),
            pl.BlockSpec((keys, 2 * HD), lambda i, j: (0, 0)),
            column(pairs),
            column(2 * pairs),
            HBM,
        ]
        + [HBM] * late,
        out_specs=[
            pl.BlockSpec((block, 2 * HD), lambda i, j: (j, i)),
            pl.BlockSpec((None, 8, block), lambda i, j: (i, 0, j)),
        ]
        + [HBM] * late,
        out_shape=[
            jax.ShapeDtypeStruct((rows, width), BF),
            jax.ShapeDtypeStruct((pairs, 8, rows), F32),
        ]
        + [jax.ShapeDtypeStruct((devices,) + shard.shape, BF) for shard in shards],
        scratch_shapes=[
            pltpu.VMEM((2, keys, 2 * HD), BF),
            pltpu.VMEM((2, keys, 2 * HD), BF),
            pltpu.VMEM((max(count - 1, 1), 2, pairs, rows, 2 * HD), BF),
            pltpu.SemaphoreType.DMA(()),
        ]
        + gather_semaphores(grid, late)
        + [far_sems, far_sems]
        + [pltpu.VMEM(shard.shape, BF) for shard in shards],
        compiler_params=pltpu.CompilerParams(
            collective_id=1, has_side_effects=True, vmem_limit_bytes=48 << 20
        ),
        cost_estimate=pl.CostEstimate(
            flops=16 * H * rows * keys * HD, bytes_accessed=8 * rows * width, transcendentals=H * rows * keys
        ),
        name="attention",
    )(inputs, key_bias, inputs, inputs, inputs, *shards)


def attention_back(grid, inputs, key_bias, log_totals, context, grad_context, wholes, rows_out, block=256, chunk=1024):
    rows = inputs.shape[0]
    width = inputs.shape[1] // 3
    pairs = width // (2 * HD)
    count = grid.group
    keys = rows * count
    blocks = rows // block
    steps = pairs * blocks
    chunk = min(chunk, rows)
    chunks = keys // chunk
    late = len(wholes)
    shapes = [whole.shape[2:] for whole in wholes]
    away = max(count - 1, 1)

    def kernel(q_ref, bias_ref, l_ref, o_ref, g_ref, k_ref, v_ref, all_ref, rows_ref, *refs):
        whole_refs = refs[:late]
        out_ref, back_ref = refs[late : late + 2]
        results = refs[late + 2 : 2 * late + 2]
        rest = refs[2 * late + 2 :]
        k_own, k_turned, v_all, grad_k, grad_v, far, far_out, far_in, row_hold, hold_sem = rest[:10]
        far_send, far_receive, out_send, in_receive, row_send, row_receive = rest[10:16]
        pair, turn = pl.program_id(0), pl.program_id(1)
        now = pair * blocks + turn
        place = Place(grid)
        reduce = reduce_of(place, whole_refs, results, rest[16:])
        start_rows, finish_rows = row_exchange(place, rows_ref, back_ref, row_send, row_receive)

        def far_copy(step, which, kind):
            first = pl.multiple_of(which * 2 * HD + (kind + 1) * width, 2 * HD)
            return remote(
                all_ref.at[:, pl.ds(first, 2 * HD)],
                far.at[step - 1, kind, which],
                far_send.at[step - 1, kind, which],
                far_receive.at[step - 1, kind, which],
                place.at_member(step),
            )

        def back_copy(step, which, kind):
            return remote(
                far_out.at[step - 1, kind, which],
                far_in.at[step - 1, kind, which],
                out_send.at[step - 1, kind, which],
                in_receive.at[step - 1, kind, which],
                place.at_member(count - step),
            )

        def take_back(which):
            for kind in range(2):
                first = pl.multiple_of(which * 2 * HD + (kind + 1) * width, 2 * HD)
                total = out_ref[:, pl.ds(first, 2 * HD)].astype(F32)
                for step in range(1, count):
                    back_copy(step, which, kind).wait_recv()
                    total = total + far_in[step - 1, kind, which].astype(F32)
                out_ref[:, pl.ds(first, 2 * HD)] = total.astype(BF)

        def send_back(which):
            for step in range(1, count):
                for kind in range(2):
                    back_copy(step, which, kind).start()

        def first_step():
            meet(place.neighbours() + [place.at_member(s) for s in range(1, count) if count > 2])
            for which in range(pairs):
                for step in range(1, count):
                    for kind in range(2):
                        far_copy(step, which, kind).start()

        actions = [(0, first_step)] + reduce.plan()
        actions.append((0, start_rows))
        actions.append(
            (1, lambda: through(rows_ref.at[place.owner], row_hold, back_ref.at[place.owner], hold_sem))
        )
        moments = {}
        for moment, action in actions:
            moments.setdefault(moment * steps // 24, []).append(action)
        for moment, group in sorted(moments.items()):

            @pl.when(now == moment)
            def _(group=group):
                for action in group:
                    action()

        @pl.when((turn == 0) & (pair > 0))
        def _():
            send_back(pair - 1)

        @pl.when(turn == 0)
        def _():
            for step in range(1, count):
                for kind in range(2):
                    far_copy(step, pair, kind).wait_recv()
            for i in range(count):
                at = slice(i * rows, (i + 1) * rows)
                v_all[at, :] = v_ref[...] if i == 0 else far[i - 1, 1, pair]
                key = k_ref[...] if i == 0 else far[i - 1, 0, pair]
                for half in range(2):
                    own, spare = own_lanes(half, rows)
                    zero = jnp.zeros_like(key)
                    k_own[half, at, :] = jnp.where(own, key, jnp.where(spare, bias_ref[at, :], zero))
                    k_turned[half, :, at] = jnp.transpose(jnp.where(own, key, zero))
            grad_k[...] = jnp.zeros_like(grad_k)
            grad_v[...] = jnp.zeros_like(grad_v)

        query, grad = q_ref[...], g_ref[...]
        turned = jnp.transpose(grad.astype(F32) * o_ref[...].astype(F32))
        asks, plain, grads, centres, logs = [], [], [], [], []
        for half in range(2):
            own, spare = own_lanes(half, block)
            zero = jnp.zeros_like(query)
            asks.append(jnp.where(own, query, jnp.where(spare, zero + 1, zero)))
            plain.append(jnp.where(own, query, zero))
            grads.append(jnp.where(own, grad, zero))
            centres.append(jnp.sum(turned[HD * half : HD * half + HD], axis=0, keepdims=True))
            logs.append(l_ref[half : half + 1, :])
        grad_q = None
        for c in range(chunks):
            span = slice(c * chunk, (c + 1) * chunk)
            weights, slopes = [], []
            for half in range(2):
                scores = dot_nt(k_own[half, span, :], asks[half])
                grad_weights = dot_nt(v_all[span, :], grads[half])
                exact = jnp.exp2(scores * SCALE - logs[half])
                slope = (exact * (grad_weights - centres[half])).astype(BF)
                weights.append(exact.astype(BF))
                slopes.append(slope)
                step = matmul(k_turned[half, :, span], slope)
                grad_q = step if grad_q is None else grad_q + step
            grad_v[span, :] += matmul(weights[0], grads[0]) + matmul(weights[1], grads[1])
            grad_k[span, :] += matmul(slopes[0], plain[0]) + matmul(slopes[1], plain[1])
        at = pl.ds(pl.multiple_of(turn * block, block), block)
        out_ref[at, pl.ds(pl.multiple_of(pair * 2 * HD, 2 * HD), 2 * HD)] = (
            jnp.transpose(grad_q) * 0.125
        ).astype(BF)

        @pl.when(turn == blocks - 1)
        def _():
            for i in range(count):
                at = slice(i * rows, (i + 1) * rows)
                for kind, value, scale in ((0, grad_k, 0.125), (1, grad_v, 1.0)):
                    low = (value[at, :] * scale).astype(BF)
                    if i == 0:
                        first = pl.multiple_of(pair * 2 * HD + (kind + 1) * width, 2 * HD)
                        out_ref[:, pl.ds(first, 2 * HD)] = low
                    else:
                        far_out[i - 1, kind, pair] = low

        @pl.when((turn == blocks - 1) & (pair > 0))
        def _():
            take_back(pair - 1)

        @pl.when(now == steps - 1)
        def _():
            reduce.finish()
            send_back(pairs - 1)
            finish_rows()
            take_back(pairs - 1)
            for step in range(1, count):
                for which in range(pairs):
                    for kind in range(2):
                        far_copy(step, which, kind).wait_send()
                        back_copy(step, which, kind).wait_send()

    def column(first):
        return pl.BlockSpec((rows, 2 * HD), lambda i, j: (0, i + first))

    def tile():
        return pl.BlockSpec((block, 2 * HD), lambda i, j: (j, i))

    def resident(shape):
        return pl.BlockSpec(shape, lambda i, j: (0,) * len(shape))

    far_sems = pltpu.SemaphoreType.DMA((away, 2, pairs))
    far_buffer = pltpu.VMEM((away, 2, pairs, rows, 2 * HD), BF)
    return pl.pallas_call(
        kernel,
        grid=(pairs, blocks),
        in_specs=[
            tile(),
            resident((keys, 2 * HD)),
            pl.BlockSpec((None, 8, block), lambda i, j: (i, 0, j)),
            tile(),
            tile(),
            column(pairs),
            column(2 * pairs),
            HBM,
            HBM,
        ]
        + [HBM] * late,
        out_specs=[resident(inputs.shape), HBM] + [resident(tuple(shape)) for shape in shapes],
        out_shape=[jax.ShapeDtypeStruct(inputs.shape, BF), jax.ShapeDtypeStruct(rows_out.shape, BF)]
        + [jax.ShapeDtypeStruct(shape, F32) for shape in shapes],
        scratch_shapes=[
            pltpu.VMEM((2, keys, 2 * HD), BF),
            pltpu.VMEM((2, 2 * HD, keys), BF),
            pltpu.VMEM((keys, 2 * HD), BF),
            pltpu.VMEM((keys, 2 * HD), F32),
            pltpu.VMEM((keys, 2 * HD), F32),
            far_buffer,
            far_buffer,
            far_buffer,
            pltpu.VMEM(rows_out.shape[1:], BF),
            pltpu.SemaphoreType.DMA(()),
        ]
        + [far_sems] * 4
        + [pltpu.SemaphoreType.DMA((grid.seqs,))] * 2
        + reduce_scratch(grid, shapes),
        compiler_params=pltpu.CompilerParams(
            collective_id=2, has_side_effects=True, vmem_limit_bytes=61 << 20
        ),
        cost_estimate=pl.CostEstimate(
            flops=40 * H * rows * keys * HD, bytes_accessed=12 * rows * width, transcendentals=H * rows * keys
        ),
        name="attention_back",
    )(inputs, key_bias, log_totals, context, grad_context, inputs, inputs, inputs, rows_out, *wholes)


def body(
    tokens,
    lengths,
    query_weight,
    key_weight,
    value_weight,
    out_weight,
    up_weight,
    down_weight,
    query_bias,
    value_bias,
    out_bias,
    up_bias,
    down_bias,
    first_gain,
    first_shift,
    second_gain,
    second_shift,
    cotangent,
):
    seqs, length, width = tokens.shape
    grid = Grid(seqs)
    devices = grid.columns * grid.n
    slim = query_weight.shape[0]
    hidden = up_weight.shape[1]
    tall = hidden // devices
    wide = hidden // width

    vectors = (
        query_bias,
        value_bias,
        out_bias,
        down_bias,
        first_gain,
        first_shift,
        second_gain,
        second_shift,
    )
    vectors = vectors + (up_bias,)
    lines = -(-len(vectors) // 16) * 16
    tile = jnp.zeros((lines, 128), BF)
    for i, vector in enumerate(vectors):
        size = vector.shape[0]
        tile = tile + jnp.pad(vector[None, :], ((i, lines - 1 - i), (0, 128 - size)))
    flat_in, into_full, _, key_bias, live_rows, *whole_vectors = start_exchange(
        grid,
        tokens,
        (query_weight, key_weight, value_weight),
        tile,
        lengths,
        tuple(vector.shape[0] for vector in vectors),
    )
    flat_in = flat_in.reshape(-1, width)
    into_full = into_full.reshape(width, 3 * width)
    query_add, value_add, out_add, down_add, gain_one, shift_one, gain_two, shift_two, up_add = whole_vectors

    into_add = jnp.concatenate([query_add, jnp.zeros_like(query_add), value_add], axis=1)
    inputs = (matmul(flat_in, into_full) + into_add).astype(BF)
    context, log_totals, out_full, up_full, down_full = attention(
        grid, inputs, key_bias, (out_weight, up_weight, down_weight)
    )
    out_full = out_full.reshape(width, width)
    up_full = up_full.reshape(width, hidden)
    down_full = down_full.reshape(hidden, width)
    cotangent = lax.optimization_barrier((cotangent, context))[0]
    grad_in = to_sequences(grid, cotangent)

    first_sum = flat_in.astype(F32) + matmul(context, out_full) + out_add
    first_norm, first_unit, first_factor = normalize(first_sum, gain_one, shift_one)
    first_low = first_norm.astype(BF)
    up_pre = matmul(first_low, up_full) + up_add
    below = 0.5 * (1.0 + lax.erf(up_pre * ROOT_HALF))
    slope = (below + up_pre * INV_ROOT_TWO_PI * jnp.exp(-0.5 * up_pre * up_pre)).astype(BF)
    activated, slope = lax.optimization_barrier(((up_pre * below).astype(BF), slope))
    second_sum = first_low.astype(F32) + matmul(activated, down_full) + down_add
    second_norm, second_unit, second_factor = normalize(second_sum, gain_two, shift_two)
    output = (second_norm * live_rows).astype(BF).reshape(seqs, length, width)

    grad_output = grad_in.astype(F32) * live_rows
    grad_gain_two = jnp.sum(grad_output * second_unit, axis=0)
    grad_shift_two = jnp.sum(grad_output, axis=0)
    grad_second = norm_back(grad_output, second_unit, second_factor, gain_two)
    grad_branch = grad_second.astype(BF)
    grad_down_add = jnp.sum(grad_branch.astype(F32), axis=0)
    grad_down = left_product(activated, grad_branch).astype(BF)
    grad_up_low = (right_product(grad_branch, down_full) * slope.astype(F32)).astype(BF)
    grad_up_add = jnp.sum(grad_up_low.astype(F32), axis=0)
    grad_up = left_product(first_low, grad_up_low).astype(BF)
    grad_first = right_product(grad_up_low, up_full) + grad_second
    grad_gain_one = jnp.sum(grad_first * first_unit, axis=0)
    grad_shift_one = jnp.sum(grad_first, axis=0)
    grad_residual = norm_back(grad_first, first_unit, first_factor, gain_one)
    grad_attend = grad_residual.astype(BF)
    grad_out_add = jnp.sum(grad_attend.astype(F32), axis=0)
    grad_out = left_product(context, grad_attend).astype(BF)
    grad_context = right_product(grad_attend, out_full).astype(BF)

    def pack(grads, more=()):
        count = len(grads)
        table = jnp.stack(grads).reshape(count, devices, slim).transpose(1, 0, 2)
        table = jnp.concatenate([table.reshape(devices, count * slim), *more], axis=1).astype(BF)
        size = table.shape[1]
        table = jnp.pad(table, ((0, 0), (0, -size % 128)))
        return jnp.broadcast_to(table[:, None, :], (devices, 8, table.shape[1])).reshape(devices * 8, -1)

    middle = pack(
        [grad_out_add, grad_down_add, grad_gain_one, grad_shift_one, grad_gain_two, grad_shift_two],
        (grad_up_add.reshape(devices, tall),),
    )
    wholes = [
        by_place(grid, grad_up, slim),
        by_place(grid, grad_down, tall),
        by_place(grid, grad_out, slim),
        by_place(grid, middle, 8),
    ]
    low, output, grad_up_own, grad_down_own, grad_out_own, middle_own = attention_back(
        grid, inputs, key_bias, log_totals, context, grad_context, wholes, output
    )
    query_adds = jnp.sum(low[:, :width].astype(F32), axis=0)
    value_adds = jnp.sum(low[:, 2 * width :].astype(F32), axis=0)
    tokens_grad = right_product(low, into_full) + grad_residual
    wholes = [
        by_place(grid, left_product(flat_in, low).astype(BF), slim),
        by_place(grid, pack([query_adds, value_adds]), 8),
    ]
    tokens_grad = tokens_grad.astype(BF).reshape(seqs, length, width)
    tokens_grad, grad_into_own, last_own = end_exchange(grid, tokens_grad, wholes)
    tokens_grad = tokens_grad.astype(F32)
    middle_own, last_own = middle_own[0], last_own[0]
    vector_outs = [last_own[:slim], last_own[slim : 2 * slim]]
    vector_outs = vector_outs + [middle_own[i * slim : (i + 1) * slim] for i in range(6)]
    up_add_own = middle_own[6 * slim : 6 * slim + tall]
    matrix_outs = [grad_into_own[:, i * width : (i + 1) * width] for i in range(3)]
    return (
        output,
        tokens_grad,
        matrix_outs[0],
        matrix_outs[1],
        matrix_outs[2],
        grad_out_own,
        grad_up_own,
        grad_down_own,
        vector_outs[0],
        vector_outs[1],
        vector_outs[2],
        up_add_own,
        vector_outs[3],
        vector_outs[4],
        vector_outs[5],
        vector_outs[6],
        vector_outs[7],
    )


def solution(mesh):
    whole = ("dp", "seq")
    matrix, vector, rows = P(whole, None), P(whole), P("dp", "seq", None)
    return jax.shard_map(
        body,
        mesh=mesh,
        in_specs=(rows, P("dp")) + (matrix,) * 6 + (vector,) * 9 + (rows,),
        out_specs=(rows, rows) + (matrix,) * 6 + (vector,) * 9,
        check_vma=False,
    )
```

```python
import jax
import jax.numpy as jnp
from jax import lax
from jax.experimental import pallas as pl
from jax.experimental.pallas import tpu as pltpu
from jax.sharding import PartitionSpec as P

H = 12
HD = 64

EPSILON = 1e-05
ROOT_HALF = 0.7071067811865476
INV_ROOT_TWO_PI = 0.3989422804014327
BF = jnp.bfloat16
F32 = jnp.float32


def matmul(left, right):
    return jnp.dot(left, right, preferred_element_type=F32)


def left_product(left, right):
    return lax.dot_general(left, right, (((0,), (0,)), ((), ())), preferred_element_type=F32)


def right_product(left, right):
    return lax.dot_general(left, right, (((1,), (1,)), ((), ())), preferred_element_type=F32)


def normalize(inputs, gains, shifts):
    centre = inputs - jnp.mean(inputs, axis=-1, keepdims=True)
    factor = lax.rsqrt(jnp.mean(centre * centre, axis=-1, keepdims=True) + EPSILON)
    unit_rows = centre * factor
    return (unit_rows * gains + shifts, unit_rows, factor)


def norm_back(grad_in, unit_rows, factor, gains):
    grad_unit = grad_in * gains
    return factor * (
        grad_unit
        - jnp.mean(grad_unit, axis=-1, keepdims=True)
        - unit_rows * jnp.mean(grad_unit * unit_rows, axis=-1, keepdims=True)
    )


class Grid:
    def __init__(self, seqs):
        self.columns = lax.axis_size("dp")
        self.n = lax.axis_size("seq")
        self.seqs = seqs
        self.group = self.n // seqs
        self.chips = self.n // 2
        self.column = lax.axis_index("dp")
        place = lax.axis_index("seq")
        self.chip = place // 2
        self.core = place % 2
        self.owner = place // self.group
        self.member = place % self.group


MESH = pl.DeviceIdType.MESH
HBM = pl.BlockSpec(memory_space=pl.ANY)


def remote(source, target, send, receive, device):
    return pltpu.make_async_remote_copy(
        src_ref=source, dst_ref=target, send_sem=send, recv_sem=receive, device_id=device, device_id_type=MESH
    )


def meet(devices):
    barrier = pltpu.get_barrier_semaphore()
    for device in devices:
        pl.semaphore_signal(barrier, inc=1, device_id=device, device_id_type=MESH)
    pl.semaphore_wait(barrier, len(devices))


class Place:
    def __init__(self, grid):
        self.columns, self.chips, self.n = grid.columns, grid.chips, grid.n
        self.seqs, self.group = grid.seqs, grid.group
        self.column = lax.axis_index("dp")
        self.spot = lax.axis_index("seq")
        self.chip = lax.div(self.spot, 2)
        self.core = lax.rem(self.spot, 2)
        self.owner = lax.div(self.spot, self.group)
        self.member = lax.rem(self.spot, self.group)

    def near(self, chip_step):
        return (self.column, (self.chip ^ chip_step) * 2 + self.core)

    def beside(self, column_step):
        return (self.column ^ column_step, self.spot)

    def twin(self):
        return (self.column, self.chip * 2 + (1 - self.core))

    def at_owner(self, step):
        return (self.column, (self.owner ^ step) * self.group + self.member)

    def at_member(self, step):
        return (self.column, self.owner * self.group + lax.rem(self.member + step, self.group))

    def index(self, column_step, chip_step, other=False):
        core = 1 - self.core if other else self.core
        return ((self.column ^ column_step) * self.chips + (self.chip ^ chip_step)) * 2 + core

    def neighbours(self):
        chips = [self.near(step) for step in range(1, self.chips)]
        columns = [self.beside(step) for step in range(1, self.columns)]
        return chips + columns + [self.twin()]


class Gather:
    def __init__(self, place, arrays, send, receive):
        self.place, self.arrays, self.send, self.receive = place, arrays, send, receive
        self.square = place.columns == 4
        self.sent = []

    def copies(self, kind, column_step, chip_step, device, own=False, where=None):
        slot = column_step * self.place.chips + chip_step
        for k, (shard, whole, block) in enumerate(self.arrays):
            held = block(whole, self.place.index(*(where or (column_step, chip_step))))
            yield remote(
                shard if own else held, held, self.send.at[k, kind, slot], self.receive.at[k, kind, slot], device
            )

    def begin(self, kind, column_step, chip_step, device, own=False, where=None):
        self.sent.append((kind, column_step, chip_step, own, where))
        for copy in self.copies(kind, column_step, chip_step, device, own, where):
            copy.start()

    def to_twin(self, column_step, chip_step, own=False):
        self.begin(1, column_step, chip_step, self.place.twin(), own=own)

    def outward(self, chip_step):
        place, own = self.place, chip_step == 0
        for step in range(1, place.columns):
            if not (self.square and step == 3):
                self.begin(0, step, chip_step, place.beside(step), own=own, where=(0, chip_step))
        self.to_twin(0, chip_step, own=own)

    def to_chip(self, step):
        self.begin(0, 0, step, self.place.near(step), own=True, where=(0, 0))

    def start(self):
        for step in range(1, self.place.chips):
            self.to_chip(step)
        self.outward(0)

    def arrive(self, column_step, chip_step, other=False):
        for k, (_, whole, block) in enumerate(self.arrays):
            held = block(whole, self.place.index(column_step, chip_step, other))
            kind = 1 if other else 0
            slot = column_step * self.place.chips + chip_step
            remote(
                held, held, self.send.at[k, kind, slot], self.receive.at[k, kind, slot], self.place.twin()
            ).wait_recv()

    def from_chip(self, chip_step):
        self.arrive(0, chip_step)
        self.outward(chip_step)

    def from_columns(self, chip_step):
        for step in range(1, self.place.columns):
            if self.square and step == 3:
                continue
            self.arrive(step, chip_step)
            if self.square and step == 1 + chip_step % 2:
                self.begin(0, 3, chip_step, self.place.beside(3 - step), where=(step, chip_step))
            self.to_twin(step, chip_step)

    def from_corner(self, chip_step):
        if self.square:
            self.arrive(3, chip_step)
            self.to_twin(3, chip_step)

    def finish(self):
        place = self.place
        for column_step in range(place.columns):
            for chip_step in range(place.chips):
                self.arrive(column_step, chip_step, other=True)
        for kind, column_step, chip_step, own, where in self.sent:
            for copy in self.copies(kind, column_step, chip_step, place.twin(), own, where):
                copy.wait_send()


def gather_semaphores(grid, count):
    shape = (count, 2, grid.columns * grid.chips)
    return [pltpu.SemaphoreType.DMA(shape), pltpu.SemaphoreType.DMA(shape)]


def through(source, held, target, sem):
    copy = pltpu.make_async_copy(source, held, sem)
    copy.start()
    copy.wait()
    copy = pltpu.make_async_copy(held, target, sem)
    copy.start()
    copy.wait()


def start_exchange(grid, tokens, into, vectors, lengths, vector_widths):
    seqs, length, width = tokens.shape
    devices = grid.columns * grid.n
    slim = into[0].shape[0]
    parts = len(into)
    rows = seqs * length
    tile = vectors.shape

    def spread(table, size):
        lane = lax.broadcasted_iota(jnp.int32, (128, devices * size), 1).astype(F32)
        row = lax.broadcasted_iota(jnp.int32, (128, devices * size), 0).astype(F32)
        within = lane - size * jnp.floor((lane + 0.5) * (1.0 / size))
        return matmul(table, (row == within).astype(BF))

    def own_block(count, size):
        lane = lax.broadcasted_iota(jnp.int32, (count, devices * size), 1).astype(F32)
        return jnp.floor((lane + 0.5) * (1.0 / size))

    def kernel(tokens_ref, query_ref, key_ref, value_ref, vectors_ref, lengths_ref, rows_ref, into_all, vectors_all, *rest):
        into_refs = (query_ref, key_ref, value_ref)
        bias_ref, live_ref = rest[:2]
        vector_refs = rest[2 : 2 + len(vector_widths)]
        scratch = rest[2 + len(vector_widths) :]
        row_hold, into_hold, vector_hold, table_hold, hold_sem, send, receive, row_send, row_receive = scratch
        place = Place(grid)
        meet(place.neighbours())

        def part(k):
            return lambda ref, i: ref.at[i, :, pl.ds(k * width, width)]

        gather = Gather(
            place,
            [(into_refs[k], into_all, part(k)) for k in range(parts)]
            + [(vectors_ref, vectors_all, lambda ref, i: ref.at[i])],
            send,
            receive,
        )
        gather.start()

        def row_copy(step):
            return remote(
                tokens_ref.at[place.owner ^ step],
                rows_ref.at[place.owner],
                row_send.at[step],
                row_receive.at[step],
                place.at_owner(step),
            )

        for step in range(1, seqs):
            row_copy(step).start()
        me = place.index(0, 0)
        for k in range(parts):
            through(into_refs[k], into_hold, part(k)(into_all, me), hold_sem)
        through(vectors_ref, vector_hold, vectors_all.at[me], hold_sem)
        through(tokens_ref.at[place.owner], row_hold, rows_ref.at[place.owner], hold_sem)

        my_length = lengths_ref[place.owner]
        for step in range(place.group):
            member = lax.rem(place.member - step + place.group, place.group)
            for source in range(seqs):
                first = (source * place.group + member) * length
                at = slice(step * rows + source * length, step * rows + (source + 1) * length)
                here = lax.broadcasted_iota(jnp.int32, (length, 2 * HD), 0) + first
                bias_ref[at, :] = jnp.where(here < my_length, 0.0, -1e30).astype(BF)
                if step == 0:
                    here = lax.broadcasted_iota(jnp.int32, (length, 1), 0) + first
                    live_ref[at, :] = jnp.where(here < my_length, 1.0, 0.0).astype(F32)

        for step in range(1, place.chips):
            gather.from_chip(step)
            gather.from_columns(step - 1)
        gather.from_columns(place.chips - 1)
        for step in range(place.chips):
            gather.from_corner(step)
        gather.finish()
        copy = pltpu.make_async_copy(vectors_all, table_hold, hold_sem)
        copy.start()
        copy.wait()
        table = table_hold[...].astype(F32)
        kind = lax.broadcasted_iota(jnp.int32, table.shape, 1)
        source = lax.broadcasted_iota(jnp.int32, (devices, 1), 0).astype(F32)
        for k, size in enumerate(vector_widths):
            own = jnp.sum(jnp.where(kind == k, table, 0.0), axis=1).astype(BF)
            apart = jnp.where(own_block(devices, size) == source, spread(own, size), 0.0)
            vector_refs[k][...] = jnp.sum(apart, axis=0, keepdims=True)
        for step in range(1, seqs):
            landed = rows_ref.at[place.owner ^ step]
            remote(
                landed, landed, row_send.at[step], row_receive.at[step], place.at_owner(step)
            ).wait_recv()
            row_copy(step).wait_send()

    vmem = pl.BlockSpec(memory_space=pltpu.VMEM)
    shapes = [tokens.shape, (devices, slim, parts * width), (devices,) + tile]
    return pl.pallas_call(
        kernel,
        in_specs=[HBM] * (parts + 2) + [pl.BlockSpec(memory_space=pltpu.SMEM)],
        out_specs=[HBM] * 3 + [vmem] * (2 + len(vector_widths)),
        out_shape=[jax.ShapeDtypeStruct(shape, BF) for shape in shapes]
        + [jax.ShapeDtypeStruct((grid.group * rows, 2 * HD), BF), jax.ShapeDtypeStruct((rows, 1), F32)]
        + [jax.ShapeDtypeStruct((1, devices * size), F32) for size in vector_widths],
        scratch_shapes=[
            pltpu.VMEM(tokens.shape[1:], BF),
            pltpu.VMEM(into[0].shape, BF),
            pltpu.VMEM(tile, BF),
            pltpu.VMEM((devices,) + tile, BF),
            pltpu.SemaphoreType.DMA(()),
        ]
        + gather_semaphores(grid, parts + 1)
        + [pltpu.SemaphoreType.DMA((seqs,)), pltpu.SemaphoreType.DMA((seqs,))],
        compiler_params=pltpu.CompilerParams(collective_id=0, has_side_effects=True),
        name="start_exchange",
    )(tokens, *into, vectors, lengths)


class Reduce:
    def __init__(self, place, arrays, buffers, semaphores):
        self.place, self.arrays = place, arrays
        self.halves, self.twins, self.sides, self.deeps = buffers
        self.load, self.twin_sems, self.side_sems, self.deep_sems = semaphores
        self.square = place.columns == 4
        self.every = range(len(arrays))
        self.sent = []

    def spot(self, column_step, chip_step):
        return (self.place.column ^ column_step) * self.place.chips + (self.place.chip ^ chip_step)

    def strip(self, column_step):
        return pl.ds((self.place.column ^ column_step) * self.place.chips, self.place.chips)

    def load_copy(self, k, step):
        whole = self.arrays[k][0].at[self.strip(step), self.place.core]
        return pltpu.make_async_copy(whole, self.halves[k].at[self.strip(step)], self.load.at[k, step])

    def twin_copy(self, k, step):
        place = self.place
        whole = self.arrays[k][0].at[self.strip(step), 1 - place.core]
        return remote(
            whole,
            self.twins[k].at[self.strip(step)],
            self.twin_sems[0].at[k, step],
            self.twin_sems[1].at[k, step],
            place.twin(),
        )

    def side_copy(self, k, column_step, chip_step, device):
        return remote(
            self.halves[k].at[self.spot(column_step, chip_step)],
            self.sides[k].at[column_step, chip_step],
            self.side_sems[0].at[k, column_step, chip_step],
            self.side_sems[1].at[k, column_step, chip_step],
            device,
        )

    def deep_copy(self, k, chip_step):
        return remote(
            self.halves[k].at[self.spot(0, chip_step)],
            self.deeps[k].at[chip_step],
            self.deep_sems[0].at[k, chip_step],
            self.deep_sems[1].at[k, chip_step],
            self.place.near(chip_step),
        )

    def start(self):
        order = range(self.place.columns - 1, -1, -1)
        for step in order:
            for k in self.every:
                self.twin_copy(k, step).start()
                self.load_copy(k, step).start()

    def fold(self, step):
        for k in self.every:
            self.load_copy(k, step).wait()
            self.twin_copy(k, step).wait_recv()
            half, twin = self.halves[k], self.twins[k]
            for chip_step in range(self.place.chips):
                spot = self.spot(step, chip_step)
                half[spot] = (half[spot].astype(F32) + twin[spot].astype(F32)).astype(BF)

    def corner(self, chip_step):
        self.sent.append((3, chip_step))
        for k in self.every:
            self.side_copy(k, 3, chip_step, self.place.beside(1 + chip_step % 2)).start()

    def side(self, column_step, chip_step):
        self.sent.append((column_step, chip_step))
        for k in self.every:
            self.side_copy(k, column_step, chip_step, self.place.beside(column_step)).start()

    def combine(self, chip_step):
        for k in self.every:
            self.side_copy(k, 3, chip_step, self.place.twin()).wait_recv()
            spot = self.spot(2 - chip_step % 2, chip_step)
            half = self.halves[k]
            half[spot] = (half[spot].astype(F32) + self.sides[k][3, chip_step].astype(F32)).astype(BF)

    def merge(self, chip_step):
        last = 3 if self.square else self.place.columns
        for k in self.every:
            spot = self.spot(0, chip_step)
            total = self.halves[k][spot].astype(F32)
            for step in range(1, last):
                self.side_copy(k, step, chip_step, self.place.twin()).wait_recv()
                total = total + self.sides[k][step, chip_step].astype(F32)
            self.halves[k][spot] = total.astype(BF)

    def deep(self, chip_step):
        for k in self.every:
            self.deep_copy(k, chip_step).start()

    def finish(self):
        place = self.place
        for k in self.every:
            total = self.halves[k][self.spot(0, 0)].astype(F32)
            for step in range(1, place.chips):
                self.deep_copy(k, step).wait_recv()
                total = total + self.deeps[k][step].astype(F32)
            self.arrays[k][1][...] = total
            for step in range(1, place.chips):
                self.deep_copy(k, step).wait_send()
            for step in range(place.columns):
                self.twin_copy(k, step).wait_send()
            for column_step, chip_step in self.sent:
                self.side_copy(k, column_step, chip_step, place.twin()).wait_send()

    def plan(self):
        chips, columns = self.place.chips, self.place.columns
        stages = [(0, self.start)]
        if not self.square:
            for step in range(columns):
                stages.append((1, lambda step=step: self.fold(step)))
            for step in range(1, columns):
                for chip_step in range(chips):
                    stages.append((3, lambda a=step, b=chip_step: self.side(a, b)))
            for chip_step in range(chips):
                stages.append((16, lambda b=chip_step: self.merge(b)))
            for chip_step in range(1, chips):
                stages.append((17, lambda b=chip_step: self.deep(b)))
            return stages
        odd = list(range(1, chips, 2))
        even = list(range(2, chips, 2))
        first = [("corner", b) for b in even] + [(1, b) for b in even] + [(1, b) for b in odd] + [("corner", 0), (1, 0)]
        second = [("corner", b) for b in odd] + [(2, b) for b in odd] + [(2, b) for b in even] + [(2, 0)]
        slots = max(len(first), len(second))
        pace = 14.4 / slots
        mixed = [("fold", 3, 1.9), ("fold", 1, 3.9), ("fold", 2, 3.9), ("fold", 0, 6)]
        corners, last_side = {}, {}
        for link, orders in ((1, first), (2, second)):
            for i, (kind, b) in enumerate(orders):
                if kind == "corner":
                    corners[b] = 2 + pace * i
                    mixed.append(("corner", b, corners[b]))
        for link, orders in ((1, first), (2, second)):
            for i, (kind, b) in enumerate(orders):
                if kind == "corner":
                    continue
                moment = 2 + pace * i
                if link == 2 - b % 2:
                    moment = max(moment, corners[b] + pace + 1.6)
                    mixed.append(("combine", b, moment - 1))
                mixed.append((("side", link), b, moment))
                last_side[b] = max(last_side.get(b, 0), moment)
        for b, moment in last_side.items():
            mixed.append(("merge", b, moment + pace + 0.6))
            if b:
                mixed.append(("deep", b, moment + pace + 1.6))
        mixed.sort(key=lambda item: item[2])
        for kind, b, moment in mixed:
            if isinstance(kind, tuple):
                stages.append((moment, lambda a=kind[1], b=b: self.side(a, b)))
            else:
                stages.append((moment, lambda kind=kind, b=b: getattr(self, kind)(b)))
        return stages


def reduce_scratch(grid, shapes):
    columns, chips, count = grid.columns, grid.chips, len(shapes)
    buffers = []
    for lead in ((columns * chips,), (columns * chips,), (columns, chips), (chips,)):
        buffers = buffers + [pltpu.VMEM(lead + tuple(shape), BF) for shape in shapes]
    dma = pltpu.SemaphoreType.DMA
    sems = [dma((count, columns))] * 3 + [dma((count, columns, chips))] * 2 + [dma((count, chips))] * 2
    return buffers + sems


def reduce_of(place, wholes, results, scratch):
    count = len(wholes)
    groups = [scratch[i * count : (i + 1) * count] for i in range(4)]
    sems = scratch[4 * count : 4 * count + 7]
    return Reduce(
        place, list(zip(wholes, results)), groups, (sems[0], sems[1:3], sems[3:5], sems[5:7])
    )


def by_place(grid, array_in, rows):
    return array_in.reshape(grid.columns * grid.chips, 2, rows, -1)


def row_exchange(place, source, target, send, receive):
    def copy(step):
        return remote(
            source.at[place.owner ^ step],
            target.at[place.owner],
            send.at[step],
            receive.at[step],
            place.at_owner(step),
        )

    def finish():
        for step in range(1, place.seqs):
            landed = target.at[place.owner ^ step]
            remote(landed, landed, send.at[step], receive.at[step], place.at_owner(step)).wait_recv()
            copy(step).wait_send()

    def start():
        for step in range(1, place.seqs):
            copy(step).start()

    return start, finish


def end_exchange(grid, rows, wholes):
    shapes = [whole.shape[2:] for whole in wholes]
    count = len(wholes)

    def kernel(rows_ref, *refs):
        whole_refs, back_ref, results = refs[:count], refs[count], refs[count + 1 : 2 * count + 1]
        row_hold, hold_sem, row_send, row_receive = refs[2 * count + 1 : 2 * count + 5]
        place = Place(grid)
        meet(place.neighbours())
        reduce = reduce_of(place, whole_refs, results, refs[2 * count + 5 :])
        start_rows, finish_rows = row_exchange(place, rows_ref, back_ref, row_send, row_receive)
        stages = reduce.plan()
        stages[0][1]()
        start_rows()
        through(rows_ref.at[place.owner], row_hold, back_ref.at[place.owner], hold_sem)
        for _, action in stages[1:]:
            action()
        reduce.finish()
        finish_rows()

    return pl.pallas_call(
        kernel,
        in_specs=[HBM] * (count + 1),
        out_specs=[HBM] + [pl.BlockSpec(memory_space=pltpu.VMEM)] * count,
        out_shape=[jax.ShapeDtypeStruct(rows.shape, BF)]
        + [jax.ShapeDtypeStruct(shape, F32) for shape in shapes],
        scratch_shapes=[
            pltpu.VMEM(rows.shape[1:], BF),
            pltpu.SemaphoreType.DMA(()),
            pltpu.SemaphoreType.DMA((grid.seqs,)),
            pltpu.SemaphoreType.DMA((grid.seqs,)),
        ]
        + reduce_scratch(grid, shapes),
        compiler_params=pltpu.CompilerParams(
            collective_id=3, has_side_effects=True, vmem_limit_bytes=40 << 20
        ),
        name="end_exchange",
    )(rows, *wholes)


LOG2E = 1.4426950408889634
SCALE = 0.125 * LOG2E


def dot_nt(left, right):
    return lax.dot_general(left, right, (((1,), (1,)), ((), ())), preferred_element_type=F32)


def own_lanes(half, count):
    lane = lax.broadcasted_iota(jnp.int32, (count, 2 * HD), 1)
    return (lane // HD) == half, lane == HD * (1 - half)


def attention(grid, inputs, key_bias, shards, rows_in, block=256):
    rows = inputs.shape[0]
    width = inputs.shape[1] // 3
    pairs = width // (2 * HD)
    count = grid.group
    keys = rows * count
    blocks = rows // block
    steps = pairs * blocks
    devices = grid.columns * grid.n
    late = len(shards)

    def kernel(bias_ref, own_ref, all_ref, rows_ref, *refs):
        shard_refs = refs[:late]
        o_ref, l_ref, block_ref = refs[late : late + 3]
        whole_refs = refs[late + 3 : 2 * late + 3]
        rest = refs[2 * late + 3 :]
        k_own, v_own, far, hold_sem, send, receive, far_send, far_receive, row_send, row_receive = rest[:10]
        holds = rest[10:]
        pair, turn = pl.program_id(0), pl.program_id(1)
        now = pair * blocks + turn
        place = Place(grid)
        gather = Gather(
            place,
            [(s, w, lambda ref, i: ref.at[i]) for s, w in zip(shard_refs, whole_refs)],
            send,
            receive,
        )

        def part(kind):
            return own_ref[:, pl.ds(pl.multiple_of(kind * width + pair * 2 * HD, 2 * HD), 2 * HD)]

        def far_copy(step, which, kind):
            first = pl.multiple_of(which * 2 * HD + (kind + 1) * width, 2 * HD)
            return remote(
                all_ref.at[:, pl.ds(first, 2 * HD)],
                far.at[step - 1, kind, which],
                far_send.at[step - 1, kind, which],
                far_receive.at[step - 1, kind, which],
                place.at_member(step),
            )

        def first_step():
            meet(place.neighbours() + [place.at_member(s) for s in range(1, count) if count > 2])
            start_far(0)
            gather.start()
            for k in range(late + 1):
                own_copy(k, 0).start()
            for which in range(1, pairs):
                start_far(which)

        def start_far(which):
            for step in range(1, count):
                for kind in range(2):
                    far_copy(step, which, kind).start()

        start_rows, finish_rows = row_exchange(place, rows_ref, block_ref, row_send, row_receive)

        def own_copy(k, way):
            if k == late:
                source, target = rows_ref.at[place.owner], block_ref.at[place.owner]
            else:
                source, target = shard_refs[k], whole_refs[k].at[place.index(0, 0)]
            if way == 0:
                return pltpu.make_async_copy(source, holds[k], hold_sem.at[k, 0])
            return pltpu.make_async_copy(holds[k], target, hold_sem.at[k, 1])

        def own_onward():
            for k in range(late + 1):
                own_copy(k, 0).wait()
                own_copy(k, 1).start()

        chips = place.chips
        pace = 8 / max(chips - 2, 1)
        plan = [(0, first_step), (1, own_onward), (8, lambda: gather.from_chip(1)), (8, lambda: gather.from_columns(0))]
        plan.append((10, start_rows))
        for step in range(2, chips):
            moment = 12 + pace * (step - 2)
            plan.append((moment - 0.01 * (step > 2), lambda step=step: gather.from_chip(step)))
            plan.append((moment, lambda step=step: gather.from_columns(step - 1)))
        plan.append((20, lambda: gather.from_columns(chips - 1)))
        moments = {}
        for moment, action in plan:
            moments.setdefault(min(int(moment * steps / 24), steps - 1), []).append(action)

        def last_step():
            for step in range(chips):
                gather.from_corner(step)
            gather.finish()
            for k in range(late + 1):
                own_copy(k, 1).wait()
            finish_rows()
            for step in range(1, count):
                for which in range(pairs):
                    for kind in range(2):
                        far_copy(step, which, kind).wait_send()

        for moment, group in sorted(moments.items()):

            @pl.when(now == moment)
            def _(group=group):
                for action in group:
                    action()

        @pl.when(turn == 0)
        def _():
            for step in range(1, count):
                for kind in range(2):
                    far_copy(step, pair, kind).wait_recv()
            for half in range(2):
                own, spare = own_lanes(half, rows)
                zero = jnp.zeros((rows, 2 * HD), BF)
                for i in range(count):
                    at = slice(i * rows, (i + 1) * rows)
                    key = part(1) if i == 0 else far[i - 1, 0, pair]
                    value = part(2) if i == 0 else far[i - 1, 1, pair]
                    k_own[half, at, :] = jnp.where(own, key, jnp.where(spare, bias_ref[at, :], zero))
                    v_own[half, at, :] = jnp.where(own, value, jnp.where(spare, zero + 1, zero))

        at = pl.ds(pl.multiple_of(turn * block, block), block)
        lanes = pl.ds(pl.multiple_of(pair * 2 * HD, 2 * HD), 2 * HD)
        query = own_ref[at, lanes]
        results = []
        for half in range(2):
            own, spare = own_lanes(half, block)
            zero = jnp.zeros_like(query)
            query_h = jnp.where(own, query, jnp.where(spare, zero + 1, zero))
            scores = dot_nt(query_h, k_own[half])
            largest = jnp.max(scores, axis=1, keepdims=True)
            weights = jnp.exp2((scores - largest) * SCALE).astype(BF)
            summed = matmul(weights, v_own[half])
            totals = summed[:, HD * (1 - half) : HD * (1 - half) + 1]
            results.append(summed / totals)
            log_total = jnp.broadcast_to(largest * SCALE + jnp.log2(totals), (block, 2 * HD))
            l_ref[pair, half : half + 1, at] = jnp.transpose(log_total)[0:1, :]
        lane = lax.broadcasted_iota(jnp.int32, (block, 2 * HD), 1)
        o_ref[at, lanes] = jnp.where(lane < HD, results[0], results[1]).astype(BF)
        pl.when(now == steps - 1)(last_step)

    def resident(shape):
        return pl.BlockSpec(shape, lambda i, j: (0,) * len(shape))

    far_sems = pltpu.SemaphoreType.DMA((max(count - 1, 1), 2, pairs))
    return pl.pallas_call(
        kernel,
        grid=(pairs, blocks),
        in_specs=[
            resident((keys, 2 * HD)),
            resident(inputs.shape),
            HBM,
            HBM,
        ]
        + [HBM] * late,
        out_specs=[
            resident((rows, width)),
            resident((pairs, 8, rows)),
            HBM,
        ]
        + [HBM] * late,
        out_shape=[
            jax.ShapeDtypeStruct((rows, width), BF),
            jax.ShapeDtypeStruct((pairs, 8, rows), F32),
            jax.ShapeDtypeStruct(rows_in.shape, BF),
        ]
        + [jax.ShapeDtypeStruct((devices,) + shard.shape, BF) for shard in shards],
        scratch_shapes=[
            pltpu.VMEM((2, keys, 2 * HD), BF),
            pltpu.VMEM((2, keys, 2 * HD), BF),
            pltpu.VMEM((max(count - 1, 1), 2, pairs, rows, 2 * HD), BF),
            pltpu.SemaphoreType.DMA((late + 1, 2)),
        ]
        + gather_semaphores(grid, late)
        + [far_sems, far_sems]
        + [pltpu.SemaphoreType.DMA((grid.seqs,))] * 2
        + [pltpu.VMEM(shard.shape, BF) for shard in shards]
        + [pltpu.VMEM(rows_in.shape[1:], BF)],
        compiler_params=pltpu.CompilerParams(
            collective_id=1, has_side_effects=True, vmem_limit_bytes=48 << 20
        ),
        cost_estimate=pl.CostEstimate(
            flops=16 * H * rows * keys * HD, bytes_accessed=8 * rows * width, transcendentals=H * rows * keys
        ),
        name="attention",
    )(key_bias, inputs, inputs, rows_in, *shards)


def attention_back(grid, inputs, key_bias, log_totals, context, grad_context, wholes, rows_out, block=256, chunk=1024):
    rows = inputs.shape[0]
    width = inputs.shape[1] // 3
    pairs = width // (2 * HD)
    count = grid.group
    keys = rows * count
    blocks = rows // block
    steps = pairs * blocks
    chunk = min(chunk, rows)
    chunks = keys // chunk
    late = len(wholes)
    shapes = [whole.shape[2:] for whole in wholes]
    away = max(count - 1, 1)

    def kernel(q_ref, bias_ref, l_ref, o_ref, g_ref, k_ref, v_ref, all_ref, rows_ref, *refs):
        whole_refs = refs[:late]
        out_ref, back_ref = refs[late : late + 2]
        results = refs[late + 2 : 2 * late + 2]
        rest = refs[2 * late + 2 :]
        k_own, k_turned, v_all, grad_k, grad_v, far, far_out, far_in, row_hold, hold_sem = rest[:10]
        far_send, far_receive, out_send, in_receive, row_send, row_receive = rest[10:16]
        pair, turn = pl.program_id(0), pl.program_id(1)
        now = pair * blocks + turn
        place = Place(grid)
        reduce = reduce_of(place, whole_refs, results, rest[16:])
        start_rows, finish_rows = row_exchange(place, rows_ref, back_ref, row_send, row_receive)

        def far_copy(step, which, kind):
            first = pl.multiple_of(which * 2 * HD + (kind + 1) * width, 2 * HD)
            return remote(
                all_ref.at[:, pl.ds(first, 2 * HD)],
                far.at[step - 1, kind, which],
                far_send.at[step - 1, kind, which],
                far_receive.at[step - 1, kind, which],
                place.at_member(step),
            )

        def back_copy(step, which, kind):
            return remote(
                far_out.at[step - 1, kind, which],
                far_in.at[step - 1, kind, which],
                out_send.at[step - 1, kind, which],
                in_receive.at[step - 1, kind, which],
                place.at_member(count - step),
            )

        def take_back(which):
            for kind in range(2):
                first = pl.multiple_of(which * 2 * HD + (kind + 1) * width, 2 * HD)
                total = out_ref[:, pl.ds(first, 2 * HD)].astype(F32)
                for step in range(1, count):
                    back_copy(step, which, kind).wait_recv()
                    total = total + far_in[step - 1, kind, which].astype(F32)
                out_ref[:, pl.ds(first, 2 * HD)] = total.astype(BF)

        def send_back(which):
            for step in range(1, count):
                for kind in range(2):
                    back_copy(step, which, kind).start()

        def first_step():
            meet(place.neighbours() + [place.at_member(s) for s in range(1, count) if count > 2])
            start_far(0)

        def start_far(which):
            for step in range(1, count):
                for kind in range(2):
                    far_copy(step, which, kind).start()

        def more_far():
            start_rows()
            own_in.start()
            for which in range(1, pairs):
                start_far(which)

        def own_onward():
            own_in.wait()
            own_out.start()

        own_in = pltpu.make_async_copy(rows_ref.at[place.owner], row_hold, hold_sem.at[0])
        own_out = pltpu.make_async_copy(row_hold, back_ref.at[place.owner], hold_sem.at[1])
        stages = reduce.plan()
        actions = [(0, first_step), stages[0], (0, more_far), (1, own_onward)] + stages[1:]
        moments = {}
        for moment, action in actions:
            moments.setdefault(min(int(moment * steps / 24), steps - 1), []).append(action)
        for moment, group in sorted(moments.items()):

            @pl.when(now == moment)
            def _(group=group):
                for action in group:
                    action()

        @pl.when((turn == 0) & (pair > 0))
        def _():
            send_back(pair - 1)

        @pl.when(turn == 0)
        def _():
            for step in range(1, count):
                for kind in range(2):
                    far_copy(step, pair, kind).wait_recv()
            for i in range(count):
                at = slice(i * rows, (i + 1) * rows)
                v_all[at, :] = v_ref[...] if i == 0 else far[i - 1, 1, pair]
                key = k_ref[...] if i == 0 else far[i - 1, 0, pair]
                for half in range(2):
                    own, spare = own_lanes(half, rows)
                    zero = jnp.zeros_like(key)
                    k_own[half, at, :] = jnp.where(own, key, jnp.where(spare, bias_ref[at, :], zero))
                    k_turned[half, :, at] = jnp.transpose(jnp.where(own, key, zero))
            grad_k[...] = jnp.zeros_like(grad_k)
            grad_v[...] = jnp.zeros_like(grad_v)

        query, grad = q_ref[...], g_ref[...]
        turned = jnp.transpose(grad.astype(F32) * o_ref[...].astype(F32))
        asks, plain, grads, centres, logs = [], [], [], [], []
        for half in range(2):
            own, spare = own_lanes(half, block)
            zero = jnp.zeros_like(query)
            asks.append(jnp.where(own, query, jnp.where(spare, zero + 1, zero)))
            plain.append(jnp.where(own, query, zero))
            grads.append(jnp.where(own, grad, zero))
            centres.append(jnp.sum(turned[HD * half : HD * half + HD], axis=0, keepdims=True))
            logs.append(l_ref[half : half + 1, :])
        grad_q = None
        for c in range(chunks):
            span = slice(c * chunk, (c + 1) * chunk)
            weights, slopes = [], []
            for half in range(2):
                scores = dot_nt(k_own[half, span, :], asks[half])
                grad_weights = dot_nt(v_all[span, :], grads[half])
                exact = jnp.exp2(scores * SCALE - logs[half])
                slope = (exact * (grad_weights - centres[half])).astype(BF)
                weights.append(exact.astype(BF))
                slopes.append(slope)
                step = matmul(k_turned[half, :, span], slope)
                grad_q = step if grad_q is None else grad_q + step
            grad_v[span, :] += matmul(weights[0], grads[0]) + matmul(weights[1], grads[1])
            grad_k[span, :] += matmul(slopes[0], plain[0]) + matmul(slopes[1], plain[1])
        at = pl.ds(pl.multiple_of(turn * block, block), block)
        out_ref[at, pl.ds(pl.multiple_of(pair * 2 * HD, 2 * HD), 2 * HD)] = (
            jnp.transpose(grad_q) * 0.125
        ).astype(BF)

        @pl.when(turn == blocks - 1)
        def _():
            for i in range(count):
                at = slice(i * rows, (i + 1) * rows)
                for kind, value, scale in ((0, grad_k, 0.125), (1, grad_v, 1.0)):
                    low = (value[at, :] * scale).astype(BF)
                    if i == 0:
                        first = pl.multiple_of(pair * 2 * HD + (kind + 1) * width, 2 * HD)
                        out_ref[:, pl.ds(first, 2 * HD)] = low
                    else:
                        far_out[i - 1, kind, pair] = low

        @pl.when((turn == blocks - 1) & (pair > 0))
        def _():
            take_back(pair - 1)

        @pl.when(now == steps - 1)
        def _():
            send_back(pairs - 1)
            reduce.finish()
            finish_rows()
            own_out.wait()
            take_back(pairs - 1)
            for step in range(1, count):
                for which in range(pairs):
                    for kind in range(2):
                        far_copy(step, which, kind).wait_send()
                        back_copy(step, which, kind).wait_send()

    def column(first):
        return pl.BlockSpec((rows, 2 * HD), lambda i, j: (0, i + first))

    def tile():
        return pl.BlockSpec((block, 2 * HD), lambda i, j: (j, i))

    def resident(shape):
        return pl.BlockSpec(shape, lambda i, j: (0,) * len(shape))

    far_sems = pltpu.SemaphoreType.DMA((away, 2, pairs))
    far_buffer = pltpu.VMEM((away, 2, pairs, rows, 2 * HD), BF)
    return pl.pallas_call(
        kernel,
        grid=(pairs, blocks),
        in_specs=[
            tile(),
            resident((keys, 2 * HD)),
            pl.BlockSpec((None, 8, block), lambda i, j: (i, 0, j)),
            tile(),
            tile(),
            column(pairs),
            column(2 * pairs),
            HBM,
            HBM,
        ]
        + [HBM] * late,
        out_specs=[resident(inputs.shape), HBM] + [resident(tuple(shape)) for shape in shapes],
        out_shape=[jax.ShapeDtypeStruct(inputs.shape, BF), jax.ShapeDtypeStruct(rows_out.shape, BF)]
        + [jax.ShapeDtypeStruct(shape, F32) for shape in shapes],
        scratch_shapes=[
            pltpu.VMEM((2, keys, 2 * HD), BF),
            pltpu.VMEM((2, 2 * HD, keys), BF),
            pltpu.VMEM((keys, 2 * HD), BF),
            pltpu.VMEM((keys, 2 * HD), F32),
            pltpu.VMEM((keys, 2 * HD), F32),
            far_buffer,
            far_buffer,
            far_buffer,
            pltpu.VMEM(rows_out.shape[1:], BF),
            pltpu.SemaphoreType.DMA((2,)),
        ]
        + [far_sems] * 4
        + [pltpu.SemaphoreType.DMA((grid.seqs,))] * 2
        + reduce_scratch(grid, shapes),
        compiler_params=pltpu.CompilerParams(
            collective_id=2, has_side_effects=True, vmem_limit_bytes=61 << 20
        ),
        cost_estimate=pl.CostEstimate(
            flops=40 * H * rows * keys * HD, bytes_accessed=12 * rows * width, transcendentals=H * rows * keys
        ),
        name="attention_back",
    )(inputs, key_bias, log_totals, context, grad_context, inputs, inputs, inputs, rows_out, *wholes)


def body(
    tokens,
    lengths,
    query_weight,
    key_weight,
    value_weight,
    out_weight,
    up_weight,
    down_weight,
    query_bias,
    value_bias,
    out_bias,
    up_bias,
    down_bias,
    first_gain,
    first_shift,
    second_gain,
    second_shift,
    cotangent,
):
    seqs, length, width = tokens.shape
    grid = Grid(seqs)
    devices = grid.columns * grid.n
    slim = query_weight.shape[0]
    hidden = up_weight.shape[1]
    tall = hidden // devices
    wide = hidden // width

    vectors = (
        query_bias,
        value_bias,
        out_bias,
        down_bias,
        first_gain,
        first_shift,
        second_gain,
        second_shift,
    )
    vectors = vectors + (up_bias,)
    lines = -(-len(vectors) // 16) * 16
    tile = jnp.zeros((lines, 128), BF)
    for i, vector in enumerate(vectors):
        size = vector.shape[0]
        tile = tile + jnp.pad(vector[None, :], ((i, lines - 1 - i), (0, 128 - size)))
    flat_in, into_full, _, key_bias, live_rows, *whole_vectors = start_exchange(
        grid,
        tokens,
        (query_weight, key_weight, value_weight),
        tile,
        lengths,
        tuple(vector.shape[0] for vector in vectors),
    )
    flat_in = flat_in.reshape(-1, width)
    into_full = into_full.reshape(width, 3 * width)
    query_add, value_add, out_add, down_add, gain_one, shift_one, gain_two, shift_two, up_add = whole_vectors

    into_add = jnp.concatenate([query_add, jnp.zeros_like(query_add), value_add], axis=1)
    inputs = (matmul(flat_in, into_full) + into_add).astype(BF)
    context, log_totals, grad_in, out_full, up_full, down_full = attention(
        grid, inputs, key_bias, (out_weight, up_weight, down_weight), cotangent
    )
    out_full = out_full.reshape(width, width)
    up_full = up_full.reshape(width, hidden)
    down_full = down_full.reshape(hidden, width)
    grad_in = grad_in.reshape(-1, width)

    first_sum = flat_in.astype(F32) + matmul(context, out_full) + out_add
    first_norm, first_unit, first_factor = normalize(first_sum, gain_one, shift_one)
    first_low = first_norm.astype(BF)
    up_pre = matmul(first_low, up_full) + up_add
    below = 0.5 * (1.0 + lax.erf(up_pre * ROOT_HALF))
    slope = (below + up_pre * INV_ROOT_TWO_PI * jnp.exp(-0.5 * up_pre * up_pre)).astype(BF)
    activated, slope = lax.optimization_barrier(((up_pre * below).astype(BF), slope))
    second_sum = first_low.astype(F32) + matmul(activated, down_full) + down_add
    second_norm, second_unit, second_factor = normalize(second_sum, gain_two, shift_two)
    output = (second_norm * live_rows).astype(BF).reshape(seqs, length, width)

    grad_output = grad_in.astype(F32) * live_rows
    grad_gain_two = jnp.sum(grad_output * second_unit, axis=0)
    grad_shift_two = jnp.sum(grad_output, axis=0)
    grad_second = norm_back(grad_output, second_unit, second_factor, gain_two)
    grad_branch = grad_second.astype(BF)
    grad_down_add = jnp.sum(grad_branch.astype(F32), axis=0)
    grad_down = left_product(activated, grad_branch).astype(BF)
    grad_up_low = (right_product(grad_branch, down_full) * slope.astype(F32)).astype(BF)
    grad_up_add = jnp.sum(grad_up_low.astype(F32), axis=0)
    grad_up = left_product(first_low, grad_up_low).astype(BF)
    grad_first = right_product(grad_up_low, up_full) + grad_second
    grad_gain_one = jnp.sum(grad_first * first_unit, axis=0)
    grad_shift_one = jnp.sum(grad_first, axis=0)
    grad_residual = norm_back(grad_first, first_unit, first_factor, gain_one)
    grad_attend = grad_residual.astype(BF)
    grad_out_add = jnp.sum(grad_attend.astype(F32), axis=0)
    grad_out = left_product(context, grad_attend).astype(BF)
    grad_context = right_product(grad_attend, out_full).astype(BF)

    def pack(grads, more=()):
        count = len(grads)
        table = jnp.stack(grads).reshape(count, devices, slim).transpose(1, 0, 2)
        table = jnp.concatenate([table.reshape(devices, count * slim), *more], axis=1).astype(BF)
        size = table.shape[1]
        table = jnp.pad(table, ((0, 0), (0, -size % 128)))
        return jnp.broadcast_to(table[:, None, :], (devices, 8, table.shape[1])).reshape(devices * 8, -1)

    middle = pack(
        [grad_out_add, grad_down_add, grad_gain_one, grad_shift_one, grad_gain_two, grad_shift_two],
        (grad_up_add.reshape(devices, tall),),
    )
    wholes = [
        by_place(grid, grad_up, slim),
        by_place(grid, grad_down, tall),
        by_place(grid, grad_out, slim),
        by_place(grid, middle, 8),
    ]
    low, output, grad_up_own, grad_down_own, grad_out_own, middle_own = attention_back(
        grid, inputs, key_bias, log_totals, context, grad_context, wholes, output
    )
    query_adds = jnp.sum(low[:, :width].astype(F32), axis=0)
    value_adds = jnp.sum(low[:, 2 * width :].astype(F32), axis=0)
    tokens_grad = right_product(low, into_full) + grad_residual
    wholes = [
        by_place(grid, left_product(flat_in, low).astype(BF), slim),
        by_place(grid, pack([query_adds, value_adds]), 8),
    ]
    tokens_grad = tokens_grad.astype(BF).reshape(seqs, length, width)
    tokens_grad, grad_into_own, last_own = end_exchange(grid, tokens_grad, wholes)
    tokens_grad = tokens_grad.astype(F32)
    middle_own, last_own = middle_own[0], last_own[0]
    vector_outs = [last_own[:slim], last_own[slim : 2 * slim]]
    vector_outs = vector_outs + [middle_own[i * slim : (i + 1) * slim] for i in range(6)]
    up_add_own = middle_own[6 * slim : 6 * slim + tall]
    matrix_outs = [grad_into_own[:, i * width : (i + 1) * width] for i in range(3)]
    return (
        output,
        tokens_grad,
        matrix_outs[0],
        matrix_outs[1],
        matrix_outs[2],
        grad_out_own,
        grad_up_own,
        grad_down_own,
        vector_outs[0],
        vector_outs[1],
        vector_outs[2],
        up_add_own,
        vector_outs[3],
        vector_outs[4],
        vector_outs[5],
        vector_outs[6],
        vector_outs[7],
    )


def solution(mesh):
    whole = ("dp", "seq")
    matrix, vector, rows = P(whole, None), P(whole), P("dp", "seq", None)
    return jax.shard_map(
        body,
        mesh=mesh,
        in_specs=(rows, P("dp")) + (matrix,) * 6 + (vector,) * 9 + (rows,),
        out_specs=(rows, rows) + (matrix,) * 6 + (vector,) * 9,
        check_vma=False,
    )
```

```python
import jax
import jax.numpy as jnp
from jax import lax
from jax.experimental import pallas as pl
from jax.experimental.pallas import tpu as pltpu
from jax.sharding import PartitionSpec as P

H = 12
HD = 64

EPSILON = 1e-05
ROOT_HALF = 0.7071067811865476
INV_ROOT_TWO_PI = 0.3989422804014327
BF = jnp.bfloat16
F32 = jnp.float32


def matmul(left, right):
    return jnp.dot(left, right, preferred_element_type=F32)


def left_product(left, right):
    return lax.dot_general(left, right, (((0,), (0,)), ((), ())), preferred_element_type=F32)


def right_product(left, right):
    return lax.dot_general(left, right, (((1,), (1,)), ((), ())), preferred_element_type=F32)


def normalize(inputs, gains, shifts):
    centre = inputs - jnp.mean(inputs, axis=-1, keepdims=True)
    factor = lax.rsqrt(jnp.mean(centre * centre, axis=-1, keepdims=True) + EPSILON)
    unit_rows = centre * factor
    return (unit_rows * gains + shifts, unit_rows, factor)


def norm_back(grad_in, unit_rows, factor, gains):
    grad_unit = grad_in * gains
    return factor * (
        grad_unit
        - jnp.mean(grad_unit, axis=-1, keepdims=True)
        - unit_rows * jnp.mean(grad_unit * unit_rows, axis=-1, keepdims=True)
    )


class Grid:
    def __init__(self, seqs):
        self.columns = lax.axis_size("dp")
        self.n = lax.axis_size("seq")
        self.seqs = seqs
        self.group = self.n // seqs
        self.chips = self.n // 2
        self.column = lax.axis_index("dp")
        place = lax.axis_index("seq")
        self.chip = place // 2
        self.core = place % 2
        self.owner = place // self.group
        self.member = place % self.group


MESH = pl.DeviceIdType.MESH
HBM = pl.BlockSpec(memory_space=pl.ANY)


def remote(source, target, send, receive, device):
    return pltpu.make_async_remote_copy(
        src_ref=source, dst_ref=target, send_sem=send, recv_sem=receive, device_id=device, device_id_type=MESH
    )


def meet(devices):
    barrier = pltpu.get_barrier_semaphore()
    for device in devices:
        pl.semaphore_signal(barrier, inc=1, device_id=device, device_id_type=MESH)
    pl.semaphore_wait(barrier, len(devices))


class Place:
    def __init__(self, grid):
        self.columns, self.chips, self.n = grid.columns, grid.chips, grid.n
        self.seqs, self.group = grid.seqs, grid.group
        self.column = lax.axis_index("dp")
        self.spot = lax.axis_index("seq")
        self.chip = lax.div(self.spot, 2)
        self.core = lax.rem(self.spot, 2)
        self.owner = lax.div(self.spot, self.group)
        self.member = lax.rem(self.spot, self.group)

    def near(self, chip_step):
        return (self.column, (self.chip ^ chip_step) * 2 + self.core)

    def beside(self, column_step):
        return (self.column ^ column_step, self.spot)

    def twin(self):
        return (self.column, self.chip * 2 + (1 - self.core))

    def at_owner(self, step):
        return (self.column, (self.owner ^ step) * self.group + self.member)

    def at_member(self, step):
        return (self.column, self.owner * self.group + lax.rem(self.member + step, self.group))

    def index(self, column_step, chip_step, other=False):
        core = 1 - self.core if other else self.core
        return ((self.column ^ column_step) * self.chips + (self.chip ^ chip_step)) * 2 + core

    def neighbours(self):
        chips = [self.near(step) for step in range(1, self.chips)]
        columns = [self.beside(step) for step in range(1, self.columns)]
        return chips + columns + [self.twin()]


class Gather:
    def __init__(self, place, arrays, send, receive):
        self.place, self.arrays, self.send, self.receive = place, arrays, send, receive
        self.square = place.columns == 4
        self.sent = []

    def copies(self, kind, column_step, chip_step, device, own=False, where=None):
        slot = column_step * self.place.chips + chip_step
        for k, (shard, whole, block) in enumerate(self.arrays):
            held = block(whole, self.place.index(*(where or (column_step, chip_step))))
            yield remote(
                shard if own else held, held, self.send.at[k, kind, slot], self.receive.at[k, kind, slot], device
            )

    def begin(self, kind, column_step, chip_step, device, own=False, where=None):
        self.sent.append((kind, column_step, chip_step, own, where))
        for copy in self.copies(kind, column_step, chip_step, device, own, where):
            copy.start()

    def to_twin(self, column_step, chip_step, own=False):
        self.begin(1, column_step, chip_step, self.place.twin(), own=own)

    def outward(self, chip_step):
        place, own = self.place, chip_step == 0
        for step in range(1, place.columns):
            if not (self.square and step == 3):
                self.begin(0, step, chip_step, place.beside(step), own=own, where=(0, chip_step))
        self.to_twin(0, chip_step, own=own)

    def to_chip(self, step):
        self.begin(0, 0, step, self.place.near(step), own=True, where=(0, 0))

    def start(self):
        for step in range(1, self.place.chips):
            self.to_chip(step)
        self.outward(0)

    def arrive(self, column_step, chip_step, other=False):
        for k, (_, whole, block) in enumerate(self.arrays):
            held = block(whole, self.place.index(column_step, chip_step, other))
            kind = 1 if other else 0
            slot = column_step * self.place.chips + chip_step
            remote(
                held, held, self.send.at[k, kind, slot], self.receive.at[k, kind, slot], self.place.twin()
            ).wait_recv()

    def from_chip(self, chip_step):
        self.arrive(0, chip_step)
        self.outward(chip_step)

    def from_columns(self, chip_step):
        for step in range(1, self.place.columns):
            if self.square and step == 3:
                continue
            self.arrive(step, chip_step)
            if self.square and step == 1 + chip_step % 2:
                self.begin(0, 3, chip_step, self.place.beside(3 - step), where=(step, chip_step))
            self.to_twin(step, chip_step)

    def from_corner(self, chip_step):
        if self.square:
            self.arrive(3, chip_step)
            self.to_twin(3, chip_step)

    def finish(self):
        place = self.place
        for column_step in range(place.columns):
            for chip_step in range(place.chips):
                self.arrive(column_step, chip_step, other=True)
        for kind, column_step, chip_step, own, where in self.sent:
            for copy in self.copies(kind, column_step, chip_step, place.twin(), own, where):
                copy.wait_send()


def gather_semaphores(grid, count):
    shape = (count, 2, grid.columns * grid.chips)
    return [pltpu.SemaphoreType.DMA(shape), pltpu.SemaphoreType.DMA(shape)]


def through(source, held, target, sem):
    copy = pltpu.make_async_copy(source, held, sem)
    copy.start()
    copy.wait()
    copy = pltpu.make_async_copy(held, target, sem)
    copy.start()
    copy.wait()


def start_exchange(grid, tokens, into, vectors, lengths, vector_widths):
    seqs, length, width = tokens.shape
    devices = grid.columns * grid.n
    slim = into[0].shape[0]
    parts = len(into)
    rows = seqs * length
    tile = vectors.shape

    def spread(table, size):
        lane = lax.broadcasted_iota(jnp.int32, (128, devices * size), 1).astype(F32)
        row = lax.broadcasted_iota(jnp.int32, (128, devices * size), 0).astype(F32)
        within = lane - size * jnp.floor((lane + 0.5) * (1.0 / size))
        return matmul(table, (row == within).astype(BF))

    def own_block(count, size):
        lane = lax.broadcasted_iota(jnp.int32, (count, devices * size), 1).astype(F32)
        return jnp.floor((lane + 0.5) * (1.0 / size))

    def kernel(tokens_ref, query_ref, key_ref, value_ref, vectors_ref, lengths_ref, rows_ref, into_all, vectors_all, *rest):
        into_refs = (query_ref, key_ref, value_ref)
        bias_ref, live_ref = rest[:2]
        vector_refs = rest[2 : 2 + len(vector_widths)]
        scratch = rest[2 + len(vector_widths) :]
        row_hold, into_hold, vector_hold, table_hold, hold_sem, send, receive, row_send, row_receive = scratch
        place = Place(grid)
        meet(place.neighbours())

        def part(k):
            return lambda ref, i: ref.at[i, :, pl.ds(k * width, width)]

        gather = Gather(
            place,
            [(into_refs[k], into_all, part(k)) for k in range(parts)]
            + [(vectors_ref, vectors_all, lambda ref, i: ref.at[i])],
            send,
            receive,
        )
        gather.start()

        def row_copy(step):
            return remote(
                tokens_ref.at[place.owner ^ step],
                rows_ref.at[place.owner],
                row_send.at[step],
                row_receive.at[step],
                place.at_owner(step),
            )

        for step in range(1, seqs):
            row_copy(step).start()
        me = place.index(0, 0)
        for k in range(parts):
            through(into_refs[k], into_hold, part(k)(into_all, me), hold_sem)
        through(vectors_ref, vector_hold, vectors_all.at[me], hold_sem)
        through(tokens_ref.at[place.owner], row_hold, rows_ref.at[place.owner], hold_sem)

        my_length = lengths_ref[place.owner]
        for step in range(place.group):
            member = lax.rem(place.member - step + place.group, place.group)
            for source in range(seqs):
                first = (source * place.group + member) * length
                at = slice(step * rows + source * length, step * rows + (source + 1) * length)
                here = lax.broadcasted_iota(jnp.int32, (length, 2 * HD), 0) + first
                bias_ref[at, :] = jnp.where(here < my_length, 0.0, -1e30).astype(BF)
                if step == 0:
                    here = lax.broadcasted_iota(jnp.int32, (length, 1), 0) + first
                    live_ref[at, :] = jnp.where(here < my_length, 1.0, 0.0).astype(F32)

        for step in range(1, place.chips):
            gather.from_chip(step)
            gather.from_columns(step - 1)
        gather.from_columns(place.chips - 1)
        for step in range(place.chips):
            gather.from_corner(step)
        gather.finish()
        copy = pltpu.make_async_copy(vectors_all, table_hold, hold_sem)
        copy.start()
        copy.wait()
        table = table_hold[...].astype(F32)
        kind = lax.broadcasted_iota(jnp.int32, table.shape, 1)
        source = lax.broadcasted_iota(jnp.int32, (devices, 1), 0).astype(F32)
        for k, size in enumerate(vector_widths):
            own = jnp.sum(jnp.where(kind == k, table, 0.0), axis=1).astype(BF)
            apart = jnp.where(own_block(devices, size) == source, spread(own, size), 0.0)
            vector_refs[k][...] = jnp.sum(apart, axis=0, keepdims=True)
        for step in range(1, seqs):
            landed = rows_ref.at[place.owner ^ step]
            remote(
                landed, landed, row_send.at[step], row_receive.at[step], place.at_owner(step)
            ).wait_recv()
            row_copy(step).wait_send()

    vmem = pl.BlockSpec(memory_space=pltpu.VMEM)
    shapes = [tokens.shape, (devices, slim, parts * width), (devices,) + tile]
    return pl.pallas_call(
        kernel,
        in_specs=[HBM] * (parts + 2) + [pl.BlockSpec(memory_space=pltpu.SMEM)],
        out_specs=[HBM] * 3 + [vmem] * (2 + len(vector_widths)),
        out_shape=[jax.ShapeDtypeStruct(shape, BF) for shape in shapes]
        + [jax.ShapeDtypeStruct((grid.group * rows, 2 * HD), BF), jax.ShapeDtypeStruct((rows, 1), F32)]
        + [jax.ShapeDtypeStruct((1, devices * size), F32) for size in vector_widths],
        scratch_shapes=[
            pltpu.VMEM(tokens.shape[1:], BF),
            pltpu.VMEM(into[0].shape, BF),
            pltpu.VMEM(tile, BF),
            pltpu.VMEM((devices,) + tile, BF),
            pltpu.SemaphoreType.DMA(()),
        ]
        + gather_semaphores(grid, parts + 1)
        + [pltpu.SemaphoreType.DMA((seqs,)), pltpu.SemaphoreType.DMA((seqs,))],
        compiler_params=pltpu.CompilerParams(collective_id=0, has_side_effects=True),
        name="start_exchange",
    )(tokens, *into, vectors, lengths)


class Reduce:
    def __init__(self, place, arrays, buffers, semaphores):
        self.place, self.arrays = place, arrays
        self.halves, self.twins, self.sides, self.deeps = buffers
        self.load, self.twin_sems, self.side_sems, self.deep_sems = semaphores
        self.square = place.columns == 4
        self.every = range(len(arrays))
        self.sent = []

    def spot(self, column_step, chip_step):
        return (self.place.column ^ column_step) * self.place.chips + (self.place.chip ^ chip_step)

    def strip(self, column_step):
        return pl.ds((self.place.column ^ column_step) * self.place.chips, self.place.chips)

    def load_copy(self, k, step):
        whole = self.arrays[k][0].at[self.strip(step), self.place.core]
        return pltpu.make_async_copy(whole, self.halves[k].at[self.strip(step)], self.load.at[k, step])

    def twin_copy(self, k, step):
        place = self.place
        whole = self.arrays[k][0].at[self.strip(step), 1 - place.core]
        return remote(
            whole,
            self.twins[k].at[self.strip(step)],
            self.twin_sems[0].at[k, step],
            self.twin_sems[1].at[k, step],
            place.twin(),
        )

    def side_copy(self, k, column_step, chip_step, device):
        return remote(
            self.halves[k].at[self.spot(column_step, chip_step)],
            self.sides[k].at[column_step, chip_step],
            self.side_sems[0].at[k, column_step, chip_step],
            self.side_sems[1].at[k, column_step, chip_step],
            device,
        )

    def deep_copy(self, k, chip_step):
        return remote(
            self.halves[k].at[self.spot(0, chip_step)],
            self.deeps[k].at[chip_step],
            self.deep_sems[0].at[k, chip_step],
            self.deep_sems[1].at[k, chip_step],
            self.place.near(chip_step),
        )

    def start(self):
        order = range(self.place.columns - 1, -1, -1)
        for step in order:
            for k in self.every:
                self.twin_copy(k, step).start()
                self.load_copy(k, step).start()

    def fold(self, step):
        for k in self.every:
            self.load_copy(k, step).wait()
            self.twin_copy(k, step).wait_recv()
            half, twin = self.halves[k], self.twins[k]
            for chip_step in range(self.place.chips):
                spot = self.spot(step, chip_step)
                half[spot] = half[spot] + twin[spot]

    def corner(self, chip_step):
        self.sent.append((3, chip_step))
        for k in self.every:
            self.side_copy(k, 3, chip_step, self.place.beside(1 + chip_step % 2)).start()

    def side(self, column_step, chip_step):
        self.sent.append((column_step, chip_step))
        for k in self.every:
            self.side_copy(k, column_step, chip_step, self.place.beside(column_step)).start()

    def combine(self, chip_step):
        for k in self.every:
            self.side_copy(k, 3, chip_step, self.place.twin()).wait_recv()
            spot = self.spot(2 - chip_step % 2, chip_step)
            half = self.halves[k]
            half[spot] = half[spot] + self.sides[k][3, chip_step]

    def merge(self, chip_step):
        last = 3 if self.square else self.place.columns
        for k in self.every:
            spot = self.spot(0, chip_step)
            total = self.halves[k][spot].astype(F32)
            for step in range(1, last):
                self.side_copy(k, step, chip_step, self.place.twin()).wait_recv()
                total = total + self.sides[k][step, chip_step].astype(F32)
            self.halves[k][spot] = total.astype(BF)

    def deep(self, chip_step):
        for k in self.every:
            self.deep_copy(k, chip_step).start()

    def finish(self):
        place = self.place
        for k in self.every:
            total = self.halves[k][self.spot(0, 0)].astype(F32)
            for step in range(1, place.chips):
                self.deep_copy(k, step).wait_recv()
                total = total + self.deeps[k][step].astype(F32)
            self.arrays[k][1][...] = total
            for step in range(1, place.chips):
                self.deep_copy(k, step).wait_send()
            for step in range(place.columns):
                self.twin_copy(k, step).wait_send()
            for column_step, chip_step in self.sent:
                self.side_copy(k, column_step, chip_step, place.twin()).wait_send()

    def plan(self):
        chips, columns = self.place.chips, self.place.columns
        stages = [(0, self.start)]
        if not self.square:
            for step in range(columns):
                stages.append((1, lambda step=step: self.fold(step)))
            for step in range(1, columns):
                for chip_step in range(chips):
                    stages.append((3, lambda a=step, b=chip_step: self.side(a, b)))
            for chip_step in range(chips):
                stages.append((16, lambda b=chip_step: self.merge(b)))
            for chip_step in range(1, chips):
                stages.append((17, lambda b=chip_step: self.deep(b)))
            return stages
        odd = list(range(1, chips, 2))
        even = list(range(2, chips, 2))
        first = [("corner", b) for b in even] + [(1, b) for b in even] + [(1, b) for b in odd] + [("corner", 0), (1, 0)]
        second = [("corner", b) for b in odd] + [(2, b) for b in odd] + [(2, b) for b in even] + [(2, 0)]
        slots = max(len(first), len(second))
        pace = 14.4 / slots
        mixed = [("fold", 3, 1.9), ("fold", 1, 3.9), ("fold", 2, 3.9), ("fold", 0, 6)]
        corners, last_side = {}, {}
        for link, orders in ((1, first), (2, second)):
            for i, (kind, b) in enumerate(orders):
                if kind == "corner":
                    corners[b] = 2 + pace * i
                    mixed.append(("corner", b, corners[b]))
        for link, orders in ((1, first), (2, second)):
            for i, (kind, b) in enumerate(orders):
                if kind == "corner":
                    continue
                moment = 2 + pace * i
                if link == 2 - b % 2:
                    moment = max(moment, corners[b] + pace + 1.6)
                    mixed.append(("combine", b, moment - 1))
                mixed.append((("side", link), b, moment))
                last_side[b] = max(last_side.get(b, 0), moment)
        for b, moment in last_side.items():
            mixed.append(("merge", b, moment + pace + 0.6))
            if b:
                mixed.append(("deep", b, moment + pace + 1.6))
        mixed.sort(key=lambda item: item[2])
        for kind, b, moment in mixed:
            if isinstance(kind, tuple):
                stages.append((moment, lambda a=kind[1], b=b: self.side(a, b)))
            else:
                stages.append((moment, lambda kind=kind, b=b: getattr(self, kind)(b)))
        return stages


def reduce_scratch(grid, shapes):
    columns, chips, count = grid.columns, grid.chips, len(shapes)
    buffers = []
    for lead in ((columns * chips,), (columns * chips,), (columns, chips), (chips,)):
        buffers = buffers + [pltpu.VMEM(lead + tuple(shape), BF) for shape in shapes]
    dma = pltpu.SemaphoreType.DMA
    sems = [dma((count, columns))] * 3 + [dma((count, columns, chips))] * 2 + [dma((count, chips))] * 2
    return buffers + sems


def reduce_of(place, wholes, results, scratch):
    count = len(wholes)
    groups = [scratch[i * count : (i + 1) * count] for i in range(4)]
    sems = scratch[4 * count : 4 * count + 7]
    return Reduce(
        place, list(zip(wholes, results)), groups, (sems[0], sems[1:3], sems[3:5], sems[5:7])
    )


def by_place(grid, array_in, rows):
    return array_in.reshape(grid.columns * grid.chips, 2, rows, -1)


def row_exchange(place, source, target, send, receive):
    def copy(step):
        return remote(
            source.at[place.owner ^ step],
            target.at[place.owner],
            send.at[step],
            receive.at[step],
            place.at_owner(step),
        )

    def finish():
        for step in range(1, place.seqs):
            landed = target.at[place.owner ^ step]
            remote(landed, landed, send.at[step], receive.at[step], place.at_owner(step)).wait_recv()
            copy(step).wait_send()

    def start():
        for step in range(1, place.seqs):
            copy(step).start()

    return start, finish


def end_exchange(grid, rows, wholes):
    shapes = [whole.shape[2:] for whole in wholes]
    count = len(wholes)

    def kernel(rows_ref, *refs):
        whole_refs, back_ref, results = refs[:count], refs[count], refs[count + 1 : 2 * count + 1]
        row_hold, hold_sem, row_send, row_receive = refs[2 * count + 1 : 2 * count + 5]
        place = Place(grid)
        meet(place.neighbours())
        reduce = reduce_of(place, whole_refs, results, refs[2 * count + 5 :])
        start_rows, finish_rows = row_exchange(place, rows_ref, back_ref, row_send, row_receive)
        stages = reduce.plan()
        stages[0][1]()
        start_rows()
        through(rows_ref.at[place.owner], row_hold, back_ref.at[place.owner], hold_sem)
        for _, action in stages[1:]:
            action()
        reduce.finish()
        finish_rows()

    return pl.pallas_call(
        kernel,
        in_specs=[HBM] * (count + 1),
        out_specs=[HBM] + [pl.BlockSpec(memory_space=pltpu.VMEM)] * count,
        out_shape=[jax.ShapeDtypeStruct(rows.shape, BF)]
        + [jax.ShapeDtypeStruct(shape, F32) for shape in shapes],
        scratch_shapes=[
            pltpu.VMEM(rows.shape[1:], BF),
            pltpu.SemaphoreType.DMA(()),
            pltpu.SemaphoreType.DMA((grid.seqs,)),
            pltpu.SemaphoreType.DMA((grid.seqs,)),
        ]
        + reduce_scratch(grid, shapes),
        compiler_params=pltpu.CompilerParams(
            collective_id=3, has_side_effects=True, vmem_limit_bytes=40 << 20
        ),
        name="end_exchange",
    )(rows, *wholes)


LOG2E = 1.4426950408889634
SCALE = 0.125 * LOG2E


def dot_nt(left, right):
    return lax.dot_general(left, right, (((1,), (1,)), ((), ())), preferred_element_type=F32)


def own_lanes(half, count):
    lane = lax.broadcasted_iota(jnp.int32, (count, 2 * HD), 1)
    return (lane // HD) == half, lane == HD * (1 - half)


def attention(grid, inputs, key_bias, shards, rows_in, block=256):
    rows = inputs.shape[0]
    width = inputs.shape[1] // 3
    pairs = width // (2 * HD)
    count = grid.group
    keys = rows * count
    blocks = rows // block
    steps = pairs * blocks
    devices = grid.columns * grid.n
    late = len(shards)

    def kernel(bias_ref, own_ref, all_ref, rows_ref, *refs):
        shard_refs = refs[:late]
        o_ref, l_ref, block_ref = refs[late : late + 3]
        whole_refs = refs[late + 3 : 2 * late + 3]
        rest = refs[2 * late + 3 :]
        k_own, v_own, far, hold_sem, send, receive, far_send, far_receive, row_send, row_receive = rest[:10]
        holds = rest[10:]
        pair, turn = pl.program_id(0), pl.program_id(1)
        now = pair * blocks + turn
        place = Place(grid)
        gather = Gather(
            place,
            [(s, w, lambda ref, i: ref.at[i]) for s, w in zip(shard_refs, whole_refs)],
            send,
            receive,
        )

        def part(kind):
            return own_ref[:, pl.ds(pl.multiple_of(kind * width + pair * 2 * HD, 2 * HD), 2 * HD)]

        def far_copy(step, which, kind):
            first = pl.multiple_of(which * 2 * HD + (kind + 1) * width, 2 * HD)
            return remote(
                all_ref.at[:, pl.ds(first, 2 * HD)],
                far.at[step - 1, kind, which],
                far_send.at[step - 1, kind, which],
                far_receive.at[step - 1, kind, which],
                place.at_member(step),
            )

        def first_step():
            meet(place.neighbours() + [place.at_member(s) for s in range(1, count) if count > 2])
            start_far(0)
            gather.start()
            for k in range(late + 1):
                own_copy(k, 0).start()
            for which in range(1, pairs):
                start_far(which)

        def start_far(which):
            for step in range(1, count):
                for kind in range(2):
                    far_copy(step, which, kind).start()

        start_rows, finish_rows = row_exchange(place, rows_ref, block_ref, row_send, row_receive)

        def own_copy(k, way):
            if k == late:
                source, target = rows_ref.at[place.owner], block_ref.at[place.owner]
            else:
                source, target = shard_refs[k], whole_refs[k].at[place.index(0, 0)]
            if way == 0:
                return pltpu.make_async_copy(source, holds[k], hold_sem.at[k, 0])
            return pltpu.make_async_copy(holds[k], target, hold_sem.at[k, 1])

        def own_onward():
            for k in range(late + 1):
                own_copy(k, 0).wait()
                own_copy(k, 1).start()

        chips = place.chips
        pace = 8 / max(chips - 2, 1)
        plan = [(0, first_step), (1, own_onward), (8, lambda: gather.from_chip(1)), (8, lambda: gather.from_columns(0))]
        plan.append((10, start_rows))
        for step in range(2, chips):
            moment = 12 + pace * (step - 2)
            plan.append((moment - 0.01 * (step > 2), lambda step=step: gather.from_chip(step)))
            plan.append((moment, lambda step=step: gather.from_columns(step - 1)))
        plan.append((20, lambda: gather.from_columns(chips - 1)))
        moments = {}
        for moment, action in plan:
            moments.setdefault(min(int(moment * steps / 24), steps - 1), []).append(action)

        def last_step():
            for step in range(chips):
                gather.from_corner(step)
            gather.finish()
            for k in range(late + 1):
                own_copy(k, 1).wait()
            finish_rows()
            for step in range(1, count):
                for which in range(pairs):
                    for kind in range(2):
                        far_copy(step, which, kind).wait_send()

        for moment, group in sorted(moments.items()):

            @pl.when(now == moment)
            def _(group=group):
                for action in group:
                    action()

        @pl.when(turn == 0)
        def _():
            for step in range(1, count):
                for kind in range(2):
                    far_copy(step, pair, kind).wait_recv()
            for half in range(2):
                own, spare = own_lanes(half, rows)
                zero = jnp.zeros((rows, 2 * HD), BF)
                for i in range(count):
                    at = slice(i * rows, (i + 1) * rows)
                    key = part(1) if i == 0 else far[i - 1, 0, pair]
                    value = part(2) if i == 0 else far[i - 1, 1, pair]
                    k_own[half, at, :] = jnp.where(own, key, jnp.where(spare, bias_ref[at, :], zero))
                    v_own[half, at, :] = jnp.where(own, value, jnp.where(spare, zero + 1, zero))

        at = pl.ds(pl.multiple_of(turn * block, block), block)
        lanes = pl.ds(pl.multiple_of(pair * 2 * HD, 2 * HD), 2 * HD)
        query = own_ref[at, lanes]
        results = []
        for half in range(2):
            own, spare = own_lanes(half, block)
            zero = jnp.zeros_like(query)
            query_h = jnp.where(own, query, jnp.where(spare, zero + 1, zero))
            scores = dot_nt(query_h, k_own[half])
            largest = jnp.max(scores, axis=1, keepdims=True)
            weights = jnp.exp2((scores - largest) * SCALE).astype(BF)
            summed = matmul(weights, v_own[half])
            totals = summed[:, HD * (1 - half) : HD * (1 - half) + 1]
            results.append(summed / totals)
            log_total = jnp.broadcast_to(largest * SCALE + jnp.log2(totals), (block, 2 * HD))
            l_ref[pair, half : half + 1, at] = jnp.transpose(log_total)[0:1, :]
        lane = lax.broadcasted_iota(jnp.int32, (block, 2 * HD), 1)
        o_ref[at, lanes] = jnp.where(lane < HD, results[0], results[1]).astype(BF)
        pl.when(now == steps - 1)(last_step)

    def resident(shape):
        return pl.BlockSpec(shape, lambda i, j: (0,) * len(shape))

    far_sems = pltpu.SemaphoreType.DMA((max(count - 1, 1), 2, pairs))
    return pl.pallas_call(
        kernel,
        grid=(pairs, blocks),
        in_specs=[
            resident((keys, 2 * HD)),
            resident(inputs.shape),
            HBM,
            HBM,
        ]
        + [HBM] * late,
        out_specs=[
            resident((rows, width)),
            resident((pairs, 8, rows)),
            HBM,
        ]
        + [HBM] * late,
        out_shape=[
            jax.ShapeDtypeStruct((rows, width), BF),
            jax.ShapeDtypeStruct((pairs, 8, rows), F32),
            jax.ShapeDtypeStruct(rows_in.shape, BF),
        ]
        + [jax.ShapeDtypeStruct((devices,) + shard.shape, BF) for shard in shards],
        scratch_shapes=[
            pltpu.VMEM((2, keys, 2 * HD), BF),
            pltpu.VMEM((2, keys, 2 * HD), BF),
            pltpu.VMEM((max(count - 1, 1), 2, pairs, rows, 2 * HD), BF),
            pltpu.SemaphoreType.DMA((late + 1, 2)),
        ]
        + gather_semaphores(grid, late)
        + [far_sems, far_sems]
        + [pltpu.SemaphoreType.DMA((grid.seqs,))] * 2
        + [pltpu.VMEM(shard.shape, BF) for shard in shards]
        + [pltpu.VMEM(rows_in.shape[1:], BF)],
        compiler_params=pltpu.CompilerParams(
            collective_id=1, has_side_effects=True, vmem_limit_bytes=48 << 20
        ),
        cost_estimate=pl.CostEstimate(
            flops=16 * H * rows * keys * HD, bytes_accessed=8 * rows * width, transcendentals=H * rows * keys
        ),
        name="attention",
    )(key_bias, inputs, inputs, rows_in, *shards)


def attention_back(grid, inputs, key_bias, log_totals, context, grad_context, wholes, rows_out, block=1024, chunk=512):
    rows = inputs.shape[0]
    width = inputs.shape[1] // 3
    pairs = width // (2 * HD)
    count = grid.group
    keys = rows * count
    block, chunk = min(block, rows), min(chunk, rows)
    blocks, chunks = rows // block, keys // chunk
    steps = pairs * blocks * chunks
    late = len(wholes)
    shapes = [whole.shape[2:] for whole in wholes]
    away = max(count - 1, 1)

    def kernel(q_ref, bias_ref, l_ref, o_ref, g_ref, k_ref, v_ref, all_ref, rows_ref, *refs):
        whole_refs = refs[:late]
        out_ref, back_ref = refs[late : late + 2]
        results = refs[late + 2 : 2 * late + 2]
        rest = refs[2 * late + 2 :]
        k_own, k_turned, v_all, grad_k, grad_v, grad_q, far, far_out, far_in, row_hold, hold_sem = rest[:11]
        far_send, far_receive, out_send, in_receive, row_send, row_receive = rest[11:17]
        pair, turn = pl.program_id(0), pl.program_id(1)
        now = pair * blocks + turn
        place = Place(grid)
        reduce = reduce_of(place, whole_refs, results, rest[17:])
        start_rows, finish_rows = row_exchange(place, rows_ref, back_ref, row_send, row_receive)

        def far_copy(step, which, kind):
            first = pl.multiple_of(which * 2 * HD + (kind + 1) * width, 2 * HD)
            return remote(
                all_ref.at[:, pl.ds(first, 2 * HD)],
                far.at[step - 1, kind, which],
                far_send.at[step - 1, kind, which],
                far_receive.at[step - 1, kind, which],
                place.at_member(step),
            )

        def back_copy(step, which, kind):
            return remote(
                far_out.at[step - 1, kind, which],
                far_in.at[step - 1, kind, which],
                out_send.at[step - 1, kind, which],
                in_receive.at[step - 1, kind, which],
                place.at_member(count - step),
            )

        def take_back(which):
            for kind in range(2):
                first = pl.multiple_of(which * 2 * HD + (kind + 1) * width, 2 * HD)
                total = out_ref[:, pl.ds(first, 2 * HD)].astype(F32)
                for step in range(1, count):
                    back_copy(step, which, kind).wait_recv()
                    total = total + far_in[step - 1, kind, which].astype(F32)
                out_ref[:, pl.ds(first, 2 * HD)] = total.astype(BF)

        def send_back(which):
            for step in range(1, count):
                for kind in range(2):
                    back_copy(step, which, kind).start()

        def first_step():
            meet(place.neighbours() + [place.at_member(s) for s in range(1, count) if count > 2])
            start_far(0)

        def start_far(which):
            for step in range(1, count):
                for kind in range(2):
                    far_copy(step, which, kind).start()

        def more_far():
            start_rows()
            own_in.start()
            for which in range(1, pairs):
                start_far(which)

        def own_onward():
            own_in.wait()
            own_out.start()

        own_in = pltpu.make_async_copy(rows_ref.at[place.owner], row_hold, hold_sem.at[0])
        own_out = pltpu.make_async_copy(row_hold, back_ref.at[place.owner], hold_sem.at[1])
        stages = reduce.plan()
        actions = [(0, first_step), stages[0], (0, more_far), (1, own_onward)] + stages[1:]
        moments = {}
        for moment, action in actions:
            moments.setdefault(min(int(moment * steps / 24), steps - 1), []).append(action)

        def act(here, some):
            for moment, group in sorted(moments.items()):
                if some(moment):

                    @pl.when(here == moment)
                    def _(group=group):
                        for action in group:
                            action()

        act(now * chunks, lambda moment: moment == 0)

        @pl.when((turn == 0) & (pair > 0))
        def _():
            send_back(pair - 1)

        @pl.when(turn == 0)
        def _():
            for step in range(1, count):
                for kind in range(2):
                    far_copy(step, pair, kind).wait_recv()
            for i in range(count):
                at = slice(i * rows, (i + 1) * rows)
                v_all[at, :] = v_ref[...] if i == 0 else far[i - 1, 1, pair]
                key = k_ref[...] if i == 0 else far[i - 1, 0, pair]
                for half in range(2):
                    own, spare = own_lanes(half, rows)
                    zero = jnp.zeros_like(key)
                    k_own[half, at, :] = jnp.where(own, key, jnp.where(spare, bias_ref[at, :], zero))
                    k_turned[half, :, at] = jnp.transpose(jnp.where(own, key, zero))
            grad_k[...] = jnp.zeros_like(grad_k)
            grad_v[...] = jnp.zeros_like(grad_v)

        query, grad = q_ref[...], g_ref[...]
        turned = jnp.transpose(grad.astype(F32) * o_ref[...].astype(F32))
        asks, plain, grads, centres, logs = [], [], [], [], []
        for half in range(2):
            own, spare = own_lanes(half, block)
            zero = jnp.zeros_like(query)
            asks.append(jnp.where(own, query, jnp.where(spare, zero + 1, zero)))
            plain.append(jnp.where(own, query, zero))
            grads.append(jnp.where(own, grad, zero))
            centres.append(jnp.sum(turned[HD * half : HD * half + HD], axis=0, keepdims=True))
            logs.append(l_ref[half : half + 1, :])
        grad_q[...] = jnp.zeros_like(grad_q)

        @pl.loop(0, chunks)
        def _(c):
            act(now * chunks + c, lambda moment: moment > 0)
            span = pl.ds(pl.multiple_of(c * chunk, chunk), chunk)
            weights, slopes = [], []
            for half in range(2):
                scores = dot_nt(k_own[half, span, :], asks[half])
                grad_weights = dot_nt(v_all[span, :], grads[half])
                exact = jnp.exp2(scores * SCALE - logs[half])
                slope = (exact * (grad_weights - centres[half])).astype(BF)
                weights.append(exact.astype(BF))
                slopes.append(slope)
                grad_q[...] += matmul(k_turned[half, :, span], slope)
            grad_v[span, :] += matmul(weights[0], grads[0]) + matmul(weights[1], grads[1])
            grad_k[span, :] += matmul(slopes[0], plain[0]) + matmul(slopes[1], plain[1])
        at = pl.ds(pl.multiple_of(turn * block, block), block)
        out_ref[at, pl.ds(pl.multiple_of(pair * 2 * HD, 2 * HD), 2 * HD)] = (
            jnp.transpose(grad_q[...]) * 0.125
        ).astype(BF)

        @pl.when(turn == blocks - 1)
        def _():
            for i in range(count):
                at = slice(i * rows, (i + 1) * rows)
                for kind, value, scale in ((0, grad_k, 0.125), (1, grad_v, 1.0)):
                    low = (value[at, :] * scale).astype(BF)
                    if i == 0:
                        first = pl.multiple_of(pair * 2 * HD + (kind + 1) * width, 2 * HD)
                        out_ref[:, pl.ds(first, 2 * HD)] = low
                    else:
                        far_out[i - 1, kind, pair] = low

        @pl.when((turn == blocks - 1) & (pair > 0))
        def _():
            take_back(pair - 1)

        @pl.when(now == pairs * blocks - 1)
        def _():
            send_back(pairs - 1)
            reduce.finish()
            finish_rows()
            own_out.wait()
            take_back(pairs - 1)
            for step in range(1, count):
                for which in range(pairs):
                    for kind in range(2):
                        far_copy(step, which, kind).wait_send()
                        back_copy(step, which, kind).wait_send()

    def column(first):
        return pl.BlockSpec((rows, 2 * HD), lambda i, j: (0, i + first))

    def tile():
        return pl.BlockSpec((block, 2 * HD), lambda i, j: (j, i))

    def resident(shape):
        return pl.BlockSpec(shape, lambda i, j: (0,) * len(shape))

    far_sems = pltpu.SemaphoreType.DMA((away, 2, pairs))
    far_buffer = pltpu.VMEM((away, 2, pairs, rows, 2 * HD), BF)
    return pl.pallas_call(
        kernel,
        grid=(pairs, blocks),
        in_specs=[
            tile(),
            resident((keys, 2 * HD)),
            pl.BlockSpec((None, 8, block), lambda i, j: (i, 0, j)),
            tile(),
            tile(),
            column(pairs),
            column(2 * pairs),
            HBM,
            HBM,
        ]
        + [HBM] * late,
        out_specs=[resident(inputs.shape), HBM] + [resident(tuple(shape)) for shape in shapes],
        out_shape=[jax.ShapeDtypeStruct(inputs.shape, BF), jax.ShapeDtypeStruct(rows_out.shape, BF)]
        + [jax.ShapeDtypeStruct(shape, F32) for shape in shapes],
        scratch_shapes=[
            pltpu.VMEM((2, keys, 2 * HD), BF),
            pltpu.VMEM((2, 2 * HD, keys), BF),
            pltpu.VMEM((keys, 2 * HD), BF),
            pltpu.VMEM((keys, 2 * HD), F32),
            pltpu.VMEM((keys, 2 * HD), F32),
            pltpu.VMEM((2 * HD, block), F32),
            far_buffer,
            far_buffer,
            far_buffer,
            pltpu.VMEM(rows_out.shape[1:], BF),
            pltpu.SemaphoreType.DMA((2,)),
        ]
        + [far_sems] * 4
        + [pltpu.SemaphoreType.DMA((grid.seqs,))] * 2
        + reduce_scratch(grid, shapes),
        compiler_params=pltpu.CompilerParams(
            collective_id=2, has_side_effects=True, vmem_limit_bytes=61 << 20
        ),
        cost_estimate=pl.CostEstimate(
            flops=40 * H * rows * keys * HD, bytes_accessed=12 * rows * width, transcendentals=H * rows * keys
        ),
        name="attention_back",
    )(inputs, key_bias, log_totals, context, grad_context, inputs, inputs, inputs, rows_out, *wholes)


def body(
    tokens,
    lengths,
    query_weight,
    key_weight,
    value_weight,
    out_weight,
    up_weight,
    down_weight,
    query_bias,
    value_bias,
    out_bias,
    up_bias,
    down_bias,
    first_gain,
    first_shift,
    second_gain,
    second_shift,
    cotangent,
):
    seqs, length, width = tokens.shape
    grid = Grid(seqs)
    devices = grid.columns * grid.n
    slim = query_weight.shape[0]
    hidden = up_weight.shape[1]
    tall = hidden // devices
    wide = hidden // width

    vectors = (
        query_bias,
        value_bias,
        out_bias,
        down_bias,
        first_gain,
        first_shift,
        second_gain,
        second_shift,
    )
    vectors = vectors + (up_bias,)
    lines = -(-len(vectors) // 16) * 16
    tile = jnp.zeros((lines, 128), BF)
    for i, vector in enumerate(vectors):
        size = vector.shape[0]
        tile = tile + jnp.pad(vector[None, :], ((i, lines - 1 - i), (0, 128 - size)))
    flat_in, into_full, _, key_bias, live_rows, *whole_vectors = start_exchange(
        grid,
        tokens,
        (query_weight, key_weight, value_weight),
        tile,
        lengths,
        tuple(vector.shape[0] for vector in vectors),
    )
    flat_in = flat_in.reshape(-1, width)
    into_full = into_full.reshape(width, 3 * width)
    query_add, value_add, out_add, down_add, gain_one, shift_one, gain_two, shift_two, up_add = whole_vectors

    into_add = jnp.concatenate([query_add, jnp.zeros_like(query_add), value_add], axis=1)
    inputs = (matmul(flat_in, into_full) + into_add).astype(BF)
    context, log_totals, grad_in, out_full, up_full, down_full = attention(
        grid, inputs, key_bias, (out_weight, up_weight, down_weight), cotangent
    )
    out_full = out_full.reshape(width, width)
    up_full = up_full.reshape(width, hidden)
    down_full = down_full.reshape(hidden, width)
    grad_in = grad_in.reshape(-1, width)

    first_sum = flat_in.astype(F32) + matmul(context, out_full) + out_add
    first_norm, first_unit, first_factor = normalize(first_sum, gain_one, shift_one)
    first_low = first_norm.astype(BF)
    up_pre = matmul(first_low, up_full) + up_add
    below = 0.5 * (1.0 + lax.erf(up_pre * ROOT_HALF))
    slope = (below + up_pre * INV_ROOT_TWO_PI * jnp.exp(-0.5 * up_pre * up_pre)).astype(BF)
    activated, slope = lax.optimization_barrier(((up_pre * below).astype(BF), slope))
    second_sum = first_low.astype(F32) + matmul(activated, down_full) + down_add
    second_norm, second_unit, second_factor = normalize(second_sum, gain_two, shift_two)
    output = (second_norm * live_rows).astype(BF).reshape(seqs, length, width)

    grad_output = grad_in.astype(F32) * live_rows
    grad_gain_two = jnp.sum(grad_output * second_unit, axis=0)
    grad_shift_two = jnp.sum(grad_output, axis=0)
    grad_second = norm_back(grad_output, second_unit, second_factor, gain_two)
    grad_branch = grad_second.astype(BF)
    grad_down_add = jnp.sum(grad_branch.astype(F32), axis=0)
    grad_down = left_product(activated, grad_branch).astype(BF)
    grad_up_low = (right_product(grad_branch, down_full) * slope.astype(F32)).astype(BF)
    grad_up_add = jnp.sum(grad_up_low.astype(F32), axis=0)
    grad_up = left_product(first_low, grad_up_low).astype(BF)
    grad_first = right_product(grad_up_low, up_full) + grad_second
    grad_gain_one = jnp.sum(grad_first * first_unit, axis=0)
    grad_shift_one = jnp.sum(grad_first, axis=0)
    grad_residual = norm_back(grad_first, first_unit, first_factor, gain_one)
    grad_attend = grad_residual.astype(BF)
    grad_out_add = jnp.sum(grad_attend.astype(F32), axis=0)
    grad_out = left_product(context, grad_attend).astype(BF)
    grad_context = right_product(grad_attend, out_full).astype(BF)

    def pack(grads, more=()):
        count = len(grads)
        table = jnp.stack(grads).reshape(count, devices, slim).transpose(1, 0, 2)
        table = jnp.concatenate([table.reshape(devices, count * slim), *more], axis=1).astype(BF)
        size = table.shape[1]
        table = jnp.pad(table, ((0, 0), (0, -size % 128)))
        return jnp.broadcast_to(table[:, None, :], (devices, 8, table.shape[1])).reshape(devices * 8, -1)

    middle = pack(
        [grad_out_add, grad_down_add, grad_gain_one, grad_shift_one, grad_gain_two, grad_shift_two],
        (grad_up_add.reshape(devices, tall),),
    )
    wholes = [
        by_place(grid, grad_up, slim),
        by_place(grid, grad_down, tall),
        by_place(grid, grad_out, slim),
        by_place(grid, middle, 8),
    ]
    low, output, grad_up_own, grad_down_own, grad_out_own, middle_own = attention_back(
        grid, inputs, key_bias, log_totals, context, grad_context, wholes, output
    )
    query_adds = jnp.sum(low[:, :width].astype(F32), axis=0)
    value_adds = jnp.sum(low[:, 2 * width :].astype(F32), axis=0)
    tokens_grad = right_product(low, into_full) + grad_residual
    wholes = [
        by_place(grid, left_product(flat_in, low).astype(BF), slim),
        by_place(grid, pack([query_adds, value_adds]), 8),
    ]
    tokens_grad = tokens_grad.astype(BF).reshape(seqs, length, width)
    tokens_grad, grad_into_own, last_own = end_exchange(grid, tokens_grad, wholes)
    tokens_grad = tokens_grad.astype(F32)
    middle_own, last_own = middle_own[0], last_own[0]
    vector_outs = [last_own[:slim], last_own[slim : 2 * slim]]
    vector_outs = vector_outs + [middle_own[i * slim : (i + 1) * slim] for i in range(6)]
    up_add_own = middle_own[6 * slim : 6 * slim + tall]
    matrix_outs = [grad_into_own[:, i * width : (i + 1) * width] for i in range(3)]
    return (
        output,
        tokens_grad,
        matrix_outs[0],
        matrix_outs[1],
        matrix_outs[2],
        grad_out_own,
        grad_up_own,
        grad_down_own,
        vector_outs[0],
        vector_outs[1],
        vector_outs[2],
        up_add_own,
        vector_outs[3],
        vector_outs[4],
        vector_outs[5],
        vector_outs[6],
        vector_outs[7],
    )


def solution(mesh):
    whole = ("dp", "seq")
    matrix, vector, rows = P(whole, None), P(whole), P("dp", "seq", None)
    return jax.shard_map(
        body,
        mesh=mesh,
        in_specs=(rows, P("dp")) + (matrix,) * 6 + (vector,) * 9 + (rows,),
        out_specs=(rows, rows) + (matrix,) * 6 + (vector,) * 9,
        check_vma=False,
    )
```

```python
import jax
import jax.numpy as jnp
from jax import lax
from jax.experimental import pallas as pl
from jax.experimental.pallas import tpu as pltpu
from jax.sharding import PartitionSpec as P

H = 12
HD = 64

EPSILON = 1e-05
ROOT_HALF = 0.7071067811865476
INV_ROOT_TWO_PI = 0.3989422804014327
BF = jnp.bfloat16
F32 = jnp.float32


def matmul(left, right):
    return jnp.dot(left, right, preferred_element_type=F32)


def left_product(left, right):
    return lax.dot_general(left, right, (((0,), (0,)), ((), ())), preferred_element_type=F32)


def right_product(left, right):
    return lax.dot_general(left, right, (((1,), (1,)), ((), ())), preferred_element_type=F32)


def normalize(inputs, gains, shifts):
    centre = inputs - jnp.mean(inputs, axis=-1, keepdims=True)
    factor = lax.rsqrt(jnp.mean(centre * centre, axis=-1, keepdims=True) + EPSILON)
    unit_rows = centre * factor
    return (unit_rows * gains + shifts, unit_rows, factor)


def norm_back(grad_in, unit_rows, factor, gains):
    grad_unit = grad_in * gains
    return factor * (
        grad_unit
        - jnp.mean(grad_unit, axis=-1, keepdims=True)
        - unit_rows * jnp.mean(grad_unit * unit_rows, axis=-1, keepdims=True)
    )


class Grid:
    def __init__(self, seqs):
        self.columns = lax.axis_size("dp")
        self.n = lax.axis_size("seq")
        self.seqs = seqs
        self.group = self.n // seqs
        self.chips = self.n // 2
        self.column = lax.axis_index("dp")
        place = lax.axis_index("seq")
        self.chip = place // 2
        self.core = place % 2
        self.owner = place // self.group
        self.member = place % self.group


MESH = pl.DeviceIdType.MESH
HBM = pl.BlockSpec(memory_space=pl.ANY)


def remote(source, target, send, receive, device):
    return pltpu.make_async_remote_copy(
        src_ref=source, dst_ref=target, send_sem=send, recv_sem=receive, device_id=device, device_id_type=MESH
    )


def meet(devices):
    barrier = pltpu.get_barrier_semaphore()
    for device in devices:
        pl.semaphore_signal(barrier, inc=1, device_id=device, device_id_type=MESH)
    pl.semaphore_wait(barrier, len(devices))


class Place:
    def __init__(self, grid):
        self.columns, self.chips, self.n = grid.columns, grid.chips, grid.n
        self.seqs, self.group = grid.seqs, grid.group
        self.column = lax.axis_index("dp")
        self.spot = lax.axis_index("seq")
        self.chip = lax.div(self.spot, 2)
        self.core = lax.rem(self.spot, 2)
        self.owner = lax.div(self.spot, self.group)
        self.member = lax.rem(self.spot, self.group)

    def near(self, chip_step):
        return (self.column, (self.chip ^ chip_step) * 2 + self.core)

    def beside(self, column_step):
        return (self.column ^ column_step, self.spot)

    def twin(self):
        return (self.column, self.chip * 2 + (1 - self.core))

    def at_owner(self, step):
        return (self.column, (self.owner ^ step) * self.group + self.member)

    def at_member(self, step):
        return (self.column, self.owner * self.group + lax.rem(self.member + step, self.group))

    def index(self, column_step, chip_step, other=False):
        core = 1 - self.core if other else self.core
        return ((self.column ^ column_step) * self.chips + (self.chip ^ chip_step)) * 2 + core

    def neighbours(self):
        chips = [self.near(step) for step in range(1, self.chips)]
        columns = [self.beside(step) for step in range(1, self.columns)]
        return chips + columns + [self.twin()]


class Gather:
    def __init__(self, place, arrays, send, receive):
        self.place, self.arrays, self.send, self.receive = place, arrays, send, receive
        self.square = place.columns == 4
        self.sent = []

    def copies(self, kind, column_step, chip_step, device, own=False, where=None):
        slot = column_step * self.place.chips + chip_step
        for k, (shard, whole, block) in enumerate(self.arrays):
            held = block(whole, self.place.index(*(where or (column_step, chip_step))))
            yield remote(
                shard if own else held, held, self.send.at[k, kind, slot], self.receive.at[k, kind, slot], device
            )

    def begin(self, kind, column_step, chip_step, device, own=False, where=None):
        self.sent.append((kind, column_step, chip_step, own, where))
        for copy in self.copies(kind, column_step, chip_step, device, own, where):
            copy.start()

    def to_twin(self, column_step, chip_step, own=False):
        self.begin(1, column_step, chip_step, self.place.twin(), own=own)

    def outward(self, chip_step):
        place, own = self.place, chip_step == 0
        for step in range(1, place.columns):
            if not (self.square and step == 3):
                self.begin(0, step, chip_step, place.beside(step), own=own, where=(0, chip_step))
        self.to_twin(0, chip_step, own=own)

    def to_chip(self, step):
        self.begin(0, 0, step, self.place.near(step), own=True, where=(0, 0))

    def start(self):
        for step in range(1, self.place.chips):
            self.to_chip(step)
        self.outward(0)

    def arrive(self, column_step, chip_step, other=False):
        for k, (_, whole, block) in enumerate(self.arrays):
            held = block(whole, self.place.index(column_step, chip_step, other))
            kind = 1 if other else 0
            slot = column_step * self.place.chips + chip_step
            remote(
                held, held, self.send.at[k, kind, slot], self.receive.at[k, kind, slot], self.place.twin()
            ).wait_recv()

    def from_chip(self, chip_step):
        self.arrive(0, chip_step)
        self.outward(chip_step)

    def from_columns(self, chip_step):
        for step in range(1, self.place.columns):
            if self.square and step == 3:
                continue
            self.arrive(step, chip_step)
            if self.square and step == 1 + chip_step % 2:
                self.begin(0, 3, chip_step, self.place.beside(3 - step), where=(step, chip_step))
            self.to_twin(step, chip_step)

    def from_corner(self, chip_step):
        if self.square:
            self.arrive(3, chip_step)
            self.to_twin(3, chip_step)

    def finish(self):
        place = self.place
        for column_step in range(place.columns):
            for chip_step in range(place.chips):
                self.arrive(column_step, chip_step, other=True)
        for kind, column_step, chip_step, own, where in self.sent:
            for copy in self.copies(kind, column_step, chip_step, place.twin(), own, where):
                copy.wait_send()


def gather_semaphores(grid, count):
    shape = (count, 2, grid.columns * grid.chips)
    return [pltpu.SemaphoreType.DMA(shape), pltpu.SemaphoreType.DMA(shape)]


def through(source, held, target, sem):
    copy = pltpu.make_async_copy(source, held, sem)
    copy.start()
    copy.wait()
    copy = pltpu.make_async_copy(held, target, sem)
    copy.start()
    copy.wait()


def start_exchange(grid, tokens, into, vectors, lengths, vector_widths):
    seqs, length, width = tokens.shape
    devices = grid.columns * grid.n
    slim = into[0].shape[0]
    parts = len(into)
    rows = seqs * length
    tile = vectors.shape

    def spread(table, size):
        lane = lax.broadcasted_iota(jnp.int32, (128, devices * size), 1).astype(F32)
        row = lax.broadcasted_iota(jnp.int32, (128, devices * size), 0).astype(F32)
        within = lane - size * jnp.floor((lane + 0.5) * (1.0 / size))
        return matmul(table, (row == within).astype(BF))

    def own_block(count, size):
        lane = lax.broadcasted_iota(jnp.int32, (count, devices * size), 1).astype(F32)
        return jnp.floor((lane + 0.5) * (1.0 / size))

    def kernel(tokens_ref, query_ref, key_ref, value_ref, vectors_ref, lengths_ref, rows_ref, into_all, vectors_all, *rest):
        into_refs = (query_ref, key_ref, value_ref)
        bias_ref, live_ref = rest[:2]
        vector_refs = rest[2 : 2 + len(vector_widths)]
        scratch = rest[2 + len(vector_widths) :]
        row_hold, into_hold, vector_hold, table_hold, hold_sem, send, receive, row_send, row_receive = scratch
        place = Place(grid)
        meet(place.neighbours())

        def part(k):
            return lambda ref, i: ref.at[i, :, pl.ds(k * width, width)]

        gather = Gather(
            place,
            [(into_refs[k], into_all, part(k)) for k in range(parts)]
            + [(vectors_ref, vectors_all, lambda ref, i: ref.at[i])],
            send,
            receive,
        )
        gather.start()

        def row_copy(step):
            return remote(
                tokens_ref.at[place.owner ^ step],
                rows_ref.at[place.owner],
                row_send.at[step],
                row_receive.at[step],
                place.at_owner(step),
            )

        for step in range(1, seqs):
            row_copy(step).start()
        me = place.index(0, 0)
        for k in range(parts):
            through(into_refs[k], into_hold, part(k)(into_all, me), hold_sem)
        through(vectors_ref, vector_hold, vectors_all.at[me], hold_sem)
        through(tokens_ref.at[place.owner], row_hold, rows_ref.at[place.owner], hold_sem)

        my_length = lengths_ref[place.owner]
        for step in range(place.group):
            member = lax.rem(place.member - step + place.group, place.group)
            for source in range(seqs):
                first = (source * place.group + member) * length
                at = slice(step * rows + source * length, step * rows + (source + 1) * length)
                here = lax.broadcasted_iota(jnp.int32, (length, 2 * HD), 0) + first
                bias_ref[at, :] = jnp.where(here < my_length, 0.0, -1e30).astype(BF)
                if step == 0:
                    here = lax.broadcasted_iota(jnp.int32, (length, 1), 0) + first
                    live_ref[at, :] = jnp.where(here < my_length, 1.0, 0.0).astype(F32)

        for step in range(1, place.chips):
            gather.from_chip(step)
            gather.from_columns(step - 1)
        gather.from_columns(place.chips - 1)
        for step in range(place.chips):
            gather.from_corner(step)
        gather.finish()
        copy = pltpu.make_async_copy(vectors_all, table_hold, hold_sem)
        copy.start()
        copy.wait()
        table = table_hold[...].astype(F32)
        kind = lax.broadcasted_iota(jnp.int32, table.shape, 1)
        source = lax.broadcasted_iota(jnp.int32, (devices, 1), 0).astype(F32)
        for k, size in enumerate(vector_widths):
            own = jnp.sum(jnp.where(kind == k, table, 0.0), axis=1).astype(BF)
            apart = jnp.where(own_block(devices, size) == source, spread(own, size), 0.0)
            vector_refs[k][...] = jnp.sum(apart, axis=0, keepdims=True)
        for step in range(1, seqs):
            landed = rows_ref.at[place.owner ^ step]
            remote(
                landed, landed, row_send.at[step], row_receive.at[step], place.at_owner(step)
            ).wait_recv()
            row_copy(step).wait_send()

    vmem = pl.BlockSpec(memory_space=pltpu.VMEM)
    shapes = [tokens.shape, (devices, slim, parts * width), (devices,) + tile]
    return pl.pallas_call(
        kernel,
        in_specs=[HBM] * (parts + 2) + [pl.BlockSpec(memory_space=pltpu.SMEM)],
        out_specs=[HBM] * 3 + [vmem] * (2 + len(vector_widths)),
        out_shape=[jax.ShapeDtypeStruct(shape, BF) for shape in shapes]
        + [jax.ShapeDtypeStruct((grid.group * rows, 2 * HD), BF), jax.ShapeDtypeStruct((rows, 1), F32)]
        + [jax.ShapeDtypeStruct((1, devices * size), F32) for size in vector_widths],
        scratch_shapes=[
            pltpu.VMEM(tokens.shape[1:], BF),
            pltpu.VMEM(into[0].shape, BF),
            pltpu.VMEM(tile, BF),
            pltpu.VMEM((devices,) + tile, BF),
            pltpu.SemaphoreType.DMA(()),
        ]
        + gather_semaphores(grid, parts + 1)
        + [pltpu.SemaphoreType.DMA((seqs,)), pltpu.SemaphoreType.DMA((seqs,))],
        compiler_params=pltpu.CompilerParams(collective_id=0, has_side_effects=True),
        name="start_exchange",
    )(tokens, *into, vectors, lengths)


class Reduce:
    def __init__(self, place, arrays, buffers, semaphores):
        self.place, self.arrays = place, arrays
        self.halves, self.twins, self.sides, self.deeps = buffers
        self.load, self.twin_sems, self.side_sems, self.deep_sems = semaphores
        self.square = place.columns == 4
        self.every = range(len(arrays))
        self.sent = []

    def spot(self, column_step, chip_step):
        return (self.place.column ^ column_step) * self.place.chips + (self.place.chip ^ chip_step)

    def strip(self, column_step):
        return pl.ds((self.place.column ^ column_step) * self.place.chips, self.place.chips)

    def load_copy(self, k, step):
        whole = self.arrays[k][0].at[self.strip(step), self.place.core]
        return pltpu.make_async_copy(whole, self.halves[k].at[self.strip(step)], self.load.at[k, step])

    def twin_copy(self, k, step):
        place = self.place
        whole = self.arrays[k][0].at[self.strip(step), 1 - place.core]
        return remote(
            whole,
            self.twins[k].at[self.strip(step)],
            self.twin_sems[0].at[k, step],
            self.twin_sems[1].at[k, step],
            place.twin(),
        )

    def side_copy(self, k, column_step, chip_step, device):
        return remote(
            self.halves[k].at[self.spot(column_step, chip_step)],
            self.sides[k].at[column_step, chip_step],
            self.side_sems[0].at[k, column_step, chip_step],
            self.side_sems[1].at[k, column_step, chip_step],
            device,
        )

    def deep_copy(self, k, chip_step):
        return remote(
            self.halves[k].at[self.spot(0, chip_step)],
            self.deeps[k].at[chip_step],
            self.deep_sems[0].at[k, chip_step],
            self.deep_sems[1].at[k, chip_step],
            self.place.near(chip_step),
        )

    def start(self):
        order = range(self.place.columns - 1, -1, -1)
        for step in order:
            for k in self.every:
                self.twin_copy(k, step).start()
                self.load_copy(k, step).start()

    def fold(self, step):
        for k in self.every:
            self.load_copy(k, step).wait()
            self.twin_copy(k, step).wait_recv()
            half, twin = self.halves[k], self.twins[k]
            for chip_step in range(self.place.chips):
                spot = self.spot(step, chip_step)
                half[spot] = half[spot] + twin[spot]

    def corner(self, chip_step):
        self.sent.append((3, chip_step))
        for k in self.every:
            self.side_copy(k, 3, chip_step, self.place.beside(1 + chip_step % 2)).start()

    def side(self, column_step, chip_step):
        self.sent.append((column_step, chip_step))
        for k in self.every:
            self.side_copy(k, column_step, chip_step, self.place.beside(column_step)).start()

    def combine(self, chip_step):
        for k in self.every:
            self.side_copy(k, 3, chip_step, self.place.twin()).wait_recv()
            spot = self.spot(2 - chip_step % 2, chip_step)
            half = self.halves[k]
            half[spot] = half[spot] + self.sides[k][3, chip_step]

    def merge(self, chip_step):
        last = 3 if self.square else self.place.columns
        for k in self.every:
            spot = self.spot(0, chip_step)
            total = self.halves[k][spot].astype(F32)
            for step in range(1, last):
                self.side_copy(k, step, chip_step, self.place.twin()).wait_recv()
                total = total + self.sides[k][step, chip_step].astype(F32)
            self.halves[k][spot] = total.astype(BF)

    def deep(self, chip_step):
        for k in self.every:
            self.deep_copy(k, chip_step).start()

    def finish(self):
        place = self.place
        for k in self.every:
            total = self.halves[k][self.spot(0, 0)].astype(F32)
            for step in range(1, place.chips):
                self.deep_copy(k, step).wait_recv()
                total = total + self.deeps[k][step].astype(F32)
            self.arrays[k][1][...] = total
            for step in range(1, place.chips):
                self.deep_copy(k, step).wait_send()
            for step in range(place.columns):
                self.twin_copy(k, step).wait_send()
            for column_step, chip_step in self.sent:
                self.side_copy(k, column_step, chip_step, place.twin()).wait_send()

    def plan(self):
        chips, columns = self.place.chips, self.place.columns
        stages = [(0, self.start)]
        if not self.square:
            for step in range(columns):
                stages.append((1, lambda step=step: self.fold(step)))
            for step in range(1, columns):
                for chip_step in range(chips):
                    stages.append((3, lambda a=step, b=chip_step: self.side(a, b)))
            for chip_step in range(chips):
                stages.append((16, lambda b=chip_step: self.merge(b)))
            for chip_step in range(1, chips):
                stages.append((17, lambda b=chip_step: self.deep(b)))
            return stages
        odd = list(range(1, chips, 2))
        even = list(range(2, chips, 2))
        first = [("corner", b) for b in even] + [(1, b) for b in even] + [(1, b) for b in odd] + [("corner", 0), (1, 0)]
        second = [("corner", b) for b in odd] + [(2, b) for b in odd] + [(2, b) for b in even] + [(2, 0)]
        slots = max(len(first), len(second))
        pace = 14.4 / slots
        mixed = [("fold", 3, 1.9), ("fold", 1, 3.9), ("fold", 2, 3.9), ("fold", 0, 6)]
        corners, last_side = {}, {}
        for link, orders in ((1, first), (2, second)):
            for i, (kind, b) in enumerate(orders):
                if kind == "corner":
                    corners[b] = 2 + pace * i
                    mixed.append(("corner", b, corners[b]))
        for link, orders in ((1, first), (2, second)):
            for i, (kind, b) in enumerate(orders):
                if kind == "corner":
                    continue
                moment = 2 + pace * i
                if link == 2 - b % 2:
                    moment = max(moment, corners[b] + pace + 1.6)
                    mixed.append(("combine", b, moment - 1))
                mixed.append((("side", link), b, moment))
                last_side[b] = max(last_side.get(b, 0), moment)
        for b, moment in last_side.items():
            mixed.append(("merge", b, moment + pace + 0.6))
            if b:
                mixed.append(("deep", b, moment + pace + 1.6))
        mixed.sort(key=lambda item: item[2])
        for kind, b, moment in mixed:
            if isinstance(kind, tuple):
                stages.append((moment, lambda a=kind[1], b=b: self.side(a, b)))
            else:
                stages.append((moment, lambda kind=kind, b=b: getattr(self, kind)(b)))
        return stages


def reduce_scratch(grid, shapes):
    columns, chips, count = grid.columns, grid.chips, len(shapes)
    buffers = []
    for lead in ((columns * chips,), (columns * chips,), (columns, chips), (chips,)):
        buffers = buffers + [pltpu.VMEM(lead + tuple(shape), BF) for shape in shapes]
    dma = pltpu.SemaphoreType.DMA
    sems = [dma((count, columns))] * 3 + [dma((count, columns, chips))] * 2 + [dma((count, chips))] * 2
    return buffers + sems


def reduce_of(place, wholes, results, scratch):
    count = len(wholes)
    groups = [scratch[i * count : (i + 1) * count] for i in range(4)]
    sems = scratch[4 * count : 4 * count + 7]
    return Reduce(
        place, list(zip(wholes, results)), groups, (sems[0], sems[1:3], sems[3:5], sems[5:7])
    )


def by_place(grid, array_in, rows):
    return array_in.reshape(grid.columns * grid.chips, 2, rows, -1)


def row_exchange(place, source, target, send, receive):
    def copy(step):
        return remote(
            source.at[place.owner ^ step],
            target.at[place.owner],
            send.at[step],
            receive.at[step],
            place.at_owner(step),
        )

    def finish():
        for step in range(1, place.seqs):
            landed = target.at[place.owner ^ step]
            remote(landed, landed, send.at[step], receive.at[step], place.at_owner(step)).wait_recv()
            copy(step).wait_send()

    def start():
        for step in range(1, place.seqs):
            copy(step).start()

    return start, finish


def end_exchange(grid, rows, wholes):
    shapes = [whole.shape[2:] for whole in wholes]
    count = len(wholes)

    def kernel(rows_ref, *refs):
        whole_refs, back_ref, results = refs[:count], refs[count], refs[count + 1 : 2 * count + 1]
        row_hold, hold_sem, row_send, row_receive = refs[2 * count + 1 : 2 * count + 5]
        place = Place(grid)
        meet(place.neighbours())
        reduce = reduce_of(place, whole_refs, results, refs[2 * count + 5 :])
        start_rows, finish_rows = row_exchange(place, rows_ref, back_ref, row_send, row_receive)
        stages = reduce.plan()
        stages[0][1]()
        start_rows()
        through(rows_ref.at[place.owner], row_hold, back_ref.at[place.owner], hold_sem)
        for _, action in stages[1:]:
            action()
        reduce.finish()
        finish_rows()

    return pl.pallas_call(
        kernel,
        in_specs=[HBM] * (count + 1),
        out_specs=[HBM] + [pl.BlockSpec(memory_space=pltpu.VMEM)] * count,
        out_shape=[jax.ShapeDtypeStruct(rows.shape, BF)]
        + [jax.ShapeDtypeStruct(shape, F32) for shape in shapes],
        scratch_shapes=[
            pltpu.VMEM(rows.shape[1:], BF),
            pltpu.SemaphoreType.DMA(()),
            pltpu.SemaphoreType.DMA((grid.seqs,)),
            pltpu.SemaphoreType.DMA((grid.seqs,)),
        ]
        + reduce_scratch(grid, shapes),
        compiler_params=pltpu.CompilerParams(
            collective_id=3, has_side_effects=True, vmem_limit_bytes=40 << 20
        ),
        name="end_exchange",
    )(rows, *wholes)


LOG2E = 1.4426950408889634
SCALE = 0.125 * LOG2E


def dot_nt(left, right):
    return lax.dot_general(left, right, (((1,), (1,)), ((), ())), preferred_element_type=F32)


def own_lanes(half, count):
    lane = lax.broadcasted_iota(jnp.int32, (count, 2 * HD), 1)
    return (lane // HD) == half, lane == HD * (1 - half)


def attention(grid, inputs, key_bias, shards, rows_in, block=256):
    rows = inputs.shape[0]
    width = inputs.shape[1] // 3
    pairs = width // (2 * HD)
    count = grid.group
    keys = rows * count
    blocks = rows // block
    steps = pairs * blocks
    devices = grid.columns * grid.n
    late = len(shards)

    def kernel(bias_ref, own_ref, all_ref, rows_ref, *refs):
        shard_refs = refs[:late]
        o_ref, l_ref, block_ref = refs[late : late + 3]
        whole_refs = refs[late + 3 : 2 * late + 3]
        rest = refs[2 * late + 3 :]
        k_own, v_own, far, hold_sem, send, receive, far_send, far_receive, row_send, row_receive = rest[:10]
        holds = rest[10:]
        pair, turn = pl.program_id(0), pl.program_id(1)
        now = pair * blocks + turn
        place = Place(grid)
        gather = Gather(
            place,
            [(s, w, lambda ref, i: ref.at[i]) for s, w in zip(shard_refs, whole_refs)],
            send,
            receive,
        )

        def part(kind):
            return own_ref[:, pl.ds(pl.multiple_of(kind * width + pair * 2 * HD, 2 * HD), 2 * HD)]

        def far_copy(step, which, kind):
            first = pl.multiple_of(which * 2 * HD + (kind + 1) * width, 2 * HD)
            return remote(
                all_ref.at[:, pl.ds(first, 2 * HD)],
                far.at[step - 1, kind, which],
                far_send.at[step - 1, kind, which],
                far_receive.at[step - 1, kind, which],
                place.at_member(step),
            )

        def first_step():
            meet(place.neighbours() + [place.at_member(s) for s in range(1, count) if count > 2])
            start_far(0)
            gather.start()
            for k in range(late + 1):
                own_copy(k, 0).start()
            for which in range(1, pairs):
                start_far(which)

        def start_far(which):
            for step in range(1, count):
                for kind in range(2):
                    far_copy(step, which, kind).start()

        start_rows, finish_rows = row_exchange(place, rows_ref, block_ref, row_send, row_receive)

        def own_copy(k, way):
            if k == late:
                source, target = rows_ref.at[place.owner], block_ref.at[place.owner]
            else:
                source, target = shard_refs[k], whole_refs[k].at[place.index(0, 0)]
            if way == 0:
                return pltpu.make_async_copy(source, holds[k], hold_sem.at[k, 0])
            return pltpu.make_async_copy(holds[k], target, hold_sem.at[k, 1])

        def own_onward():
            for k in range(late + 1):
                own_copy(k, 0).wait()
                own_copy(k, 1).start()

        chips = place.chips
        pace = 8 / max(chips - 2, 1)
        plan = [(0, first_step), (1, own_onward), (8, lambda: gather.from_chip(1)), (8, lambda: gather.from_columns(0))]
        plan.append((10, start_rows))
        for step in range(2, chips):
            moment = 12 + pace * (step - 2)
            plan.append((moment - 0.01 * (step > 2), lambda step=step: gather.from_chip(step)))
            plan.append((moment, lambda step=step: gather.from_columns(step - 1)))
        plan.append((20, lambda: gather.from_columns(chips - 1)))
        moments = {}
        for moment, action in plan:
            moments.setdefault(min(int(moment * steps / 24), steps - 1), []).append(action)

        def last_step():
            for step in range(chips):
                gather.from_corner(step)
            gather.finish()
            for k in range(late + 1):
                own_copy(k, 1).wait()
            finish_rows()
            for step in range(1, count):
                for which in range(pairs):
                    for kind in range(2):
                        far_copy(step, which, kind).wait_send()

        for moment, group in sorted(moments.items()):

            @pl.when(now == moment)
            def _(group=group):
                for action in group:
                    action()

        @pl.when(turn == 0)
        def _():
            for step in range(1, count):
                for kind in range(2):
                    far_copy(step, pair, kind).wait_recv()
            for half in range(2):
                own, spare = own_lanes(half, rows)
                zero = jnp.zeros((rows, 2 * HD), BF)
                for i in range(count):
                    at = slice(i * rows, (i + 1) * rows)
                    key = part(1) if i == 0 else far[i - 1, 0, pair]
                    value = part(2) if i == 0 else far[i - 1, 1, pair]
                    k_own[half, at, :] = jnp.where(own, key, jnp.where(spare, bias_ref[at, :], zero))
                    v_own[half, at, :] = jnp.where(own, value, jnp.where(spare, zero + 1, zero))

        at = pl.ds(pl.multiple_of(turn * block, block), block)
        lanes = pl.ds(pl.multiple_of(pair * 2 * HD, 2 * HD), 2 * HD)
        query = own_ref[at, lanes]
        results = []
        for half in range(2):
            own, spare = own_lanes(half, block)
            zero = jnp.zeros_like(query)
            query_h = jnp.where(own, query, jnp.where(spare, zero + 1, zero))
            scores = dot_nt(query_h, k_own[half])
            largest = jnp.max(scores, axis=1, keepdims=True)
            weights = jnp.exp2((scores - largest) * SCALE).astype(BF)
            summed = matmul(weights, v_own[half])
            totals = summed[:, HD * (1 - half) : HD * (1 - half) + 1]
            results.append(summed / totals)
            log_total = jnp.broadcast_to(largest * SCALE + jnp.log2(totals), (block, 2 * HD))
            l_ref[pair, half : half + 1, at] = jnp.transpose(log_total)[0:1, :]
        lane = lax.broadcasted_iota(jnp.int32, (block, 2 * HD), 1)
        o_ref[at, lanes] = jnp.where(lane < HD, results[0], results[1]).astype(BF)
        pl.when(now == steps - 1)(last_step)

    def resident(shape):
        return pl.BlockSpec(shape, lambda i, j: (0,) * len(shape))

    far_sems = pltpu.SemaphoreType.DMA((max(count - 1, 1), 2, pairs))
    return pl.pallas_call(
        kernel,
        grid=(pairs, blocks),
        in_specs=[
            resident((keys, 2 * HD)),
            resident(inputs.shape),
            HBM,
            HBM,
        ]
        + [HBM] * late,
        out_specs=[
            resident((rows, width)),
            resident((pairs, 8, rows)),
            HBM,
        ]
        + [HBM] * late,
        out_shape=[
            jax.ShapeDtypeStruct((rows, width), BF),
            jax.ShapeDtypeStruct((pairs, 8, rows), F32),
            jax.ShapeDtypeStruct(rows_in.shape, BF),
        ]
        + [jax.ShapeDtypeStruct((devices,) + shard.shape, BF) for shard in shards],
        scratch_shapes=[
            pltpu.VMEM((2, keys, 2 * HD), BF),
            pltpu.VMEM((2, keys, 2 * HD), BF),
            pltpu.VMEM((max(count - 1, 1), 2, pairs, rows, 2 * HD), BF),
            pltpu.SemaphoreType.DMA((late + 1, 2)),
        ]
        + gather_semaphores(grid, late)
        + [far_sems, far_sems]
        + [pltpu.SemaphoreType.DMA((grid.seqs,))] * 2
        + [pltpu.VMEM(shard.shape, BF) for shard in shards]
        + [pltpu.VMEM(rows_in.shape[1:], BF)],
        compiler_params=pltpu.CompilerParams(
            collective_id=1, has_side_effects=True, vmem_limit_bytes=48 << 20
        ),
        cost_estimate=pl.CostEstimate(
            flops=16 * H * rows * keys * HD, bytes_accessed=8 * rows * width, transcendentals=H * rows * keys
        ),
        name="attention",
    )(key_bias, inputs, inputs, rows_in, *shards)


def attention_back(grid, inputs, key_bias, log_totals, context, grad_context, wholes, rows_out, block=1024, chunk=512):
    rows = inputs.shape[0]
    width = inputs.shape[1] // 3
    pairs = width // (2 * HD)
    count = grid.group
    keys = rows * count
    block, chunk = min(block, rows), min(chunk, rows)
    blocks, chunks = rows // block, keys // chunk
    steps = pairs * blocks * chunks
    late = len(wholes)
    shapes = [whole.shape[2:] for whole in wholes]
    away = max(count - 1, 1)

    def kernel(q_ref, bias_ref, l_ref, o_ref, g_ref, k_ref, v_ref, all_ref, rows_ref, *refs):
        whole_refs = refs[:late]
        out_ref, back_ref = refs[late : late + 2]
        results = refs[late + 2 : 2 * late + 2]
        rest = refs[2 * late + 2 :]
        k_own, k_turned, v_all, grad_k, grad_v, grad_q, far, far_out, far_in, row_hold, hold_sem = rest[:11]
        far_send, far_receive, out_send, in_receive, row_send, row_receive = rest[11:17]
        pair, turn = pl.program_id(0), pl.program_id(1)
        now = pair * blocks + turn
        place = Place(grid)
        reduce = reduce_of(place, whole_refs, results, rest[17:])
        start_rows, finish_rows = row_exchange(place, rows_ref, back_ref, row_send, row_receive)

        def far_copy(step, which, kind):
            first = pl.multiple_of(which * 2 * HD + (kind + 1) * width, 2 * HD)
            return remote(
                all_ref.at[:, pl.ds(first, 2 * HD)],
                far.at[step - 1, kind, which],
                far_send.at[step - 1, kind, which],
                far_receive.at[step - 1, kind, which],
                place.at_member(step),
            )

        def back_copy(step, which, kind):
            return remote(
                far_out.at[step - 1, kind, which],
                far_in.at[step - 1, kind, which],
                out_send.at[step - 1, kind, which],
                in_receive.at[step - 1, kind, which],
                place.at_member(count - step),
            )

        def take_back(which):
            for kind in range(2):
                first = pl.multiple_of(which * 2 * HD + (kind + 1) * width, 2 * HD)
                total = out_ref[:, pl.ds(first, 2 * HD)].astype(F32)
                for step in range(1, count):
                    back_copy(step, which, kind).wait_recv()
                    total = total + far_in[step - 1, kind, which].astype(F32)
                out_ref[:, pl.ds(first, 2 * HD)] = total.astype(BF)

        def send_back(which):
            for step in range(1, count):
                for kind in range(2):
                    back_copy(step, which, kind).start()

        def first_step():
            meet(place.neighbours() + [place.at_member(s) for s in range(1, count) if count > 2])
            start_far(0)

        def start_far(which):
            for step in range(1, count):
                for kind in range(2):
                    far_copy(step, which, kind).start()

        def more_far():
            start_rows()
            own_in.start()
            for which in range(1, pairs):
                start_far(which)

        def own_onward():
            own_in.wait()
            own_out.start()

        own_in = pltpu.make_async_copy(rows_ref.at[place.owner], row_hold, hold_sem.at[0])
        own_out = pltpu.make_async_copy(row_hold, back_ref.at[place.owner], hold_sem.at[1])
        stages = reduce.plan()
        actions = [(0, first_step), stages[0], (0, more_far), (1, own_onward)] + stages[1:]
        moments = {}
        for moment, action in actions:
            moments.setdefault(min(int(moment * steps / 24), steps - 1), []).append(action)

        def act(here, some):
            for moment, group in sorted(moments.items()):
                if some(moment):

                    @pl.when(here == moment)
                    def _(group=group):
                        for action in group:
                            action()

        act(now * chunks, lambda moment: moment == 0)

        @pl.when((turn == 0) & (pair > 0))
        def _():
            send_back(pair - 1)

        @pl.when(turn == 0)
        def _():
            for step in range(1, count):
                for kind in range(2):
                    far_copy(step, pair, kind).wait_recv()
            for i in range(count):
                at = slice(i * rows, (i + 1) * rows)
                v_all[at, :] = v_ref[...] if i == 0 else far[i - 1, 1, pair]
                key = k_ref[...] if i == 0 else far[i - 1, 0, pair]
                for half in range(2):
                    own, spare = own_lanes(half, rows)
                    zero = jnp.zeros_like(key)
                    k_own[half, at, :] = jnp.where(own, key, jnp.where(spare, bias_ref[at, :], zero))
                    k_turned[half, :, at] = jnp.transpose(jnp.where(own, key, zero))
            grad_k[...] = jnp.zeros_like(grad_k)
            grad_v[...] = jnp.zeros_like(grad_v)

        query, grad = q_ref[...], g_ref[...]
        turned = jnp.transpose(grad.astype(F32) * o_ref[...].astype(F32))
        asks, plain, grads, centres, logs = [], [], [], [], []
        for half in range(2):
            own, spare = own_lanes(half, block)
            zero = jnp.zeros_like(query)
            asks.append(jnp.where(own, query, jnp.where(spare, zero + 1, zero)))
            plain.append(jnp.where(own, query, zero))
            grads.append(jnp.where(own, grad, zero))
            centres.append(jnp.sum(turned[HD * half : HD * half + HD], axis=0, keepdims=True))
            logs.append(l_ref[half : half + 1, :])
        grad_q[...] = jnp.zeros_like(grad_q)

        @pl.loop(0, chunks)
        def _(c):
            act(now * chunks + c, lambda moment: moment > 0)
            span = pl.ds(pl.multiple_of(c * chunk, chunk), chunk)
            weights, slopes = [], []
            for half in range(2):
                scores = dot_nt(k_own[half, span, :], asks[half])
                grad_weights = dot_nt(v_all[span, :], grads[half])
                exact = jnp.exp2(scores * SCALE - logs[half])
                slope = (exact * (grad_weights - centres[half])).astype(BF)
                weights.append(exact.astype(BF))
                slopes.append(slope)
                grad_q[...] += matmul(k_turned[half, :, span], slope)
            grad_v[span, :] += matmul(weights[0], grads[0]) + matmul(weights[1], grads[1])
            grad_k[span, :] += matmul(slopes[0], plain[0]) + matmul(slopes[1], plain[1])
        at = pl.ds(pl.multiple_of(turn * block, block), block)
        out_ref[at, pl.ds(pl.multiple_of(pair * 2 * HD, 2 * HD), 2 * HD)] = (
            jnp.transpose(grad_q[...]) * 0.125
        ).astype(BF)

        @pl.when(turn == blocks - 1)
        def _():
            for i in range(count):
                at = slice(i * rows, (i + 1) * rows)
                for kind, value, scale in ((0, grad_k, 0.125), (1, grad_v, 1.0)):
                    low = (value[at, :] * scale).astype(BF)
                    if i == 0:
                        first = pl.multiple_of(pair * 2 * HD + (kind + 1) * width, 2 * HD)
                        out_ref[:, pl.ds(first, 2 * HD)] = low
                    else:
                        far_out[i - 1, kind, pair] = low

        @pl.when((turn == blocks - 1) & (pair > 0))
        def _():
            take_back(pair - 1)

        @pl.when(now == pairs * blocks - 1)
        def _():
            send_back(pairs - 1)
            reduce.finish()
            finish_rows()
            own_out.wait()
            take_back(pairs - 1)
            for step in range(1, count):
                for which in range(pairs):
                    for kind in range(2):
                        far_copy(step, which, kind).wait_send()
                        back_copy(step, which, kind).wait_send()

    def column(first):
        return pl.BlockSpec((rows, 2 * HD), lambda i, j: (0, i + first))

    def tile():
        return pl.BlockSpec((block, 2 * HD), lambda i, j: (j, i))

    def resident(shape):
        return pl.BlockSpec(shape, lambda i, j: (0,) * len(shape))

    far_sems = pltpu.SemaphoreType.DMA((away, 2, pairs))
    far_buffer = pltpu.VMEM((away, 2, pairs, rows, 2 * HD), BF)
    return pl.pallas_call(
        kernel,
        grid=(pairs, blocks),
        in_specs=[
            tile(),
            resident((keys, 2 * HD)),
            pl.BlockSpec((None, 8, block), lambda i, j: (i, 0, j)),
            tile(),
            tile(),
            column(pairs),
            column(2 * pairs),
            HBM,
            HBM,
        ]
        + [HBM] * late,
        out_specs=[resident(inputs.shape), HBM] + [resident(tuple(shape)) for shape in shapes],
        out_shape=[jax.ShapeDtypeStruct(inputs.shape, BF), jax.ShapeDtypeStruct(rows_out.shape, BF)]
        + [jax.ShapeDtypeStruct(shape, F32) for shape in shapes],
        scratch_shapes=[
            pltpu.VMEM((2, keys, 2 * HD), BF),
            pltpu.VMEM((2, 2 * HD, keys), BF),
            pltpu.VMEM((keys, 2 * HD), BF),
            pltpu.VMEM((keys, 2 * HD), F32),
            pltpu.VMEM((keys, 2 * HD), F32),
            pltpu.VMEM((2 * HD, block), F32),
            far_buffer,
            far_buffer,
            far_buffer,
            pltpu.VMEM(rows_out.shape[1:], BF),
            pltpu.SemaphoreType.DMA((2,)),
        ]
        + [far_sems] * 4
        + [pltpu.SemaphoreType.DMA((grid.seqs,))] * 2
        + reduce_scratch(grid, shapes),
        compiler_params=pltpu.CompilerParams(
            collective_id=2, has_side_effects=True, vmem_limit_bytes=61 << 20
        ),
        cost_estimate=pl.CostEstimate(
            flops=40 * H * rows * keys * HD, bytes_accessed=12 * rows * width, transcendentals=H * rows * keys
        ),
        name="attention_back",
    )(inputs, key_bias, log_totals, context, grad_context, inputs, inputs, inputs, rows_out, *wholes)


def body(
    tokens,
    lengths,
    query_weight,
    key_weight,
    value_weight,
    out_weight,
    up_weight,
    down_weight,
    query_bias,
    value_bias,
    out_bias,
    up_bias,
    down_bias,
    first_gain,
    first_shift,
    second_gain,
    second_shift,
    cotangent,
):
    seqs, length, width = tokens.shape
    grid = Grid(seqs)
    devices = grid.columns * grid.n
    slim = query_weight.shape[0]
    hidden = up_weight.shape[1]
    tall = hidden // devices
    wide = hidden // width

    vectors = (
        query_bias,
        value_bias,
        out_bias,
        down_bias,
        first_gain,
        first_shift,
        second_gain,
        second_shift,
    )
    vectors = vectors + (up_bias,)
    lines = -(-len(vectors) // 16) * 16
    tile = jnp.zeros((lines, 128), BF)
    for i, vector in enumerate(vectors):
        size = vector.shape[0]
        tile = tile + jnp.pad(vector[None, :], ((i, lines - 1 - i), (0, 128 - size)))
    flat_in, into_full, _, key_bias, live_rows, *whole_vectors = start_exchange(
        grid,
        tokens,
        (query_weight, key_weight, value_weight),
        tile,
        lengths,
        tuple(vector.shape[0] for vector in vectors),
    )
    flat_in = flat_in.reshape(-1, width)
    into_full = into_full.reshape(width, 3 * width)
    query_add, value_add, out_add, down_add, gain_one, shift_one, gain_two, shift_two, up_add = whole_vectors

    into_add = jnp.concatenate([query_add, jnp.zeros_like(query_add), value_add], axis=1)
    inputs = (matmul(flat_in, into_full) + into_add).astype(BF)
    context, log_totals, grad_in, out_full, up_full, down_full = attention(
        grid, inputs, key_bias, (out_weight, up_weight, down_weight), cotangent
    )
    out_full = out_full.reshape(width, width)
    up_full = up_full.reshape(width, hidden)
    down_full = down_full.reshape(hidden, width)
    grad_in = grad_in.reshape(-1, width)

    first_sum = flat_in.astype(F32) + matmul(context, out_full) + out_add
    first_norm, first_unit, first_factor = normalize(first_sum, gain_one, shift_one)
    first_low = lax.optimization_barrier(first_norm.astype(BF))
    up_pre = matmul(first_low, up_full) + up_add
    below = 0.5 * (1.0 + lax.erf(up_pre * ROOT_HALF))
    slope = (below + up_pre * INV_ROOT_TWO_PI * jnp.exp(-0.5 * up_pre * up_pre)).astype(BF)
    activated, slope = lax.optimization_barrier(((up_pre * below).astype(BF), slope))
    second_sum = first_low.astype(F32) + matmul(activated, down_full) + down_add
    second_norm, second_unit, second_factor = normalize(second_sum, gain_two, shift_two)
    output = (second_norm * live_rows).astype(BF).reshape(seqs, length, width)

    grad_output = grad_in.astype(F32) * live_rows
    grad_gain_two = jnp.sum(grad_output * second_unit, axis=0)
    grad_shift_two = jnp.sum(grad_output, axis=0)
    grad_second = norm_back(grad_output, second_unit, second_factor, gain_two)
    grad_branch = grad_second.astype(BF)
    grad_down_add = jnp.sum(grad_branch.astype(F32), axis=0)
    grad_down = left_product(activated, grad_branch).astype(BF)
    grad_up_low = (right_product(grad_branch, down_full) * slope.astype(F32)).astype(BF)
    grad_up_add = jnp.sum(grad_up_low.astype(F32), axis=0)
    grad_up = left_product(first_low, grad_up_low).astype(BF)
    grad_first = right_product(grad_up_low, up_full) + grad_second
    grad_gain_one = jnp.sum(grad_first * first_unit, axis=0)
    grad_shift_one = jnp.sum(grad_first, axis=0)
    grad_residual = norm_back(grad_first, first_unit, first_factor, gain_one)
    grad_attend = grad_residual.astype(BF)
    grad_out_add = jnp.sum(grad_attend.astype(F32), axis=0)
    grad_out = left_product(context, grad_attend).astype(BF)
    grad_context = right_product(grad_attend, out_full).astype(BF)

    def pack(grads, more=()):
        count = len(grads)
        table = jnp.stack(grads).reshape(count, devices, slim).transpose(1, 0, 2)
        table = jnp.concatenate([table.reshape(devices, count * slim), *more], axis=1).astype(BF)
        size = table.shape[1]
        table = jnp.pad(table, ((0, 0), (0, -size % 128)))
        return jnp.broadcast_to(table[:, None, :], (devices, 8, table.shape[1])).reshape(devices * 8, -1)

    middle = pack(
        [grad_out_add, grad_down_add, grad_gain_one, grad_shift_one, grad_gain_two, grad_shift_two],
        (grad_up_add.reshape(devices, tall),),
    )
    wholes = [
        by_place(grid, grad_up, slim),
        by_place(grid, grad_down, tall),
        by_place(grid, grad_out, slim),
        by_place(grid, middle, 8),
    ]
    low, output, grad_up_own, grad_down_own, grad_out_own, middle_own = attention_back(
        grid, inputs, key_bias, log_totals, context, grad_context, wholes, output
    )
    query_adds = jnp.sum(low[:, :width].astype(F32), axis=0)
    value_adds = jnp.sum(low[:, 2 * width :].astype(F32), axis=0)
    tokens_grad = right_product(low, into_full) + grad_residual
    wholes = [
        by_place(grid, left_product(flat_in, low).astype(BF), slim),
        by_place(grid, pack([query_adds, value_adds]), 8),
    ]
    tokens_grad = tokens_grad.astype(BF).reshape(seqs, length, width)
    tokens_grad, grad_into_own, last_own = end_exchange(grid, tokens_grad, wholes)
    tokens_grad = tokens_grad.astype(F32)
    middle_own, last_own = middle_own[0], last_own[0]
    vector_outs = [last_own[:slim], last_own[slim : 2 * slim]]
    vector_outs = vector_outs + [middle_own[i * slim : (i + 1) * slim] for i in range(6)]
    up_add_own = middle_own[6 * slim : 6 * slim + tall]
    matrix_outs = [grad_into_own[:, i * width : (i + 1) * width] for i in range(3)]
    return (
        output,
        tokens_grad,
        matrix_outs[0],
        matrix_outs[1],
        matrix_outs[2],
        grad_out_own,
        grad_up_own,
        grad_down_own,
        vector_outs[0],
        vector_outs[1],
        vector_outs[2],
        up_add_own,
        vector_outs[3],
        vector_outs[4],
        vector_outs[5],
        vector_outs[6],
        vector_outs[7],
    )


def solution(mesh):
    whole = ("dp", "seq")
    matrix, vector, rows = P(whole, None), P(whole), P("dp", "seq", None)
    return jax.shard_map(
        body,
        mesh=mesh,
        in_specs=(rows, P("dp")) + (matrix,) * 6 + (vector,) * 9 + (rows,),
        out_specs=(rows, rows) + (matrix,) * 6 + (vector,) * 9,
        check_vma=False,
    )
```

```python
import jax
import jax.numpy as jnp
from jax import lax
from jax.experimental import pallas as pl
from jax.experimental.pallas import tpu as pltpu
from jax.sharding import PartitionSpec as P

H = 12
HD = 64

EPSILON = 1e-05
ROOT_HALF = 0.7071067811865476
INV_ROOT_TWO_PI = 0.3989422804014327
BF = jnp.bfloat16
F32 = jnp.float32


def matmul(left, right):
    return jnp.dot(left, right, preferred_element_type=F32)


def left_product(left, right):
    return lax.dot_general(left, right, (((0,), (0,)), ((), ())), preferred_element_type=F32)


def right_product(left, right):
    return lax.dot_general(left, right, (((1,), (1,)), ((), ())), preferred_element_type=F32)


def normalize(inputs, gains, shifts):
    centre = inputs - jnp.mean(inputs, axis=-1, keepdims=True)
    factor = lax.rsqrt(jnp.mean(centre * centre, axis=-1, keepdims=True) + EPSILON)
    unit_rows = centre * factor
    return (unit_rows * gains + shifts, unit_rows, factor)


def norm_back(grad_in, unit_rows, factor, gains):
    grad_unit = grad_in * gains
    return factor * (
        grad_unit
        - jnp.mean(grad_unit, axis=-1, keepdims=True)
        - unit_rows * jnp.mean(grad_unit * unit_rows, axis=-1, keepdims=True)
    )


class Grid:
    def __init__(self, seqs):
        self.columns = lax.axis_size("dp")
        self.n = lax.axis_size("seq")
        self.seqs = seqs
        self.group = self.n // seqs
        self.chips = self.n // 2
        self.column = lax.axis_index("dp")
        place = lax.axis_index("seq")
        self.chip = place // 2
        self.core = place % 2
        self.owner = place // self.group
        self.member = place % self.group


MESH = pl.DeviceIdType.MESH
HBM = pl.BlockSpec(memory_space=pl.ANY)


def remote(source, target, send, receive, device):
    return pltpu.make_async_remote_copy(
        src_ref=source, dst_ref=target, send_sem=send, recv_sem=receive, device_id=device, device_id_type=MESH
    )


def meet(devices):
    barrier = pltpu.get_barrier_semaphore()
    for device in devices:
        pl.semaphore_signal(barrier, inc=1, device_id=device, device_id_type=MESH)
    pl.semaphore_wait(barrier, len(devices))


class Place:
    def __init__(self, grid):
        self.columns, self.chips, self.n = grid.columns, grid.chips, grid.n
        self.seqs, self.group = grid.seqs, grid.group
        self.column = lax.axis_index("dp")
        self.spot = lax.axis_index("seq")
        self.chip = lax.div(self.spot, 2)
        self.core = lax.rem(self.spot, 2)
        self.owner = lax.div(self.spot, self.group)
        self.member = lax.rem(self.spot, self.group)

    def near(self, chip_step):
        return (self.column, (self.chip ^ chip_step) * 2 + self.core)

    def beside(self, column_step):
        return (self.column ^ column_step, self.spot)

    def twin(self):
        return (self.column, self.chip * 2 + (1 - self.core))

    def at_owner(self, step):
        return (self.column, (self.owner ^ step) * self.group + self.member)

    def at_member(self, step):
        return (self.column, self.owner * self.group + lax.rem(self.member + step, self.group))

    def index(self, column_step, chip_step, other=False):
        core = 1 - self.core if other else self.core
        return ((self.column ^ column_step) * self.chips + (self.chip ^ chip_step)) * 2 + core

    def neighbours(self):
        chips = [self.near(step) for step in range(1, self.chips)]
        columns = [self.beside(step) for step in range(1, self.columns)]
        return chips + columns + [self.twin()]


class Gather:
    def __init__(self, place, arrays, send, receive):
        self.place, self.arrays, self.send, self.receive = place, arrays, send, receive
        self.square = place.columns == 4
        self.sent = []

    def copies(self, kind, column_step, chip_step, device, own=False, where=None):
        slot = column_step * self.place.chips + chip_step
        for k, (shard, whole, block) in enumerate(self.arrays):
            held = block(whole, self.place.index(*(where or (column_step, chip_step))))
            yield remote(
                shard if own else held, held, self.send.at[k, kind, slot], self.receive.at[k, kind, slot], device
            )

    def begin(self, kind, column_step, chip_step, device, own=False, where=None):
        self.sent.append((kind, column_step, chip_step, own, where))
        for copy in self.copies(kind, column_step, chip_step, device, own, where):
            copy.start()

    def to_twin(self, column_step, chip_step, own=False):
        self.begin(1, column_step, chip_step, self.place.twin(), own=own)

    def outward(self, chip_step):
        place, own = self.place, chip_step == 0
        for step in range(1, place.columns):
            if not (self.square and step == 3):
                self.begin(0, step, chip_step, place.beside(step), own=own, where=(0, chip_step))
        self.to_twin(0, chip_step, own=own)

    def to_chip(self, step):
        self.begin(0, 0, step, self.place.near(step), own=True, where=(0, 0))

    def start(self):
        for step in range(1, self.place.chips):
            self.to_chip(step)
        self.outward(0)

    def arrive(self, column_step, chip_step, other=False):
        for k, (_, whole, block) in enumerate(self.arrays):
            held = block(whole, self.place.index(column_step, chip_step, other))
            kind = 1 if other else 0
            slot = column_step * self.place.chips + chip_step
            remote(
                held, held, self.send.at[k, kind, slot], self.receive.at[k, kind, slot], self.place.twin()
            ).wait_recv()

    def from_chip(self, chip_step):
        self.arrive(0, chip_step)
        self.outward(chip_step)

    def from_columns(self, chip_step):
        for step in range(1, self.place.columns):
            if self.square and step == 3:
                continue
            self.arrive(step, chip_step)
            if self.square and step == 1 + chip_step % 2:
                self.begin(0, 3, chip_step, self.place.beside(3 - step), where=(step, chip_step))
            self.to_twin(step, chip_step)

    def from_corner(self, chip_step):
        if self.square:
            self.arrive(3, chip_step)
            self.to_twin(3, chip_step)

    def finish(self):
        place = self.place
        for column_step in range(place.columns):
            for chip_step in range(place.chips):
                self.arrive(column_step, chip_step, other=True)
        for kind, column_step, chip_step, own, where in self.sent:
            for copy in self.copies(kind, column_step, chip_step, place.twin(), own, where):
                copy.wait_send()


def gather_semaphores(grid, count):
    shape = (count, 2, grid.columns * grid.chips)
    return [pltpu.SemaphoreType.DMA(shape), pltpu.SemaphoreType.DMA(shape)]


def through(source, held, target, sem):
    copy = pltpu.make_async_copy(source, held, sem)
    copy.start()
    copy.wait()
    copy = pltpu.make_async_copy(held, target, sem)
    copy.start()
    copy.wait()


def start_exchange(grid, tokens, into, vectors, lengths, vector_widths):
    seqs, length, width = tokens.shape
    devices = grid.columns * grid.n
    slim = into[0].shape[0]
    parts = len(into)
    rows = seqs * length
    tile = vectors.shape

    def spread(table, size):
        lane = lax.broadcasted_iota(jnp.int32, (128, devices * size), 1).astype(F32)
        row = lax.broadcasted_iota(jnp.int32, (128, devices * size), 0).astype(F32)
        within = lane - size * jnp.floor((lane + 0.5) * (1.0 / size))
        return matmul(table, (row == within).astype(BF))

    def own_block(count, size):
        lane = lax.broadcasted_iota(jnp.int32, (count, devices * size), 1).astype(F32)
        return jnp.floor((lane + 0.5) * (1.0 / size))

    def kernel(tokens_ref, query_ref, key_ref, value_ref, vectors_ref, lengths_ref, rows_ref, into_all, vectors_all, *rest):
        into_refs = (query_ref, key_ref, value_ref)
        bias_ref, live_ref = rest[:2]
        vector_refs = rest[2 : 2 + len(vector_widths)]
        scratch = rest[2 + len(vector_widths) :]
        row_hold, into_hold, vector_hold, table_hold, hold_sem, send, receive, row_send, row_receive = scratch
        place = Place(grid)
        meet(place.neighbours())

        def part(k):
            return lambda ref, i: ref.at[i, :, pl.ds(k * width, width)]

        gather = Gather(
            place,
            [(into_refs[k], into_all, part(k)) for k in range(parts)]
            + [(vectors_ref, vectors_all, lambda ref, i: ref.at[i])],
            send,
            receive,
        )
        gather.start()

        def row_copy(step):
            return remote(
                tokens_ref.at[place.owner ^ step],
                rows_ref.at[place.owner],
                row_send.at[step],
                row_receive.at[step],
                place.at_owner(step),
            )

        for step in range(1, seqs):
            row_copy(step).start()
        me = place.index(0, 0)
        for k in range(parts):
            through(into_refs[k], into_hold, part(k)(into_all, me), hold_sem)
        through(vectors_ref, vector_hold, vectors_all.at[me], hold_sem)
        through(tokens_ref.at[place.owner], row_hold, rows_ref.at[place.owner], hold_sem)

        my_length = lengths_ref[place.owner]
        for step in range(place.group):
            member = lax.rem(place.member - step + place.group, place.group)
            for source in range(seqs):
                first = (source * place.group + member) * length
                at = slice(step * rows + source * length, step * rows + (source + 1) * length)
                here = lax.broadcasted_iota(jnp.int32, (length, 2 * HD), 0) + first
                bias_ref[at, :] = jnp.where(here < my_length, 0.0, -1e30).astype(BF)
                if step == 0:
                    here = lax.broadcasted_iota(jnp.int32, (length, 1), 0) + first
                    live_ref[at, :] = jnp.where(here < my_length, 1.0, 0.0).astype(F32)

        for step in range(1, place.chips):
            gather.from_chip(step)
            gather.from_columns(step - 1)
        gather.from_columns(place.chips - 1)
        for step in range(place.chips):
            gather.from_corner(step)
        gather.finish()
        copy = pltpu.make_async_copy(vectors_all, table_hold, hold_sem)
        copy.start()
        copy.wait()
        table = table_hold[...].astype(F32)
        kind = lax.broadcasted_iota(jnp.int32, table.shape, 1)
        source = lax.broadcasted_iota(jnp.int32, (devices, 1), 0).astype(F32)
        for k, size in enumerate(vector_widths):
            own = jnp.sum(jnp.where(kind == k, table, 0.0), axis=1).astype(BF)
            apart = jnp.where(own_block(devices, size) == source, spread(own, size), 0.0)
            vector_refs[k][...] = jnp.sum(apart, axis=0, keepdims=True)
        for step in range(1, seqs):
            landed = rows_ref.at[place.owner ^ step]
            remote(
                landed, landed, row_send.at[step], row_receive.at[step], place.at_owner(step)
            ).wait_recv()
            row_copy(step).wait_send()

    vmem = pl.BlockSpec(memory_space=pltpu.VMEM)
    shapes = [tokens.shape, (devices, slim, parts * width), (devices,) + tile]
    return pl.pallas_call(
        kernel,
        in_specs=[HBM] * (parts + 2) + [pl.BlockSpec(memory_space=pltpu.SMEM)],
        out_specs=[HBM] * 3 + [vmem] * (2 + len(vector_widths)),
        out_shape=[jax.ShapeDtypeStruct(shape, BF) for shape in shapes]
        + [jax.ShapeDtypeStruct((grid.group * rows, 2 * HD), BF), jax.ShapeDtypeStruct((rows, 1), F32)]
        + [jax.ShapeDtypeStruct((1, devices * size), F32) for size in vector_widths],
        scratch_shapes=[
            pltpu.VMEM(tokens.shape[1:], BF),
            pltpu.VMEM(into[0].shape, BF),
            pltpu.VMEM(tile, BF),
            pltpu.VMEM((devices,) + tile, BF),
            pltpu.SemaphoreType.DMA(()),
        ]
        + gather_semaphores(grid, parts + 1)
        + [pltpu.SemaphoreType.DMA((seqs,)), pltpu.SemaphoreType.DMA((seqs,))],
        compiler_params=pltpu.CompilerParams(collective_id=0, has_side_effects=True),
        name="start_exchange",
    )(tokens, *into, vectors, lengths)


class Reduce:
    def __init__(self, place, arrays, buffers, semaphores):
        self.place, self.arrays = place, arrays
        self.halves, self.twins, self.sides, self.deeps = buffers
        self.load, self.twin_sems, self.side_sems, self.deep_sems = semaphores
        self.square = place.columns == 4
        self.every = range(len(arrays))
        self.sent = []

    def spot(self, column_step, chip_step):
        return (self.place.column ^ column_step) * self.place.chips + (self.place.chip ^ chip_step)

    def strip(self, column_step):
        return pl.ds((self.place.column ^ column_step) * self.place.chips, self.place.chips)

    def load_copy(self, k, step):
        whole = self.arrays[k][0].at[self.strip(step), self.place.core]
        return pltpu.make_async_copy(whole, self.halves[k].at[self.strip(step)], self.load.at[k, step])

    def twin_copy(self, k, step):
        place = self.place
        whole = self.arrays[k][0].at[self.strip(step), 1 - place.core]
        return remote(
            whole,
            self.twins[k].at[self.strip(step)],
            self.twin_sems[0].at[k, step],
            self.twin_sems[1].at[k, step],
            place.twin(),
        )

    def side_copy(self, k, column_step, chip_step, device):
        return remote(
            self.halves[k].at[self.spot(column_step, chip_step)],
            self.sides[k].at[column_step, chip_step],
            self.side_sems[0].at[k, column_step, chip_step],
            self.side_sems[1].at[k, column_step, chip_step],
            device,
        )

    def deep_copy(self, k, chip_step):
        return remote(
            self.halves[k].at[self.spot(0, chip_step)],
            self.deeps[k].at[chip_step],
            self.deep_sems[0].at[k, chip_step],
            self.deep_sems[1].at[k, chip_step],
            self.place.near(chip_step),
        )

    def start(self):
        order = range(self.place.columns - 1, -1, -1)
        for step in order:
            for k in self.every:
                self.twin_copy(k, step).start()
                self.load_copy(k, step).start()

    def fold(self, step):
        for k in self.every:
            self.load_copy(k, step).wait()
            self.twin_copy(k, step).wait_recv()
            half, twin = self.halves[k], self.twins[k]
            for chip_step in range(self.place.chips):
                spot = self.spot(step, chip_step)
                half[spot] = half[spot] + twin[spot]

    def corner(self, chip_step):
        self.sent.append((3, chip_step))
        for k in self.every:
            self.side_copy(k, 3, chip_step, self.place.beside(1 + chip_step % 2)).start()

    def side(self, column_step, chip_step):
        self.sent.append((column_step, chip_step))
        for k in self.every:
            self.side_copy(k, column_step, chip_step, self.place.beside(column_step)).start()

    def combine(self, chip_step):
        for k in self.every:
            self.side_copy(k, 3, chip_step, self.place.twin()).wait_recv()
            spot = self.spot(2 - chip_step % 2, chip_step)
            half = self.halves[k]
            half[spot] = half[spot] + self.sides[k][3, chip_step]

    def merge(self, chip_step):
        last = 3 if self.square else self.place.columns
        for k in self.every:
            spot = self.spot(0, chip_step)
            total = self.halves[k][spot].astype(F32)
            for step in range(1, last):
                self.side_copy(k, step, chip_step, self.place.twin()).wait_recv()
                total = total + self.sides[k][step, chip_step].astype(F32)
            self.halves[k][spot] = total.astype(BF)

    def deep(self, chip_step):
        for k in self.every:
            self.deep_copy(k, chip_step).start()

    def finish(self):
        place = self.place
        for k in self.every:
            total = self.halves[k][self.spot(0, 0)].astype(F32)
            for step in range(1, place.chips):
                self.deep_copy(k, step).wait_recv()
                total = total + self.deeps[k][step].astype(F32)
            self.arrays[k][1][...] = total
            for step in range(1, place.chips):
                self.deep_copy(k, step).wait_send()
            for step in range(place.columns):
                self.twin_copy(k, step).wait_send()
            for column_step, chip_step in self.sent:
                self.side_copy(k, column_step, chip_step, place.twin()).wait_send()

    def plan(self):
        chips, columns = self.place.chips, self.place.columns
        stages = [(0, self.start)]
        if not self.square:
            for step in range(columns):
                stages.append((1, lambda step=step: self.fold(step)))
            for step in range(1, columns):
                for chip_step in range(chips):
                    stages.append((3, lambda a=step, b=chip_step: self.side(a, b)))
            for chip_step in range(chips):
                stages.append((16, lambda b=chip_step: self.merge(b)))
            for chip_step in range(1, chips):
                stages.append((17, lambda b=chip_step: self.deep(b)))
            return stages
        odd = list(range(1, chips, 2))
        even = list(range(2, chips, 2))
        first = [("corner", b) for b in even] + [(1, b) for b in even] + [(1, b) for b in odd] + [("corner", 0), (1, 0)]
        second = [("corner", b) for b in odd] + [(2, b) for b in odd] + [(2, b) for b in even] + [(2, 0)]
        slots = max(len(first), len(second))
        pace = 14.4 / slots
        mixed = [("fold", 3, 1.9), ("fold", 1, 3.9), ("fold", 2, 3.9), ("fold", 0, 6)]
        corners, last_side = {}, {}
        for link, orders in ((1, first), (2, second)):
            for i, (kind, b) in enumerate(orders):
                if kind == "corner":
                    corners[b] = 2 + pace * i
                    mixed.append(("corner", b, corners[b]))
        for link, orders in ((1, first), (2, second)):
            for i, (kind, b) in enumerate(orders):
                if kind == "corner":
                    continue
                moment = 2 + pace * i
                if link == 2 - b % 2:
                    moment = max(moment, corners[b] + pace + 1.6)
                    mixed.append(("combine", b, moment - 1))
                mixed.append((("side", link), b, moment))
                last_side[b] = max(last_side.get(b, 0), moment)
        for b, moment in last_side.items():
            mixed.append(("merge", b, moment + pace + 0.6))
            if b:
                mixed.append(("deep", b, moment + pace + 1.6))
        mixed.sort(key=lambda item: item[2])
        for kind, b, moment in mixed:
            if isinstance(kind, tuple):
                stages.append((moment, lambda a=kind[1], b=b: self.side(a, b)))
            else:
                stages.append((moment, lambda kind=kind, b=b: getattr(self, kind)(b)))
        return stages


def reduce_scratch(grid, shapes):
    columns, chips, count = grid.columns, grid.chips, len(shapes)
    buffers = []
    for lead in ((columns * chips,), (columns * chips,), (columns, chips), (chips,)):
        buffers = buffers + [pltpu.VMEM(lead + tuple(shape), BF) for shape in shapes]
    dma = pltpu.SemaphoreType.DMA
    sems = [dma((count, columns))] * 3 + [dma((count, columns, chips))] * 2 + [dma((count, chips))] * 2
    return buffers + sems


def reduce_of(place, wholes, results, scratch):
    count = len(wholes)
    groups = [scratch[i * count : (i + 1) * count] for i in range(4)]
    sems = scratch[4 * count : 4 * count + 7]
    return Reduce(
        place, list(zip(wholes, results)), groups, (sems[0], sems[1:3], sems[3:5], sems[5:7])
    )


def by_place(grid, array_in, rows):
    return array_in.reshape(grid.columns * grid.chips, 2, rows, -1)


def row_exchange(place, source, target, send, receive):
    def copy(step):
        return remote(
            source.at[place.owner ^ step],
            target.at[place.owner],
            send.at[step],
            receive.at[step],
            place.at_owner(step),
        )

    def finish():
        for step in range(1, place.seqs):
            landed = target.at[place.owner ^ step]
            remote(landed, landed, send.at[step], receive.at[step], place.at_owner(step)).wait_recv()
            copy(step).wait_send()

    def start():
        for step in range(1, place.seqs):
            copy(step).start()

    return start, finish


def end_exchange(grid, rows, wholes):
    shapes = [whole.shape[2:] for whole in wholes]
    count = len(wholes)

    def kernel(rows_ref, *refs):
        whole_refs, back_ref, results = refs[:count], refs[count], refs[count + 1 : 2 * count + 1]
        row_hold, hold_sem, row_send, row_receive = refs[2 * count + 1 : 2 * count + 5]
        place = Place(grid)
        meet(place.neighbours())
        reduce = reduce_of(place, whole_refs, results, refs[2 * count + 5 :])
        start_rows, finish_rows = row_exchange(place, rows_ref, back_ref, row_send, row_receive)
        stages = reduce.plan()
        stages[0][1]()
        start_rows()
        through(rows_ref.at[place.owner], row_hold, back_ref.at[place.owner], hold_sem)
        for _, action in stages[1:]:
            action()
        reduce.finish()
        finish_rows()

    return pl.pallas_call(
        kernel,
        in_specs=[HBM] * (count + 1),
        out_specs=[HBM] + [pl.BlockSpec(memory_space=pltpu.VMEM)] * count,
        out_shape=[jax.ShapeDtypeStruct(rows.shape, BF)]
        + [jax.ShapeDtypeStruct(shape, F32) for shape in shapes],
        scratch_shapes=[
            pltpu.VMEM(rows.shape[1:], BF),
            pltpu.SemaphoreType.DMA(()),
            pltpu.SemaphoreType.DMA((grid.seqs,)),
            pltpu.SemaphoreType.DMA((grid.seqs,)),
        ]
        + reduce_scratch(grid, shapes),
        compiler_params=pltpu.CompilerParams(
            collective_id=3, has_side_effects=True, vmem_limit_bytes=40 << 20
        ),
        name="end_exchange",
    )(rows, *wholes)


LOG2E = 1.4426950408889634
SCALE = 0.125 * LOG2E


def dot_nt(left, right):
    return lax.dot_general(left, right, (((1,), (1,)), ((), ())), preferred_element_type=F32)


def own_lanes(half, count):
    lane = lax.broadcasted_iota(jnp.int32, (count, 2 * HD), 1)
    return (lane // HD) == half, lane == HD * (1 - half)


def attention(grid, inputs, key_bias, shards, rows_in, block=256):
    rows = inputs.shape[0]
    width = inputs.shape[1] // 3
    pairs = width // (2 * HD)
    count = grid.group
    keys = rows * count
    blocks = rows // block
    steps = pairs * blocks
    devices = grid.columns * grid.n
    late = len(shards)

    def kernel(bias_ref, own_ref, all_ref, rows_ref, *refs):
        shard_refs = refs[:late]
        o_ref, l_ref, block_ref = refs[late : late + 3]
        whole_refs = refs[late + 3 : 2 * late + 3]
        rest = refs[2 * late + 3 :]
        k_own, v_own, far, hold_sem, send, receive, far_send, far_receive, row_send, row_receive = rest[:10]
        holds = rest[10:]
        pair, turn = pl.program_id(0), pl.program_id(1)
        now = pair * blocks + turn
        place = Place(grid)
        gather = Gather(
            place,
            [(s, w, lambda ref, i: ref.at[i]) for s, w in zip(shard_refs, whole_refs)],
            send,
            receive,
        )

        def part(kind):
            return own_ref[:, pl.ds(pl.multiple_of(kind * width + pair * 2 * HD, 2 * HD), 2 * HD)]

        def far_copy(step, which, kind):
            first = pl.multiple_of(which * 2 * HD + (kind + 1) * width, 2 * HD)
            return remote(
                all_ref.at[:, pl.ds(first, 2 * HD)],
                far.at[step - 1, kind, which],
                far_send.at[step - 1, kind, which],
                far_receive.at[step - 1, kind, which],
                place.at_member(step),
            )

        def first_step():
            meet(place.neighbours() + [place.at_member(s) for s in range(1, count) if count > 2])
            start_far(0)
            gather.start()
            for k in range(late + 1):
                own_copy(k, 0).start()
            for which in range(1, pairs):
                start_far(which)

        def start_far(which):
            for step in range(1, count):
                for kind in range(2):
                    far_copy(step, which, kind).start()

        start_rows, finish_rows = row_exchange(place, rows_ref, block_ref, row_send, row_receive)

        def own_copy(k, way):
            if k == late:
                source, target = rows_ref.at[place.owner], block_ref.at[place.owner]
            else:
                source, target = shard_refs[k], whole_refs[k].at[place.index(0, 0)]
            if way == 0:
                return pltpu.make_async_copy(source, holds[k], hold_sem.at[k, 0])
            return pltpu.make_async_copy(holds[k], target, hold_sem.at[k, 1])

        def own_onward():
            for k in range(late + 1):
                own_copy(k, 0).wait()
                own_copy(k, 1).start()

        chips = place.chips
        pace = 8 / max(chips - 2, 1)
        plan = [(0, first_step), (1, own_onward), (8, lambda: gather.from_chip(1)), (8, lambda: gather.from_columns(0))]
        plan.append((10, start_rows))
        for step in range(2, chips):
            moment = 12 + pace * (step - 2)
            plan.append((moment - 0.01 * (step > 2), lambda step=step: gather.from_chip(step)))
            plan.append((moment, lambda step=step: gather.from_columns(step - 1)))
        plan.append((20, lambda: gather.from_columns(chips - 1)))
        moments = {}
        for moment, action in plan:
            moments.setdefault(min(int(moment * steps / 24), steps - 1), []).append(action)

        def last_step():
            for step in range(chips):
                gather.from_corner(step)
            gather.finish()
            for k in range(late + 1):
                own_copy(k, 1).wait()
            finish_rows()
            for step in range(1, count):
                for which in range(pairs):
                    for kind in range(2):
                        far_copy(step, which, kind).wait_send()

        for moment, group in sorted(moments.items()):

            @pl.when(now == moment)
            def _(group=group):
                for action in group:
                    action()

        @pl.when(turn == 0)
        def _():
            for step in range(1, count):
                for kind in range(2):
                    far_copy(step, pair, kind).wait_recv()
            for half in range(2):
                own, spare = own_lanes(half, rows)
                zero = jnp.zeros((rows, 2 * HD), BF)
                for i in range(count):
                    at = slice(i * rows, (i + 1) * rows)
                    key = part(1) if i == 0 else far[i - 1, 0, pair]
                    value = part(2) if i == 0 else far[i - 1, 1, pair]
                    k_own[half, at, :] = jnp.where(own, key, jnp.where(spare, bias_ref[at, :], zero))
                    v_own[half, at, :] = jnp.where(own, value, jnp.where(spare, zero + 1, zero))

        at = pl.ds(pl.multiple_of(turn * block, block), block)
        lanes = pl.ds(pl.multiple_of(pair * 2 * HD, 2 * HD), 2 * HD)
        query = own_ref[at, lanes]
        results = []
        for half in range(2):
            own, spare = own_lanes(half, block)
            zero = jnp.zeros_like(query)
            query_h = jnp.where(own, query, jnp.where(spare, zero + 1, zero))
            scores = dot_nt(query_h, k_own[half])
            largest = jnp.max(scores, axis=1, keepdims=True)
            weights = jnp.exp2((scores - largest) * SCALE).astype(BF)
            summed = matmul(weights, v_own[half])
            totals = summed[:, HD * (1 - half) : HD * (1 - half) + 1]
            results.append(summed / totals)
            log_total = jnp.broadcast_to(largest * SCALE + jnp.log2(totals), (block, 2 * HD))
            l_ref[pair, half : half + 1, at] = jnp.transpose(log_total)[0:1, :]
        lane = lax.broadcasted_iota(jnp.int32, (block, 2 * HD), 1)
        o_ref[at, lanes] = jnp.where(lane < HD, results[0], results[1]).astype(BF)
        pl.when(now == steps - 1)(last_step)

    def resident(shape):
        return pl.BlockSpec(shape, lambda i, j: (0,) * len(shape))

    far_sems = pltpu.SemaphoreType.DMA((max(count - 1, 1), 2, pairs))
    return pl.pallas_call(
        kernel,
        grid=(pairs, blocks),
        in_specs=[
            resident((keys, 2 * HD)),
            resident(inputs.shape),
            HBM,
            HBM,
        ]
        + [HBM] * late,
        out_specs=[
            resident((rows, width)),
            resident((pairs, 8, rows)),
            HBM,
        ]
        + [HBM] * late,
        out_shape=[
            jax.ShapeDtypeStruct((rows, width), BF),
            jax.ShapeDtypeStruct((pairs, 8, rows), F32),
            jax.ShapeDtypeStruct(rows_in.shape, BF),
        ]
        + [jax.ShapeDtypeStruct((devices,) + shard.shape, BF) for shard in shards],
        scratch_shapes=[
            pltpu.VMEM((2, keys, 2 * HD), BF),
            pltpu.VMEM((2, keys, 2 * HD), BF),
            pltpu.VMEM((max(count - 1, 1), 2, pairs, rows, 2 * HD), BF),
            pltpu.SemaphoreType.DMA((late + 1, 2)),
        ]
        + gather_semaphores(grid, late)
        + [far_sems, far_sems]
        + [pltpu.SemaphoreType.DMA((grid.seqs,))] * 2
        + [pltpu.VMEM(shard.shape, BF) for shard in shards]
        + [pltpu.VMEM(rows_in.shape[1:], BF)],
        compiler_params=pltpu.CompilerParams(
            collective_id=1, has_side_effects=True, vmem_limit_bytes=48 << 20
        ),
        cost_estimate=pl.CostEstimate(
            flops=16 * H * rows * keys * HD, bytes_accessed=8 * rows * width, transcendentals=H * rows * keys
        ),
        name="attention",
    )(key_bias, inputs, inputs, rows_in, *shards)


def attention_back(grid, inputs, key_bias, log_totals, context, grad_context, wholes, rows_out, block=1024, chunk=512):
    rows = inputs.shape[0]
    width = inputs.shape[1] // 3
    pairs = width // (2 * HD)
    count = grid.group
    keys = rows * count
    block, chunk = min(block, rows), min(chunk, rows)
    blocks, chunks = rows // block, keys // chunk
    steps = pairs * blocks * chunks
    late = len(wholes)
    shapes = [whole.shape[2:] for whole in wholes]
    away = max(count - 1, 1)

    def kernel(q_ref, bias_ref, l_ref, o_ref, g_ref, k_ref, v_ref, all_ref, rows_ref, *refs):
        whole_refs = refs[:late]
        out_ref, back_ref = refs[late : late + 2]
        results = refs[late + 2 : 2 * late + 2]
        rest = refs[2 * late + 2 :]
        k_own, k_turned, v_all, grad_k, grad_v, grad_q, far, far_out, far_in, row_hold, hold_sem = rest[:11]
        far_send, far_receive, out_send, in_receive, row_send, row_receive = rest[11:17]
        pair, turn = pl.program_id(0), pl.program_id(1)
        now = pair * blocks + turn
        place = Place(grid)
        reduce = reduce_of(place, whole_refs, results, rest[17:])
        start_rows, finish_rows = row_exchange(place, rows_ref, back_ref, row_send, row_receive)

        def far_copy(step, which, kind):
            first = pl.multiple_of(which * 2 * HD + (kind + 1) * width, 2 * HD)
            return remote(
                all_ref.at[:, pl.ds(first, 2 * HD)],
                far.at[step - 1, kind, which],
                far_send.at[step - 1, kind, which],
                far_receive.at[step - 1, kind, which],
                place.at_member(step),
            )

        def back_copy(step, which, kind):
            return remote(
                far_out.at[step - 1, kind, which],
                far_in.at[step - 1, kind, which],
                out_send.at[step - 1, kind, which],
                in_receive.at[step - 1, kind, which],
                place.at_member(count - step),
            )

        def take_back(which):
            for kind in range(2):
                first = pl.multiple_of(which * 2 * HD + (kind + 1) * width, 2 * HD)
                total = out_ref[:, pl.ds(first, 2 * HD)].astype(F32)
                for step in range(1, count):
                    back_copy(step, which, kind).wait_recv()
                    total = total + far_in[step - 1, kind, which].astype(F32)
                out_ref[:, pl.ds(first, 2 * HD)] = total.astype(BF)

        def send_back(which):
            for step in range(1, count):
                for kind in range(2):
                    back_copy(step, which, kind).start()

        def first_step():
            meet(place.neighbours() + [place.at_member(s) for s in range(1, count) if count > 2])
            start_far(0)

        def start_far(which):
            for step in range(1, count):
                for kind in range(2):
                    far_copy(step, which, kind).start()

        def more_far():
            start_rows()
            own_in.start()
            for which in range(1, pairs):
                start_far(which)

        def own_onward():
            own_in.wait()
            own_out.start()

        own_in = pltpu.make_async_copy(rows_ref.at[place.owner], row_hold, hold_sem.at[0])
        own_out = pltpu.make_async_copy(row_hold, back_ref.at[place.owner], hold_sem.at[1])
        stages = reduce.plan()
        actions = [(0, first_step), stages[0], (0, more_far), (1, own_onward)] + stages[1:]
        moments = {}
        for moment, action in actions:
            moments.setdefault(min(int(moment * steps / 24), steps - 1), []).append(action)

        def act(here, some):
            for moment, group in sorted(moments.items()):
                if some(moment):

                    @pl.when(here == moment)
                    def _(group=group):
                        for action in group:
                            action()

        act(now * chunks, lambda moment: moment == 0)

        @pl.when((turn == 0) & (pair > 0))
        def _():
            send_back(pair - 1)

        @pl.when(turn == 0)
        def _():
            for step in range(1, count):
                for kind in range(2):
                    far_copy(step, pair, kind).wait_recv()
            for i in range(count):
                at = slice(i * rows, (i + 1) * rows)
                v_all[at, :] = v_ref[...] if i == 0 else far[i - 1, 1, pair]
                key = k_ref[...] if i == 0 else far[i - 1, 0, pair]
                for half in range(2):
                    own, spare = own_lanes(half, rows)
                    zero = jnp.zeros_like(key)
                    k_own[half, at, :] = jnp.where(own, key, jnp.where(spare, bias_ref[at, :], zero))
                    k_turned[half, :, at] = jnp.transpose(jnp.where(own, key, zero))
            grad_k[...] = jnp.zeros_like(grad_k)
            grad_v[...] = jnp.zeros_like(grad_v)

        query, grad = q_ref[...], g_ref[...]
        turned = jnp.transpose(grad.astype(F32) * o_ref[...].astype(F32))
        asks, plain, grads, centres, logs = [], [], [], [], []
        for half in range(2):
            own, spare = own_lanes(half, block)
            zero = jnp.zeros_like(query)
            asks.append(jnp.where(own, query, jnp.where(spare, zero + 1, zero)))
            plain.append(jnp.where(own, query, zero))
            grads.append(jnp.where(own, grad, zero))
            centres.append(jnp.sum(turned[HD * half : HD * half + HD], axis=0, keepdims=True))
            logs.append(l_ref[half : half + 1, :])
        grad_q[...] = jnp.zeros_like(grad_q)

        @pl.loop(0, chunks)
        def _(c):
            act(now * chunks + c, lambda moment: moment > 0)
            span = pl.ds(pl.multiple_of(c * chunk, chunk), chunk)
            weights, slopes = [], []
            for half in range(2):
                scores = dot_nt(k_own[half, span, :], asks[half])
                grad_weights = dot_nt(v_all[span, :], grads[half])
                exact = jnp.exp2(scores * SCALE - logs[half])
                slope = (exact * (grad_weights - centres[half])).astype(BF)
                weights.append(exact.astype(BF))
                slopes.append(slope)
                grad_q[...] += matmul(k_turned[half, :, span], slope)
            grad_v[span, :] += matmul(weights[0], grads[0]) + matmul(weights[1], grads[1])
            grad_k[span, :] += matmul(slopes[0], plain[0]) + matmul(slopes[1], plain[1])
        at = pl.ds(pl.multiple_of(turn * block, block), block)
        out_ref[at, pl.ds(pl.multiple_of(pair * 2 * HD, 2 * HD), 2 * HD)] = (
            jnp.transpose(grad_q[...]) * 0.125
        ).astype(BF)

        @pl.when(turn == blocks - 1)
        def _():
            for i in range(count):
                at = slice(i * rows, (i + 1) * rows)
                for kind, value, scale in ((0, grad_k, 0.125), (1, grad_v, 1.0)):
                    low = (value[at, :] * scale).astype(BF)
                    if i == 0:
                        first = pl.multiple_of(pair * 2 * HD + (kind + 1) * width, 2 * HD)
                        out_ref[:, pl.ds(first, 2 * HD)] = low
                    else:
                        far_out[i - 1, kind, pair] = low

        @pl.when((turn == blocks - 1) & (pair > 0))
        def _():
            take_back(pair - 1)

        @pl.when(now == pairs * blocks - 1)
        def _():
            send_back(pairs - 1)
            reduce.finish()
            finish_rows()
            own_out.wait()
            take_back(pairs - 1)
            for step in range(1, count):
                for which in range(pairs):
                    for kind in range(2):
                        far_copy(step, which, kind).wait_send()
                        back_copy(step, which, kind).wait_send()

    def column(first):
        return pl.BlockSpec((rows, 2 * HD), lambda i, j: (0, i + first))

    def tile():
        return pl.BlockSpec((block, 2 * HD), lambda i, j: (j, i))

    def resident(shape):
        return pl.BlockSpec(shape, lambda i, j: (0,) * len(shape))

    far_sems = pltpu.SemaphoreType.DMA((away, 2, pairs))
    far_buffer = pltpu.VMEM((away, 2, pairs, rows, 2 * HD), BF)
    return pl.pallas_call(
        kernel,
        grid=(pairs, blocks),
        in_specs=[
            tile(),
            resident((keys, 2 * HD)),
            pl.BlockSpec((None, 8, block), lambda i, j: (i, 0, j)),
            tile(),
            tile(),
            column(pairs),
            column(2 * pairs),
            HBM,
            HBM,
        ]
        + [HBM] * late,
        out_specs=[resident(inputs.shape), HBM] + [resident(tuple(shape)) for shape in shapes],
        out_shape=[jax.ShapeDtypeStruct(inputs.shape, BF), jax.ShapeDtypeStruct(rows_out.shape, BF)]
        + [jax.ShapeDtypeStruct(shape, F32) for shape in shapes],
        scratch_shapes=[
            pltpu.VMEM((2, keys, 2 * HD), BF),
            pltpu.VMEM((2, 2 * HD, keys), BF),
            pltpu.VMEM((keys, 2 * HD), BF),
            pltpu.VMEM((keys, 2 * HD), F32),
            pltpu.VMEM((keys, 2 * HD), F32),
            pltpu.VMEM((2 * HD, block), F32),
            far_buffer,
            far_buffer,
            far_buffer,
            pltpu.VMEM(rows_out.shape[1:], BF),
            pltpu.SemaphoreType.DMA((2,)),
        ]
        + [far_sems] * 4
        + [pltpu.SemaphoreType.DMA((grid.seqs,))] * 2
        + reduce_scratch(grid, shapes),
        compiler_params=pltpu.CompilerParams(
            collective_id=2, has_side_effects=True, vmem_limit_bytes=61 << 20
        ),
        cost_estimate=pl.CostEstimate(
            flops=40 * H * rows * keys * HD, bytes_accessed=12 * rows * width, transcendentals=H * rows * keys
        ),
        name="attention_back",
    )(inputs, key_bias, log_totals, context, grad_context, inputs, inputs, inputs, rows_out, *wholes)


def body(
    tokens,
    lengths,
    query_weight,
    key_weight,
    value_weight,
    out_weight,
    up_weight,
    down_weight,
    query_bias,
    value_bias,
    out_bias,
    up_bias,
    down_bias,
    first_gain,
    first_shift,
    second_gain,
    second_shift,
    cotangent,
):
    seqs, length, width = tokens.shape
    grid = Grid(seqs)
    devices = grid.columns * grid.n
    slim = query_weight.shape[0]
    hidden = up_weight.shape[1]
    tall = hidden // devices
    wide = hidden // width

    vectors = (
        query_bias,
        value_bias,
        out_bias,
        down_bias,
        first_gain,
        first_shift,
        second_gain,
        second_shift,
    )
    vectors = vectors + (up_bias,)
    lines = -(-len(vectors) // 16) * 16
    tile = jnp.zeros((lines, 128), BF)
    for i, vector in enumerate(vectors):
        size = vector.shape[0]
        tile = tile + jnp.pad(vector[None, :], ((i, lines - 1 - i), (0, 128 - size)))
    flat_in, into_full, _, key_bias, live_rows, *whole_vectors = start_exchange(
        grid,
        tokens,
        (query_weight, key_weight, value_weight),
        tile,
        lengths,
        tuple(vector.shape[0] for vector in vectors),
    )
    flat_in = flat_in.reshape(-1, width)
    into_full = into_full.reshape(width, 3 * width)
    query_add, value_add, out_add, down_add, gain_one, shift_one, gain_two, shift_two, up_add = whole_vectors

    into_add = jnp.concatenate([query_add, jnp.zeros_like(query_add), value_add], axis=1)
    inputs = (matmul(flat_in, into_full) + into_add).astype(BF)
    context, log_totals, grad_in, out_full, up_full, down_full = attention(
        grid, inputs, key_bias, (out_weight, up_weight, down_weight), cotangent
    )
    out_full = out_full.reshape(width, width)
    up_full = up_full.reshape(width, hidden)
    down_full = down_full.reshape(hidden, width)
    grad_in = grad_in.reshape(-1, width)

    first_sum = flat_in.astype(F32) + matmul(context, out_full) + out_add
    first_norm, first_unit, first_factor = normalize(first_sum, gain_one, shift_one)
    first_low = lax.optimization_barrier(first_norm.astype(BF))
    up_pre = matmul(first_low, up_full) + up_add
    below = 0.5 * (1.0 + lax.erf(up_pre * ROOT_HALF))
    slope = (below + up_pre * INV_ROOT_TWO_PI * jnp.exp(-0.5 * up_pre * up_pre)).astype(BF)
    activated, slope = lax.optimization_barrier(((up_pre * below).astype(BF), slope))
    second_sum = first_low.astype(F32) + matmul(activated, down_full) + down_add
    second_norm, second_unit, second_factor = normalize(second_sum, gain_two, shift_two)
    output = (second_norm * live_rows).astype(BF).reshape(seqs, length, width)

    grad_output = grad_in.astype(F32) * live_rows
    grad_gain_two = jnp.sum(grad_output * second_unit, axis=0)
    grad_shift_two = jnp.sum(grad_output, axis=0)
    grad_second = norm_back(grad_output, second_unit, second_factor, gain_two)
    grad_branch = grad_second.astype(BF)
    grad_down_add = jnp.sum(grad_branch.astype(F32), axis=0)
    grad_down = left_product(activated, grad_branch).astype(BF)
    grad_up_low = (right_product(grad_branch, down_full) * slope.astype(F32)).astype(BF)
    grad_up_add = jnp.sum(grad_up_low.astype(F32), axis=0)
    grad_up = left_product(first_low, grad_up_low).astype(BF)
    grad_first = right_product(grad_up_low, up_full) + grad_second
    grad_gain_one = jnp.sum(grad_first * first_unit, axis=0)
    grad_shift_one = jnp.sum(grad_first, axis=0)
    grad_residual = norm_back(grad_first, first_unit, first_factor, gain_one)
    grad_attend = grad_residual.astype(BF)
    grad_out_add = jnp.sum(grad_attend.astype(F32), axis=0)
    grad_out = left_product(context, grad_attend).astype(BF)
    grad_context = right_product(grad_attend, out_full).astype(BF)

    def pack(grads, more=()):
        count = len(grads)
        table = jnp.stack(grads).reshape(count, devices, slim).transpose(1, 0, 2)
        table = jnp.concatenate([table.reshape(devices, count * slim), *more], axis=1).astype(BF)
        size = table.shape[1]
        table = jnp.pad(table, ((0, 0), (0, -size % 128)))
        return jnp.broadcast_to(table[:, None, :], (devices, 8, table.shape[1])).reshape(devices * 8, -1)

    def spread_pack(grads):
        count = len(grads)
        place = jnp.arange(count * width, dtype=jnp.int32)
        lane = (place // width) * slim + place % slim
        owner = (place % width) // slim
        row = jnp.concatenate(grads).astype(BF)[None, :]
        apart = jnp.where(jnp.arange(devices, dtype=jnp.int32)[:, None] == owner[None, :], row, jnp.zeros_like(row))
        lanes = -(-count * slim // 128) * 128
        table = matmul(apart, (lane[:, None] == jnp.arange(lanes, dtype=jnp.int32)[None, :]).astype(BF)).astype(BF)
        return jnp.broadcast_to(table[:, None, :], (devices, 8, lanes)).reshape(devices * 8, lanes)

    middle = pack(
        [grad_out_add, grad_down_add, grad_gain_one, grad_shift_one, grad_gain_two, grad_shift_two],
        (grad_up_add.reshape(devices, tall),),
    )
    wholes = [
        by_place(grid, grad_up, slim),
        by_place(grid, grad_down, tall),
        by_place(grid, grad_out, slim),
        by_place(grid, middle, 8),
    ]
    low, output, grad_up_own, grad_down_own, grad_out_own, middle_own = attention_back(
        grid, inputs, key_bias, log_totals, context, grad_context, wholes, output
    )
    query_adds = jnp.sum(low[:, :width].astype(F32), axis=0)
    value_adds = jnp.sum(low[:, 2 * width :].astype(F32), axis=0)
    tokens_grad = right_product(low, into_full) + grad_residual
    wholes = [
        by_place(grid, left_product(flat_in, low).astype(BF), slim),
        by_place(grid, spread_pack([query_adds, value_adds]), 8),
    ]
    tokens_grad = tokens_grad.astype(BF).reshape(seqs, length, width)
    tokens_grad, grad_into_own, last_own = end_exchange(grid, tokens_grad, wholes)
    tokens_grad = tokens_grad.astype(F32)
    middle_own, last_own = middle_own[0], last_own[0]
    vector_outs = [last_own[:slim], last_own[slim : 2 * slim]]
    vector_outs = vector_outs + [middle_own[i * slim : (i + 1) * slim] for i in range(6)]
    up_add_own = middle_own[6 * slim : 6 * slim + tall]
    matrix_outs = [grad_into_own[:, i * width : (i + 1) * width] for i in range(3)]
    return (
        output,
        tokens_grad,
        matrix_outs[0],
        matrix_outs[1],
        matrix_outs[2],
        grad_out_own,
        grad_up_own,
        grad_down_own,
        vector_outs[0],
        vector_outs[1],
        vector_outs[2],
        up_add_own,
        vector_outs[3],
        vector_outs[4],
        vector_outs[5],
        vector_outs[6],
        vector_outs[7],
    )


def solution(mesh):
    whole = ("dp", "seq")
    matrix, vector, rows = P(whole, None), P(whole), P("dp", "seq", None)
    return jax.shard_map(
        body,
        mesh=mesh,
        in_specs=(rows, P("dp")) + (matrix,) * 6 + (vector,) * 9 + (rows,),
        out_specs=(rows, rows) + (matrix,) * 6 + (vector,) * 9,
        check_vma=False,
    )
```
